32 devices in a mesh: dom: 16 (over z, x, core), sub: 2 (over y).
Axes of the slice: x: 2, y: 2, z: 4, core: 2. Of those that a mesh axis runs over, the one named last changes fastest.
Arguments:
- edge_vectors: float32 [3, 32768], P(None, ('dom', 'sub')), may hold values from -4.95 to 4.95, as said below
- senders: int32 [32768], P(('dom', 'sub')), may hold values from 0 to 175, as said below
- counts: int32 [1024], P(('dom', 'sub')), may hold values from 1 to 32, as said below
- species: int32 [1024], P(('dom', 'sub')), may hold values from 0 to 3
- send_list: int32 [512], P(('dom', 'sub')), may hold values from 0 to 31, as said below
- embed: float32 [128, 4], replicated, may hold values from -6 to 6
- radial_in1: float32 [64, 8], replicated, may hold values from -4 to 4
- radial_mid1: float32 [64, 64], replicated, may hold values from -1.5 to 1.5
- radial_out1: float32 [256, 64], replicated, may hold values from -1.5 to 1.5
- mix_s1: float32 [128, 128], replicated, may hold values from -0.5 to 0.5
- mix_v1: float32 [128, 128], replicated, may hold values from -0.5 to 0.5
- mix_q1: float32 [128, 128], replicated, may hold values from -0.25 to 0.25
- radial_in2: float32 [64, 8], replicated, may hold values from -4 to 4
- radial_mid2: float32 [64, 64], replicated, may hold values from -1.5 to 1.5
- radial_out2: float32 [512, 64], replicated, may hold values from -1.5 to 1.5
- mix_s2: float32 [128, 128], replicated, may hold values from -0.5 to 0.5
- mix_v2: float32 [128, 128], replicated, may hold values from -0.5 to 0.5
- mix_q2: float32 [128, 128], replicated, may hold values from -0.25 to 0.25
- read_lin: float32 [128], replicated, may hold values from -0.5 to 0.5
- read_hidden: float32 [16, 128], replicated, may hold values from -0.5 to 0.5
- read_out: float32 [16], replicated, may hold values from -1.5 to 1.5
Outputs:
- atom_energies: float32 [1024], P(('dom', 'sub'))
- forces: float32 [3, 1024], P(None, ('dom', 'sub'))
The draws below stay inside these ranges and needn't reach their ends.
Inputs may be any that keep to these rules, and one draw needn't show every extreme that they name: `senders`: A value t of 32 or more names entry (t - 32) % 16 of the send list of the device at offset (s // 3 - 1, s % 3 - 1) along (dom, sub), s = (t - 32) // 16; s is never 4 and never names a device outside the grid. `counts`: an atom's neighbours fill its first slots; the rest are padding. `send_list`: the 16 entries of one device are distinct atoms of that device, counted from its first atom. `edge_vectors`: every column has a length between 0.75 and 4.95.
All inputs are finite; a program needn't handle non-finite values.
Results may differ from the reference program's by a relative error of at most 0.000088.
Values sent between devices are 32-bit elements; how exact they have to be, the bound alone decides.
A program may use at most 64 MiB of HBM per device.

```python
import math
import jax
import jax.numpy as jnp
from jax import lax

C = 128
BASIS = 8
HID = 64
READ_HID = 16
SPECIES = 4
K = 32
ATOM_DEV = 32
GHOSTS = 16
ATOMS = 1024
EDGES = 32768
N_DOM = 16
N_SUB = 2


def draw_edge_vectors(key, part):
    dir_key, len_key = jax.random.split(key)
    direction = jax.random.normal(dir_key, (3, EDGES), jnp.float32)
    direction = direction / jnp.maximum(jnp.sqrt(jnp.sum(direction * direction, axis=0)), 0.001)[None, :]
    uniform = jax.random.uniform(len_key, (EDGES,), jnp.float32)
    length = 0.8 + 4.1 * uniform
    return direction * length[None, :]


def draw_senders(key, part):
    raw_key, spot_key = jax.random.split(jax.random.fold_in(key, 11))
    edge_ids = jnp.arange(EDGES, dtype=jnp.int32)
    device = edge_ids // (ATOM_DEV * K)
    domain = device // N_SUB
    subdom = device % N_SUB
    table_size = ATOM_DEV + 9 * GHOSTS
    raw = jax.random.randint(raw_key, (EDGES,), 0, table_size, dtype=jnp.int32)
    ghost_slot = jnp.maximum(raw - ATOM_DEV, 0) // GHOSTS
    near_dom = domain + ghost_slot // 3 - 1
    near_sub = subdom + ghost_slot % 3 - 1
    inside = (near_dom >= 0) & (near_dom < N_DOM) & (near_sub >= 0) & (near_sub < N_SUB)
    valid = (raw < ATOM_DEV) | (ghost_slot != 4) & inside
    chosen = jnp.where(valid, raw, raw % ATOM_DEV)
    spots = jax.random.randint(spot_key, (2,), 0, ATOM_DEV * K - 1, dtype=jnp.int32)
    chosen = chosen.at[spots[0]].set(table_size - 1)
    other_spot = (spots[0] + 1 + spots[1]) % (ATOM_DEV * K)
    chosen = chosen.at[other_spot].set(0)
    return chosen.astype(jnp.int32)


def draw_counts(key, part):
    cap_key, drop_key, spot_key = jax.random.split(jax.random.fold_in(key, 23), 3)
    devices = ATOMS // ATOM_DEV
    caps = jax.random.randint(cap_key, (devices,), K // 2, K + 1, dtype=jnp.int32)
    drops = jax.random.randint(drop_key, (ATOMS,), 0, K // 2, dtype=jnp.int32)
    filled = jnp.maximum(jnp.repeat(caps, ATOM_DEV) - drops, 1)
    spot = jax.random.randint(spot_key, (), 0, ATOMS, dtype=jnp.int32)
    return filled.at[spot].set(K).astype(jnp.int32)


def draw_send_list(key, part):
    devices = ATOMS // ATOM_DEV
    base_key = jax.random.fold_in(key, 37)

    def pick(index):
        return jax.random.permutation(jax.random.fold_in(base_key, index), ATOM_DEV)[:GHOSTS]
    return jax.vmap(pick)(jnp.arange(devices)).reshape(-1).astype(jnp.int32)


def place_ends(drawn, key, low, high):
    extent = drawn.shape
    spot = [jax.random.randint(jax.random.fold_in(key, axis), (), 0, extent[axis]) for axis in range(len(extent))]
    drawn = drawn.at[tuple(spot)].set(low)
    longest = extent.index(max(extent))
    spot[longest] = (spot[longest] + 1) % extent[longest]
    return drawn.at[tuple(spot)].set(high)


def gaussian(key, shape, scale, reach, held_as=jnp.bfloat16):
    values = jax.random.normal(key, shape, jnp.float32) * scale
    return jnp.minimum(jnp.maximum(values, -reach), reach).astype(held_as)


def setup_inputs(seed: int = 0) -> dict:
    arg_keys = jax.random.split(jax.random.key(seed), 22)
    return {
        "edge_vectors": draw_edge_vectors(jax.random.fold_in(arg_keys[21], 71), 0),
        "senders": draw_senders(jax.random.fold_in(arg_keys[21], 71), 0),
        "counts": draw_counts(jax.random.fold_in(arg_keys[21], 71), 0),
        "species": place_ends(jax.random.randint(arg_keys[3], (ATOMS,), 0, SPECIES), jax.random.fold_in(arg_keys[3], 1), 0, SPECIES - 1).astype(jnp.int32),
        "send_list": draw_send_list(jax.random.fold_in(arg_keys[21], 71), 0),
        "embed": gaussian(arg_keys[5], (C, SPECIES), 1.0, 6.0, jnp.float32),
        "radial_in1": gaussian(arg_keys[6], (HID, BASIS), (BASIS // 4) ** -0.5, 4.0, jnp.float32),
        "radial_mid1": gaussian(arg_keys[7], (HID, HID), (HID // 4) ** -0.5, 1.5, jnp.float32),
        "radial_out1": gaussian(arg_keys[8], (2 * C, HID), (HID // 4) ** -0.5, 1.5, jnp.float32),
        "mix_s1": gaussian(arg_keys[9], (C, C), C ** -0.5, 0.5, jnp.float32),
        "mix_v1": gaussian(arg_keys[10], (C, C), C ** -0.5, 0.5, jnp.float32),
        "mix_q1": gaussian(arg_keys[11], (C, C), (4 * C) ** -0.5, 0.25, jnp.float32),
        "radial_in2": gaussian(arg_keys[12], (HID, BASIS), (BASIS // 4) ** -0.5, 4.0, jnp.float32),
        "radial_mid2": gaussian(arg_keys[13], (HID, HID), (HID // 4) ** -0.5, 1.5, jnp.float32),
        "radial_out2": gaussian(arg_keys[14], (4 * C, HID), (HID // 4) ** -0.5, 1.5, jnp.float32),
        "mix_s2": gaussian(arg_keys[15], (C, C), C ** -0.5, 0.5, jnp.float32),
        "mix_v2": gaussian(arg_keys[16], (C, C), C ** -0.5, 0.5, jnp.float32),
        "mix_q2": gaussian(arg_keys[17], (C, C), (4 * C) ** -0.5, 0.25, jnp.float32),
        "read_lin": gaussian(arg_keys[18], (C,), C ** -0.5, 0.5, jnp.float32),
        "read_hidden": gaussian(arg_keys[19], (READ_HID, C), C ** -0.5, 0.5, jnp.float32),
        "read_out": gaussian(arg_keys[20], (READ_HID,), READ_HID ** -0.5, 1.5, jnp.float32),
    }


cutoff_radius = 5.0
exact = lax.Precision.HIGHEST

def radial_weights(distance, w_in, w_mid, w_out):
    scaled = distance / cutoff_radius
    envelope = 1.0 - 28.0 * scaled ** 6 + 48.0 * scaled ** 7 - 21.0 * scaled ** 8
    harmonic = jnp.arange(1, w_in.shape[1] + 1).astype(distance.dtype)[:, None]
    radial_basis = math.sqrt(2.0 / cutoff_radius) * jnp.sin(harmonic * (math.pi / cutoff_radius) * distance[None, :]) / distance[None, :] * envelope[None, :]
    hidden = jax.nn.silu(jnp.dot(w_in, radial_basis, precision=exact))
    hidden = jax.nn.silu(jnp.dot(w_mid, hidden, precision=exact))
    return jnp.dot(w_out, hidden, precision=exact)

def edge_messages(lookup, vectors, sources, live_mask, weights, slots):
    channels = lookup.shape[1]
    edges = vectors.shape[1]
    distance = jnp.sqrt(lax.optimization_barrier(jnp.sum(vectors * vectors, axis=0)))
    unit_dir = vectors / distance[None, :]
    radial = radial_weights(distance, weights[0], weights[1], weights[2]).reshape(-1, channels, edges) * live_mask[None, None, :]
    picked = jnp.take(lookup, sources, axis=2)
    scalar = picked[0]
    if lookup.shape[0] == 1:
        scalar_msg = radial[0] * scalar
        vector_msg = radial[1][None] * scalar[None] * unit_dir[:, None, :]
    else:
        vector = picked[1:]
        scalar_msg = radial[0] * scalar + radial[1] * lax.optimization_barrier(jnp.sum(unit_dir[:, None, :] * vector, axis=0))
        vector_msg = radial[2][None] * scalar[None] * unit_dir[:, None, :] + radial[3][None] * vector
    stacked = jnp.concatenate([scalar_msg[None], vector_msg], axis=0)
    return lax.optimization_barrier(jnp.sum(stacked.reshape(4, channels, edges // slots, slots), axis=3)) * slots ** (-0.5)

def node_update(aggregate, scalar, vector, mix_s, mix_v, mix_q):
    mixed_scalar = jnp.dot(mix_s, aggregate[0], precision=exact)
    mixed_vector = jnp.einsum('cd,kda->kca', mix_v, aggregate[1:], precision=exact)
    squares = mixed_scalar * mixed_scalar + lax.optimization_barrier(jnp.sum(mixed_vector * mixed_vector, axis=0))
    next_scalar = scalar + mixed_scalar + jnp.dot(mix_q, squares, precision=exact)
    next_vector = vector + mixed_vector + mixed_vector * mixed_scalar[None]
    return (next_scalar, next_vector)

def atom_energy(scalar_one, scalar_two, read_lin, read_hidden, read_out):
    second_term = jnp.dot(read_out, jax.nn.silu(jnp.dot(read_hidden, scalar_two, precision=exact)), precision=exact)
    return jnp.dot(read_lin, scalar_one, precision=exact) + second_term

def global_sources(senders, send_list):
    edge_ids = jnp.arange(EDGES).astype(jnp.int32)
    device = edge_ids // (ATOM_DEV * K)
    domain = device // N_SUB
    subdom = device % N_SUB
    offset = jnp.maximum(senders - ATOM_DEV, 0)
    ghost_slot = offset // GHOSTS
    list_entry = offset % GHOSTS
    near_dom = jnp.clip(domain + ghost_slot // 3 - 1, 0, N_DOM - 1)
    near_sub = jnp.clip(subdom + ghost_slot % 3 - 1, 0, N_SUB - 1)
    neighbour = near_dom * N_SUB + near_sub
    ghost_atom = neighbour * ATOM_DEV + send_list[(neighbour * GHOSTS + list_entry).astype(jnp.int32)]
    return jnp.where(senders < ATOM_DEV, device * ATOM_DEV + senders, ghost_atom).astype(jnp.int32)

def blockwise(lookup, vectors, sources, live_mask, weights):
    block_rows = math.gcd(ATOMS, 1024)
    block_count = ATOMS // block_rows
    vec_blocks = vectors.reshape(3, block_count, block_rows * K).transpose(1, 0, 2)

    def one_block(block_items):
        return edge_messages(lookup, block_items[0], block_items[1], block_items[2], weights, K)
    outputs = lax.map(jax.checkpoint(one_block), (vec_blocks, sources.reshape(block_count, -1), live_mask.reshape(block_count, -1)))
    return outputs.transpose(1, 2, 0, 3).reshape(4, -1, ATOMS)

def reference(edge_vectors, senders, counts, species, send_list, embed, radial_in1, radial_mid1, radial_out1, mix_s1, mix_v1, mix_q1, radial_in2, radial_mid2, radial_out2, mix_s2, mix_v2, mix_q2, read_lin, read_hidden, read_out):
    sources = global_sources(senders, send_list)
    live_mask = (jnp.arange(K)[None, :] < counts[:, None]).reshape(-1).astype(edge_vectors.dtype)
    species_hot = (jnp.arange(SPECIES)[:, None] == species[None, :]).astype(embed.dtype)
    initial = jnp.dot(embed, species_hot, precision=exact)
    layer_one = (radial_in1, radial_mid1, radial_out1)
    layer_two = (radial_in2, radial_mid2, radial_out2)

    def energies(vectors):
        agg_first = blockwise(initial[None], vectors, sources, live_mask, layer_one)
        scalar_one, vector_one = node_update(agg_first, initial, jnp.zeros((3,) + initial.shape, initial.dtype), mix_s1, mix_v1, mix_q1)
        lookup = jnp.concatenate([scalar_one[None], vector_one], axis=0)
        agg_second = blockwise(lookup, vectors, sources, live_mask, layer_two)
        scalar_two = node_update(agg_second, scalar_one, vector_one, mix_s2, mix_v2, mix_q2)[0]
        return atom_energy(scalar_one, scalar_two, read_lin, read_hidden, read_out)
    atom_energies, pullback = jax.vjp(energies, edge_vectors)
    edge_grads = pullback(jnp.ones_like(atom_energies))[0]
    received = lax.optimization_barrier(jnp.sum(edge_grads.reshape(3, ATOMS, K), axis=2))
    sent_part = jnp.zeros((3, ATOMS), edge_grads.dtype).at[:, sources].add(edge_grads)
    return (atom_energies, received - sent_part)
```

```python
import functools
import math

import jax
import jax.numpy as jnp
from jax import lax
from jax.experimental import pallas as pl
from jax.experimental.pallas import tpu as pltpu
from jax.sharding import PartitionSpec as P

cutoff_radius = 5.0
f32 = jnp.float32
bf16 = jnp.bfloat16
LANES = 128
MESH = pl.DeviceIdType.MESH


def mm(a, b, ca, cb):
    return lax.dot_general(a, b, (((ca,), (cb,)), ((), ())), preferred_element_type=f32)


def split(x):
    hi = x.astype(bf16)
    return hi, (x - hi.astype(f32)).astype(bf16)


def split3(x):
    hi = x.astype(bf16)
    rest = x - hi.astype(f32)
    mid = rest.astype(bf16)
    return hi, mid, (rest - mid.astype(f32)).astype(bf16)


def dot3(a, b, ca, cb):
    a_hi, a_lo = split(a)
    b_hi, b_lo = split(b)
    return mm(a_hi, b_hi, ca, cb) + (mm(a_hi, b_lo, ca, cb) + mm(a_lo, b_hi, ca, cb))


def hot2(hot, x, ca, cb):
    hi, lo = split(x)
    return mm(hot, hi, ca, cb) + mm(hot, lo, ca, cb)


def hot3(hot, x, ca, cb):
    hi, mid, lo = split3(x)
    return mm(hot, hi, ca, cb) + (mm(hot, mid, ca, cb) + mm(hot, lo, ca, cb))


def to_column(row):
    count = row.shape[1]
    shape = (count, count)
    same = lax.broadcasted_iota(jnp.int32, shape, 0) == lax.broadcasted_iota(jnp.int32, shape, 1)
    return jnp.sum(jnp.where(same, row, 0.0), axis=1, keepdims=True)


def series(t, first, terms):
    total = jnp.ones_like(t)
    for i in reversed(range(terms)):
        low = first + 2 * i
        total = 1.0 - t * (1.0 / (low * (low + 1))) * total
    return total


def kernel(
    n_dom,
    n_sub,
    vec_ref,
    senders_ref,
    counts_ref,
    species_ref,
    list_ref,
    embed_ref,
    win1_ref,
    wmid1_ref,
    wout1_ref,
    ms1_ref,
    mv1_ref,
    mq1_ref,
    win2_ref,
    wmid2_ref,
    wout2_ref,
    ms2_ref,
    mv2_ref,
    mq2_ref,
    lin_ref,
    rh_ref,
    ro_ref,
    eout_ref,
    out_ref,
    kinds,
    kinds_out,
    table,
    feat_out,
    grad_table,
    grad_in,
    force_table,
    force_in,
    live_hot,
    spec_hot,
    src_hot,
    v8,
    dbas,
    inv_ref,
    pack,
    rhs,
    wide_rhs,
    winp,
    winp_k,
    wmid,
    wmid_f,
    wmid_b,
    w1,
    w2_k,
    hid_ref,
    u_ref,
    ds1_ref,
    ds2_ref,
    rad_ref,
    x_ref,
    sums,
    agg2,
    dagg2,
    dh_ref,
    du_ref,
    gp,
    qt,
    send_sem,
    recv_sem,
):
    dm, sb = lax.axis_index("dom"), lax.axis_index("sub")
    atoms = species_ref.shape[1]
    edges = vec_ref.shape[1]
    slots = edges // atoms
    ghosts = list_ref.shape[1]
    kinds_n, channels = embed_ref.shape
    n_basis, hidden = win1_ref.shape
    chunk = 8 * slots
    n_chunks = edges // chunk
    scale = slots ** (-0.5)
    C = channels
    sides = [s for s in range(9) if s != 4]

    def exists(s):
        ok = None
        for here, count, off in ((dm, n_dom, s // 3 - 1), (sb, n_sub, s % 3 - 1)):
            if off == 0:
                continue
            one = here > 0 if off < 0 else here < count - 1
            ok = one if ok is None else jnp.logical_and(ok, one)
        return ok

    def place(s):
        return (dm + (s // 3 - 1), sb + (s % 3 - 1))

    def copy_for(phase, s, src, dst, there):
        return pltpu.make_async_remote_copy(
            src_ref=src,
            dst_ref=dst,
            send_sem=send_sem.at[phase, s],
            recv_sem=recv_sem.at[phase, 8 - s],
            device_id=place(there),
            device_id_type=MESH,
        )

    def ghost_rows(s):
        return pl.ds(atoms + ghosts * s, ghosts)

    def copies(phase, s, there):
        pairs = (
            lambda k, r: (kinds_out, kinds.at[ghost_rows(r)]),
            lambda k, r: (feat_out, table.at[ghost_rows(r)]),
            lambda k, r: (grad_table.at[ghost_rows(k)], grad_in.at[r]),
            lambda k, r: (force_table.at[ghost_rows(k)], force_in.at[r]),
        )
        src, dst = pairs[phase](s, 8 - s)
        return copy_for(phase, s, src, dst, there)

    def send_all(phase):
        for s in sides:
            @pl.when(exists(s))
            def _():
                copies(phase, s, s).start()

    def wait_all(phase):
        for s in sides:
            @pl.when(exists(s))
            def _():
                copies(phase, s, s).wait_send()
                copies(phase, 8 - s, s).wait_recv()

    kinds[...] = jnp.zeros_like(kinds)
    table[...] = jnp.zeros_like(table)
    grad_in[...] = jnp.zeros_like(grad_in)
    force_in[...] = jnp.zeros_like(force_in)
    barrier = pltpu.get_barrier_semaphore()
    for s in sides:
        @pl.when(exists(s))
        def _():
            pl.semaphore_signal(barrier, inc=1, device_id=place(s), device_id_type=MESH)

    species_col = to_column(species_ref[...].astype(f32))
    counts_col = to_column(counts_ref[...].astype(f32)).astype(jnp.int32)
    list_col = to_column(list_ref[...].astype(f32))
    lane_a = lax.broadcasted_iota(jnp.int32, (atoms, LANES), 1).astype(f32)
    own_kinds = (species_col == lane_a).astype(f32)
    kinds[0:atoms, :] = own_kinds
    listed = (
        list_col == lax.broadcasted_iota(jnp.int32, (ghosts, atoms), 1).astype(f32)
    ).astype(f32).astype(bf16)
    kinds_out[...] = mm(listed, own_kinds.astype(bf16), 1, 0)

    wmid[...] = jnp.zeros_like(wmid)
    wmid[0:hidden, 0:hidden] = wmid1_ref[...]
    wmid[hidden:, hidden:] = wmid2_ref[...]
    hi, lo = split(wmid[...])
    wmid_f[...] = jnp.concatenate([hi, hi, lo], axis=1)
    wmid_b[...] = jnp.concatenate([hi, hi, lo], axis=0)
    w1[...] = jnp.zeros_like(w1)
    w1[0:hidden, :] = wout1_ref[...]
    hi, lo = split(wout2_ref[...])
    w2_k[...] = jnp.concatenate([lo, hi, jnp.zeros_like(hi), hi], axis=0)
    winp[...] = jnp.zeros_like(winp)
    winp[0:n_basis, 0:hidden] = win1_ref[...]
    winp[0:n_basis, hidden:] = win2_ref[...]
    hi, lo = split(winp[...])
    winp_k[...] = jnp.concatenate([hi, hi, lo], axis=1)
    n_pack = 3 * n_basis
    row_i = lax.broadcasted_iota(jnp.int32, rhs.shape, 0)
    lane_i = lax.broadcasted_iota(jnp.int32, rhs.shape, 1)
    which = jnp.zeros(rhs.shape, f32)
    for k in range(3):
        in_lanes = (lane_i >= LANES * (k + 1)) & (lane_i < LANES * (k + 2))
        for part in range(3):
            which = jnp.where(in_lanes & (row_i == n_pack + 8 * part + k), 1.0, which)
    rhs[...] = which
    hi, lo = split(winp[0:n_basis, :])
    rhs[0:n_basis, 0:LANES] = hi.astype(f32)
    rhs[n_basis : 2 * n_basis, 0:LANES] = hi.astype(f32)
    rhs[2 * n_basis : 3 * n_basis, 0:LANES] = lo.astype(f32)
    wide_rhs[...] = rhs[...].astype(bf16)

    def dot_k(a, stacked, dim):
        a_hi, a_lo = split(a)
        both = jnp.concatenate([a_hi, a_lo], axis=1)
        if dim == 1:
            first, last = stacked[:, : 2 * LANES], stacked[:, 2 * LANES :]
        else:
            first, last = stacked[: 2 * LANES, :], stacked[2 * LANES :, :]
        return mm(both, first, 1, dim) + mm(a_hi, last, 1, dim)

    def upper_half(x, other):
        lane = lax.broadcasted_iota(jnp.int32, x.shape, 1)
        return jnp.where(lane >= hidden, x, other)

    v8[...] = jnp.zeros_like(v8)
    v8[0:3, :] = vec_ref[...]
    vectors = v8[...]
    dist = jnp.sqrt(jnp.sum(vectors * vectors, axis=0, keepdims=True))
    inv = 1.0 / dist
    unit = vectors * inv
    v8[...] = unit
    inv_ref[...] = inv
    x1 = dist * (1.0 / cutoff_radius)
    x2 = x1 * x1
    x5 = x2 * x2 * x1
    x6 = x5 * x1
    env = 1.0 + x6 * (-28.0 + x1 * (48.0 - 21.0 * x1))
    denv = x5 * (-168.0 + x1 * (336.0 - 168.0 * x1)) * (1.0 / cutoff_radius)
    order = (lax.broadcasted_iota(jnp.int32, (n_basis, edges), 0) + 1).astype(f32)
    turns = order * x1
    near = jnp.floor(turns + 0.5)
    odd = near - 2.0 * jnp.floor(near * 0.5)
    sign = 1.0 - 2.0 * odd
    angle = (turns - near) * math.pi
    t = angle * angle
    sine = sign * angle * series(t, 2, 7)
    cosine = sign * series(t, 1, 7)
    norm = math.sqrt(2.0 / cutoff_radius)
    wave = (norm * inv) * sine
    basis = wave * env
    dbas[...] = ((norm * math.pi / cutoff_radius) * order * cosine * inv - wave * inv) * env + wave * denv

    peers = [
        1 + jnp.where(at > 0, 1, 0) + jnp.where(at < count - 1, 1, 0)
        for at, count in ((dm, n_dom), (sb, n_sub))
    ]
    pl.semaphore_wait(barrier, peers[0] * peers[1] - 1)
    send_all(0)

    b_hi, b_lo = split(basis)
    u_hi, u_mid, u_lo = split3(unit)
    parts = [b_hi, b_lo, b_hi, u_hi, u_mid, u_lo]
    pack[...] = jnp.concatenate([p.astype(f32) for p in parts], axis=0).astype(bf16)

    def rows_of(c):
        return slice(c * chunk, (c + 1) * chunk)

    def each_chunk(step):
        for c in range(n_chunks):
            step(c, 0)

    def radial_step(c, _):
        rows = rows_of(c)
        out = mm(pack[:, rows], wide_rhs[...], 0, 0)
        p1 = out[:, :LANES]
        u_ref[rows, :] = out[:, LANES:]
        s1 = jax.nn.sigmoid(p1)
        h1 = p1 * s1
        ds1_ref[rows, :] = s1 * (1.0 + p1 * (1.0 - s1))
        p2 = dot_k(h1, wmid_f, 1)
        s2 = jax.nn.sigmoid(p2)
        hid_ref[rows, :] = p2 * s2
        ds2_ref[rows, :] = s2 * (1.0 + p2 * (1.0 - s2))
        return 0

    each_chunk(radial_step)

    edge_i = lax.broadcasted_iota(jnp.int32, (atoms, edges), 1)
    atom_i = lax.broadcasted_iota(jnp.int32, (atoms, edges), 0)
    spot = edge_i - atom_i * slots
    live = ((spot >= 0) & (spot < counts_col)).astype(f32)
    live_hot[...] = live
    live_row = jnp.sum(live, axis=0, keepdims=True)
    entry_i = lax.broadcasted_iota(jnp.int32, src_hot.shape, 0)
    src_hot[...] = jnp.where(entry_i == senders_ref[...], live_row, 0.0).astype(bf16)

    own_kinds = kinds[0:atoms, :]
    spread_i = lax.broadcasted_iota(jnp.int32, (kinds_n * atoms, kinds_n), 0)
    kind_i = lax.broadcasted_iota(jnp.int32, (kinds_n * atoms, kinds_n), 1)
    spread = ((spread_i >= kind_i * atoms) & (spread_i < (kind_i + 1) * atoms)).astype(f32).astype(bf16)
    embed_rows = hot3(spread, embed_ref[...], 1, 0)
    initial = hot3(own_kinds[:, 0:kinds_n].astype(bf16), embed_ref[...], 1, 0)

    wait_all(0)
    seen = mm(kinds[...].astype(bf16), src_hot[...], 0, 0)
    for s in range(kinds_n):
        hot = (live_hot[...] * seen[s : s + 1, :]).astype(bf16)
        spec_hot[s * atoms : (s + 1) * atoms, :] = hot
        spec_hot[(kinds_n + s) * atoms : (kinds_n + s + 1) * atoms, :] = hot

    sums[...] = jnp.zeros_like(sums)

    def first_step(c, _):
        rows = rows_of(c)
        hid = hid_ref[rows, :]
        hot = spec_hot[0 : kinds_n * atoms, rows]
        turned = [hid * u_ref[rows, LANES * k : LANES * (k + 1)] for k in range(3)]
        sums[...] += hot2(hot, jnp.concatenate([hid] + turned, axis=1), 1, 0)
        return 0

    each_chunk(first_step)

    def by_kind(x):
        total = x[0:atoms]
        for s in range(1, kinds_n):
            total = total + x[s * atoms : (s + 1) * atoms]
        return total

    agg = []
    for k in range(4):
        weight = w1[:, 0:C] if k == 0 else w1[:, C : 2 * C]
        spread_agg = dot3(sums[:, LANES * k : LANES * (k + 1)], weight, 1, 0)
        agg.append(by_kind(spread_agg * embed_rows) * scale)

    def mixed(parts, ms, mv, mq):
        a = dot3(parts[0], ms, 1, 1)
        b = dot3(jnp.concatenate(parts[1:], axis=0), mv, 1, 1)
        b = [b[k * atoms : (k + 1) * atoms] for k in range(3)]
        squares = a * a + (b[0] * b[0] + b[1] * b[1] + b[2] * b[2])
        return a, b, dot3(squares, mq, 1, 1)

    a1, b1, q1 = mixed(agg, ms1_ref[...], mv1_ref[...], mq1_ref[...])
    scalar_one = initial + a1 + q1
    feats = [scalar_one] + [b + b * a1 for b in b1]
    for k in range(4):
        table[0:atoms, C * k : C * (k + 1)] = feats[k]
        feat_out[:, C * k : C * (k + 1)] = hot3(listed, feats[k], 1, 0)
    send_all(1)

    def second_radial(c, _):
        rows = rows_of(c)
        hid = hid_ref[rows, :]
        twice = upper_half(hid, pltpu.roll(hid, hidden, 1)).astype(bf16)
        rest = split(hid)[1]
        rad_ref[rows, :] = mm(jnp.concatenate([twice, rest], axis=1), w2_k[...], 1, 0)
        return 0

    each_chunk(second_radial)
    wait_all(1)

    def second_step(c, _):
        rows = rows_of(c)
        x = hot2(src_hot[:, rows], table[...], 0, 0)
        x_ref[rows, :] = x
        s, v = x[:, :C], [x[:, C * k : C * (k + 1)] for k in (1, 2, 3)]
        u = [u_ref[rows, LANES * k : LANES * (k + 1)] for k in range(3)]
        r = [rad_ref[rows, C * k : C * (k + 1)] for k in range(4)]
        uv = u[0] * v[0] + u[1] * v[1] + u[2] * v[2]
        rs = r[2] * s
        msgs = [r[0] * s + r[1] * uv] + [rs * u[k] + r[3] * v[k] for k in range(3)]
        group = slice(c * 8, (c + 1) * 8)
        for k in range(4):
            agg2[group, C * k : C * (k + 1)] = jnp.sum(msgs[k].reshape(8, slots, C), axis=1) * scale
        return 0

    each_chunk(second_step)

    parts = [agg2[:, C * k : C * (k + 1)] for k in range(4)]
    a2, b2, q2 = mixed(parts, ms2_ref[...], mv2_ref[...], mq2_ref[...])
    scalar_two = scalar_one + a2 + q2
    z = dot3(scalar_two, rh_ref[...], 1, 1)
    sz = jax.nn.sigmoid(z)
    lin8 = jnp.broadcast_to(lin_ref[...], (8, C))
    ro8 = jnp.broadcast_to(ro_ref[...], (8, ro_ref.shape[1]))
    energy = dot3(lin8, scalar_one, 1, 1) + dot3(ro8, z * sz, 1, 1)
    eout_ref[...] = energy[0:1, :]

    dz = ro_ref[...] * (sz * (1.0 + z * (1.0 - sz)))
    ds_two = dot3(dz, rh_ref[...], 1, 0)
    dq = dot3(ds_two, mq2_ref[...], 1, 0)
    da = ds_two + 2.0 * a2 * dq
    dagg2[:, 0:C] = dot3(da, ms2_ref[...], 1, 0) * scale
    db = dot3(jnp.concatenate([2.0 * b * dq for b in b2], axis=0), mv2_ref[...], 1, 0) * scale
    for k in range(3):
        dagg2[:, C * (k + 1) : C * (k + 2)] = db[k * atoms : (k + 1) * atoms]
    ds_direct = ds_two + lin_ref[...]

    def lane_sum(k, x):
        lane = lax.broadcasted_iota(jnp.int32, x.shape, 1)
        return jnp.where(lane == 8 + k, jnp.sum(x, axis=1, keepdims=True), 0.0)

    grad_table[...] = jnp.zeros_like(grad_table)

    def spread_rows(c):
        group = slice(c * 8, (c + 1) * 8)
        out = []
        for k in range(4):
            small = dagg2[group, C * k : C * (k + 1)]
            out.append(jnp.broadcast_to(small[:, None, :], (8, slots, C)).reshape(chunk, C))
        return out

    def second_scatter(c, _):
        rows = rows_of(c)
        d = spread_rows(c)
        u = [u_ref[rows, LANES * k : LANES * (k + 1)] for k in range(3)]
        r = [rad_ref[rows, C * k : C * (k + 1)] for k in range(4)]
        ud = u[0] * d[1] + u[1] * d[2] + u[2] * d[3]
        r1d = r[1] * d[0]
        dx = [r[0] * d[0] + r[2] * ud] + [r1d * u[k] + r[3] * d[k + 1] for k in range(3)]
        grad_table[...] += hot2(src_hot[:, rows], jnp.concatenate(dx, axis=1), 1, 0)
        return 0

    each_chunk(second_scatter)
    send_all(2)

    def second_back(c, _):
        rows = rows_of(c)
        d = spread_rows(c)
        s, v = x_ref[rows, 0:C], [x_ref[rows, C * k : C * (k + 1)] for k in (1, 2, 3)]
        u = [u_ref[rows, LANES * k : LANES * (k + 1)] for k in range(3)]
        uv = u[0] * v[0] + u[1] * v[1] + u[2] * v[2]
        ud = u[0] * d[1] + u[1] * d[2] + u[2] * d[3]
        dv = d[1] * v[0] + d[2] * v[1] + d[3] * v[2]
        drad = jnp.concatenate([d[0] * s, d[0] * uv, s * ud, dv], axis=1)
        hi, lo = split(drad)
        dh = mm(hi, w2_k[0:LANES, :], 1, 1)
        dh = dh + pltpu.roll(dh, hidden, 1) + mm(lo, w2_k[LANES:, :], 1, 1)
        dh_ref[rows, :] = upper_half(dh, 0.0)
        r1d = rad_ref[rows, C : 2 * C] * d[0]
        r2s = rad_ref[rows, 2 * C : 3 * C] * s
        du = lane_sum(0, r1d * v[0] + r2s * d[1])
        for k in (1, 2):
            du = du + lane_sum(k, r1d * v[k] + r2s * d[k + 1])
        du_ref[rows, :] = du
        return 0

    each_chunk(second_back)
    wait_all(2)
    ghost_grad = grad_in[0]
    for s in range(1, 9):
        ghost_grad = ghost_grad + grad_in[s]
    dfeat = grad_table[0:atoms, :] + hot3(listed, ghost_grad, 0, 0)
    ds = dfeat[:, 0:C] + ds_direct
    dv = [dfeat[:, C * k : C * (k + 1)] for k in (1, 2, 3)]
    dq = dot3(ds, mq1_ref[...], 1, 0)
    da = ds + 2.0 * a1 * dq + (dv[0] * b1[0] + dv[1] * b1[1] + dv[2] * b1[2])
    db = [dv[k] * (1.0 + a1) + 2.0 * b1[k] * dq for k in range(3)]
    dagg = [dot3(da, ms1_ref[...], 1, 0) * scale]
    db = dot3(jnp.concatenate(db, axis=0), mv1_ref[...], 1, 0) * scale
    dagg += [db[k * atoms : (k + 1) * atoms] for k in range(3)]
    for k in range(4):
        weight = w1[:, 0:C] if k == 0 else w1[:, C : 2 * C]
        spread_grad = jnp.concatenate([dagg[k]] * kinds_n, axis=0) * embed_rows
        hi, lo = split(dot3(spread_grad, weight, 1, 1))
        gp[:, LANES * k : LANES * (k + 1)] = jnp.concatenate([hi, lo], axis=0)

    def first_back(c, _):
        rows = rows_of(c)
        hot = spec_hot[:, rows]
        g = mm(hot, gp[...], 0, 0)
        hid = hid_ref[rows, :]
        dh = dh_ref[rows, :] + g[:, 0:LANES]
        q = du_ref[rows, :]
        for k in range(3):
            gk = g[:, LANES * (k + 1) : LANES * (k + 2)]
            dh = dh + u_ref[rows, LANES * k : LANES * (k + 1)] * gk
            q = q + lane_sum(k, hid * gk)
        dp2 = dh * ds2_ref[rows, :]
        dp1 = dot_k(dp2, wmid_b, 0) * ds1_ref[rows, :]
        q = q + dot_k(dp1, winp_k, 1)
        qt[:, rows] = jnp.transpose(q)
        return 0

    each_chunk(first_back)

    unit = v8[...]
    inv = inv_ref[...]
    dr = jnp.sum(qt[0:n_basis, :] * dbas[...], axis=0, keepdims=True)
    du = qt[8:16, :]
    along = jnp.sum(unit * du, axis=0, keepdims=True)
    g8 = dr * unit + (du - unit * along) * inv
    g_hi, g_mid, g_lo = split3(g8)
    hot = src_hot[...]
    force_table[...] = jnp.zeros_like(force_table)
    force_table[:, 0:8] = mm(hot, g_hi, 1, 1) + (mm(hot, g_mid, 1, 1) + mm(hot, g_lo, 1, 1))
    send_all(3)
    own = (live_hot[...] - src_hot[0:atoms, :].astype(f32)).astype(bf16)
    force = mm(g_hi, own, 1, 1) + (mm(g_mid, own, 1, 1) + mm(g_lo, own, 1, 1))
    wait_all(3)
    ghost_force = force_in[0]
    for s in range(1, 9):
        ghost_force = ghost_force + force_in[s]
    hi, mid, lo = split3(ghost_force)
    late = mm(hi, listed, 0, 0) + (mm(mid, listed, 0, 0) + mm(lo, listed, 0, 0))
    out_ref[...] = (force - late[0:8, :])[0:3, :]


def store_kernel(e_ref, f_ref, eo_ref, fo_ref, sem):
    one = pltpu.make_async_copy(e_ref, eo_ref, sem.at[0])
    two = pltpu.make_async_copy(f_ref, fo_ref, sem.at[1])
    one.start()
    two.start()
    one.wait()
    two.wait()


def on_device(n_dom, n_sub, *args):
    (vec, senders, counts, species, send_list, embed) = args[:6]
    weights = list(args[6:18])
    read_lin, read_hidden, read_out = args[18:]
    edges = vec.shape[1]
    atoms = species.shape[0]
    ghosts = send_list.shape[0]
    channels, kinds_n = embed.shape
    n_basis = weights[0].shape[1]
    for i in (0, 2, 6, 8):
        weights[i] = weights[i].T
    entries = -(-(atoms + 9 * ghosts) // LANES) * LANES
    wide = 4 * channels
    row = lambda x: x.reshape(1, -1)
    scratch = [
        ((entries, LANES), f32),
        ((ghosts, LANES), f32),
        ((entries, wide), f32),
        ((ghosts, wide), f32),
        ((entries, wide), f32),
        ((9, ghosts, wide), f32),
        ((entries, LANES), f32),
        ((9, ghosts, LANES), f32),
        ((atoms, edges), f32),
        ((2 * kinds_n * atoms, edges), bf16),
        ((entries, edges), bf16),
        ((8, edges), f32),
        ((n_basis, edges), f32),
        ((1, edges), f32),
        ((3 * n_basis + 24, edges), bf16),
        ((3 * n_basis + 24, 4 * LANES), f32),
        ((3 * n_basis + 24, 4 * LANES), bf16),
        ((LANES, LANES), f32),
        ((LANES, 3 * LANES), bf16),
        ((LANES, LANES), f32),
        ((LANES, 3 * LANES), bf16),
        ((3 * LANES, LANES), bf16),
        ((LANES, 2 * channels), f32),
        ((2 * LANES, wide), bf16),
        ((edges, LANES), f32),
        ((edges, 3 * LANES), f32),
        ((edges, LANES), f32),
        ((edges, LANES), f32),
        ((edges, wide), f32),
        ((edges, wide), f32),
        ((kinds_n * atoms, 4 * LANES), f32),
        ((atoms, wide), f32),
        ((atoms, wide), f32),
        ((edges, LANES), f32),
        ((edges, LANES), f32),
        ((2 * kinds_n * atoms, 4 * LANES), bf16),
        ((LANES, edges), f32),
    ]
    whole = pl.BlockSpec(memory_space=pltpu.VMEM)
    out = pl.pallas_call(
        functools.partial(kernel, n_dom, n_sub),
        out_shape=[pltpu.VMEM((1, atoms), f32), pltpu.VMEM((3, atoms), f32)],
        in_specs=[whole] * 21,
        out_specs=[whole, whole],
        scratch_shapes=[pltpu.VMEM(shape, dtype) for shape, dtype in scratch]
        + [pltpu.SemaphoreType.DMA((4, 9)), pltpu.SemaphoreType.DMA((4, 9))],
        compiler_params=pltpu.CompilerParams(
            collective_id=0, has_side_effects=True, vmem_limit_bytes=56 * 1024 * 1024
        ),
    )(
        vec,
        row(senders),
        row(counts),
        row(species),
        row(send_list),
        embed.T,
        *weights,
        row(read_lin),
        read_hidden,
        row(read_out),
    )
    hbm = pl.BlockSpec(memory_space=pltpu.HBM)
    out = pl.pallas_call(
        store_kernel,
        out_shape=[jax.ShapeDtypeStruct((1, atoms), f32), jax.ShapeDtypeStruct((3, atoms), f32)],
        in_specs=[pl.BlockSpec(memory_space=pltpu.VMEM)] * 2,
        out_specs=[hbm, hbm],
        scratch_shapes=[pltpu.SemaphoreType.DMA((2,))],
    )(*[pltpu.with_memory_space_constraint(o, pltpu.VMEM) for o in out])
    return out[0].reshape(atoms), out[1]


def solution(mesh):
    one = P(("dom", "sub"))
    return jax.shard_map(
        functools.partial(on_device, mesh.shape["dom"], mesh.shape["sub"]),
        mesh=mesh,
        in_specs=(P(None, ("dom", "sub")), one, one, one, one) + (P(),) * 16,
        out_specs=(one, P(None, ("dom", "sub"))),
        check_vma=False,
    )
```

```python
import functools
import math
import types

import jax
import jax.numpy as jnp
from jax import lax
from jax.experimental import pallas as pl
from jax.experimental.pallas import tpu as pltpu
from jax.sharding import PartitionSpec as P

cutoff_radius = 5.0
f32 = jnp.float32
bf16 = jnp.bfloat16
LANES = 128
MESH = pl.DeviceIdType.MESH


def mm(a, b, ca, cb):
    return lax.dot_general(a, b, (((ca,), (cb,)), ((), ())), preferred_element_type=f32)


def split(x):
    hi = x.astype(bf16)
    return hi, (x - hi.astype(f32)).astype(bf16)


def split3(x):
    hi = x.astype(bf16)
    rest = x - hi.astype(f32)
    mid = rest.astype(bf16)
    return hi, mid, (rest - mid.astype(f32)).astype(bf16)


def dot3(a, b, ca, cb):
    a_hi, a_lo = split(a)
    b_hi, b_lo = split(b)
    return mm(a_hi, b_hi, ca, cb) + (mm(a_hi, b_lo, ca, cb) + mm(a_lo, b_hi, ca, cb))


def hot3(hot, x, ca, cb):
    hi, mid, lo = split3(x)
    return mm(hot, hi, ca, cb) + (mm(hot, mid, ca, cb) + mm(hot, lo, ca, cb))


def to_column(row):
    count = row.shape[1]
    shape = (count, count)
    same = lax.broadcasted_iota(jnp.int32, shape, 0) == lax.broadcasted_iota(jnp.int32, shape, 1)
    return jnp.sum(jnp.where(same, row, 0.0), axis=1, keepdims=True)


def series(t, first, terms):
    total = jnp.ones_like(t)
    for i in reversed(range(terms)):
        low = first + 2 * i
        total = 1.0 - t * (1.0 / (low * (low + 1))) * total
    return total


def kernel(n_dom, n_sub, names, *refs):
    r = types.SimpleNamespace(**dict(zip(names, refs)))
    inputs = len(in_order(*range(21)))
    hbm = types.SimpleNamespace(**dict(zip(names[:inputs], refs[:inputs])))
    held = types.SimpleNamespace(**dict(zip(names[:inputs], refs[inputs + 2 : 2 * inputs + 2])))
    list_s, send_sem, recv_sem, in_sem = refs[-4:]
    dm, sb = lax.axis_index("dom"), lax.axis_index("sub")
    atoms = hbm.species.shape[1]
    edges = hbm.vec.shape[1]
    slots = edges // atoms
    G = hbm.list.shape[1]
    kinds_n, C = hbm.embed.shape
    n_basis, hidden = hbm.win1.shape
    chunk = 8 * slots
    n_chunks = edges // chunk
    scale = slots ** (-0.5)
    sides = [s for s in range(9) if s != 4]
    nodes = atoms + G

    def exists(s):
        ok = None
        for here, count, off in ((dm, n_dom, s // 3 - 1), (sb, n_sub, s % 3 - 1)):
            if off == 0:
                continue
            one = here > 0 if off < 0 else here < count - 1
            ok = one if ok is None else jnp.logical_and(ok, one)
        return ok

    def place(s):
        return (dm + (s // 3 - 1), sb + (s % 3 - 1))

    def row_of(s):
        return s if s < 4 else s - 1

    def block(s):
        return pl.ds(G * row_of(s), G)

    def copies(phase, s, there):
        o = 8 - s
        src, dst = (
            lambda: (hbm.species, r.spc.at[o]),
            lambda: (hbm.list, r.lst.at[o]),
            lambda: (r.out_v, r.ghost_v.at[block(o)]),
            lambda: (r.out_s, r.ghost_s.at[block(o)]),
            lambda: (r.grad_a.at[block(s)], r.in_a.at[row_of(o)]),
            lambda: (r.grad_b.at[block(s)], r.in_b.at[row_of(o)]),
            lambda: (r.force_g.at[block(s)], r.in_f.at[row_of(o)]),
        )[phase]()
        return pltpu.make_async_remote_copy(
            src_ref=src,
            dst_ref=dst,
            send_sem=send_sem.at[phase, s],
            recv_sem=recv_sem.at[phase, o],
            device_id=place(there),
            device_id_type=MESH,
        )

    def send_all(phase):
        for s in sides:
            @pl.when(exists(s))
            def _():
                copies(phase, s, s).start()

    def wait_in(phase):
        for s in sides:
            @pl.when(exists(s))
            def _():
                copies(phase, 8 - s, s).wait_recv()

    def wait_out(phase):
        for s in sides:
            @pl.when(exists(s))
            def _():
                copies(phase, s, s).wait_send()

    order = [hbm.species, hbm.list, hbm.vec, hbm.senders, hbm.counts, hbm.win1, hbm.win2, hbm.wmid1, hbm.wmid2]
    order += [hbm.wout2, hbm.wout1, hbm.embed]
    order += [x for x in refs[:inputs] if not any(x is y for y in order)]
    inside = dict(zip(map(id, refs[:inputs]), refs[inputs + 2 : 2 * inputs + 2]))
    pulls = [pltpu.make_async_copy(x, inside[id(x)], in_sem.at[i]) for i, x in enumerate(order)]
    pulls.append(pltpu.make_async_copy(hbm.list, list_s, in_sem.at[inputs]))
    for pull in pulls:
        pull.start()

    for ref in (r.spc, r.lst, r.ghost_v, r.ghost_s, r.in_a, r.in_b, r.in_f):
        ref[...] = jnp.zeros_like(ref)
    barrier = pltpu.get_barrier_semaphore()
    for s in sides:
        @pl.when(exists(s))
        def _():
            pl.semaphore_signal(barrier, inc=1, device_id=place(s), device_id_type=MESH)
    peers = [
        1 + jnp.where(at > 0, 1, 0) + jnp.where(at < count - 1, 1, 0)
        for at, count in ((dm, n_dom), (sb, n_sub))
    ]

    for ref in (r.rhs, r.v8, r.winp, r.wmid, r.rhp, r.rop, r.tab2):
        ref[...] = jnp.zeros_like(ref)
    pl.semaphore_wait(barrier, peers[0] * peers[1] - 1)
    send_all(0)
    send_all(1)
    for pull in pulls:
        pull.wait()

    def lanes_low(shape):
        return lax.broadcasted_iota(jnp.int32, shape, 1) < hidden

    def swap(x):
        return pltpu.roll(x, hidden, 1)

    def stack3(x, axis):
        hi, lo = split(x)
        return jnp.concatenate([hi, hi, lo], axis=axis)

    def dot_k(a, stacked, dim):
        k = a.shape[1]
        a_hi, a_lo = split(a)
        both = jnp.concatenate([a_hi, a_lo], axis=1)
        if dim == 1:
            first, last = stacked[:, : 2 * k], stacked[:, 2 * k :]
        else:
            first, last = stacked[: 2 * k, :], stacked[2 * k :, :]
        return mm(both, first, 1, dim) + mm(a_hi, last, 1, dim)

    def rows_of(c):
        return slice(c * chunk, (c + 1) * chunk)

    wmid, winp, rhs = r.wmid, r.winp, r.rhs
    wmid[0:hidden, 0:hidden] = held.wmid1[...]
    wmid[hidden:, hidden:] = held.wmid2[...]
    wmid_f = r.wmid_f
    wmid_f[...] = stack3(wmid[...], 1)
    hi, lo = split(held.wout2[...])
    r.w2_k[...] = jnp.concatenate([lo, hi, jnp.zeros_like(hi), hi], axis=0)
    winp[:, 0:hidden] = held.win1[...]
    winp[:, hidden:] = held.win2[...]
    row_i = lax.broadcasted_iota(jnp.int32, rhs.shape, 0) - 6 * n_basis
    lane_i = lax.broadcasted_iota(jnp.int32, rhs.shape, 1)
    which_block = lane_i >> 7
    part_row = row_i & 7
    hit = jnp.logical_and(which_block >= 2, part_row == which_block - 2)
    rhs[...] = jnp.where(hit & (row_i >= 0) & (row_i < 24), 1.0, 0.0)
    hi, lo = split(winp[...])
    for t in range(2):
        at = slice(LANES * t, LANES * (t + 1))
        base = 3 * n_basis * t
        rhs[base : base + n_basis, at] = hi.astype(f32)
        rhs[base + n_basis : base + 2 * n_basis, at] = hi.astype(f32)
        rhs[base + 2 * n_basis : base + 3 * n_basis, at] = lo.astype(f32)
    r.wide_rhs[...] = rhs[...].astype(bf16)

    v8 = r.v8
    v8[0:3, :] = held.vec[...]
    vectors = v8[...]
    dist = jnp.sqrt(jnp.sum(vectors * vectors, axis=0, keepdims=True))
    inv = 1.0 / dist
    unit = vectors * inv
    x1 = dist * (1.0 / cutoff_radius)
    x2 = x1 * x1
    x5 = x2 * x2 * x1
    x6 = x5 * x1
    env = 1.0 + x6 * (-28.0 + x1 * (48.0 - 21.0 * x1))
    denv = x5 * (-168.0 + x1 * (336.0 - 168.0 * x1)) * (1.0 / cutoff_radius)
    order_n = (lax.broadcasted_iota(jnp.int32, (n_basis, edges), 0) + 1).astype(f32)
    turns = order_n * x1
    near = jnp.floor(turns + 0.5)
    odd = near - 2.0 * jnp.floor(near * 0.5)
    sign = 1.0 - 2.0 * odd
    angle = (turns - near) * math.pi
    t2 = angle * angle
    sine = sign * angle * series(t2, 2, 7)
    cosine = sign * series(t2, 1, 7)
    norm = math.sqrt(2.0 / cutoff_radius)
    wave = (norm * inv) * sine
    basis = wave * env
    dbasis = ((norm * math.pi / cutoff_radius) * order_n * cosine * inv - wave * inv) * env + wave * denv

    def column(row):
        return to_column(row.astype(f32))

    species_row = held.species[...].astype(f32)
    counts_row = held.counts[...].astype(f32)
    species_col = column(species_row)
    counts_col = column(counts_row).astype(jnp.int32)
    list_col = column(held.list[...])
    listed_f = (list_col == lax.broadcasted_iota(jnp.int32, (G, atoms), 1).astype(f32)).astype(f32)
    listed = listed_f.astype(bf16)
    list_kinds = jnp.sum(listed_f * species_row, axis=1, keepdims=True)
    list_counts = jnp.sum(listed_f * counts_row, axis=1, keepdims=True).astype(jnp.int32)
    list_at = list_col.astype(jnp.int32) * slots

    def live_of(rows, start, count):
        spot = lax.broadcasted_iota(jnp.int32, (rows, edges), 1) - start
        return ((spot >= 0) & (spot < count)).astype(f32)

    live = live_of(atoms, lax.broadcasted_iota(jnp.int32, (atoms, edges), 0) * slots, counts_col)
    r.live[0:atoms, :] = live
    r.live[atoms:, :] = live_of(G, list_at, list_counts)
    live_row = jnp.sum(live, axis=0, keepdims=True)
    sent = held.senders[...]
    entry = jnp.where(sent >= atoms + 5 * G, sent - G, sent)
    src_hot = r.src_hot
    source = jnp.where(lax.broadcasted_iota(jnp.int32, src_hot.shape, 0) == entry, live_row, 0.0)
    src_hot[...] = source.astype(bf16)
    r.src_f[...] = source[atoms:, :]
    r.kind_own[...] = jnp.sum(source[0:atoms, :] * species_col, axis=0, keepdims=True)
    live_entry = jnp.where(live_row > 0.0, entry.astype(f32), -1.0)

    eight = lax.broadcasted_iota(jnp.int32, (8, edges), 0)
    unit = jnp.where(eight == 3, inv, jnp.where(eight == 4, live_entry, unit))
    b_hi, b_lo = split(basis)
    d_hi, d_lo = split(dbasis)
    parts = [b_hi, b_lo, b_hi, d_hi, d_lo, d_hi] + list(split3(unit))
    parts = [p.astype(f32) for p in parts] + [jnp.zeros((8, edges), f32)]
    r.pack[...] = jnp.concatenate(parts, axis=0).astype(bf16)

    hid_ref, th_ref, u_ref, inv_ref, ent_ref = r.hid, r.th, r.u, r.inv, r.ent
    p_hi, p_lo, rad_ref = r.p_hi, r.p_lo, r.rad

    def spread_w2(h):
        h_hi, h_lo = split(h)
        twice = jnp.where(lanes_low(h.shape), swap(h), h).astype(bf16)
        return mm(jnp.concatenate([twice, h_lo], axis=1), r.w2_k[...], 1, 0)

    for c in range(n_chunks):
        rows = rows_of(c)
        out = mm(r.pack[:, rows], r.wide_rhs[...], 0, 0)
        p1, t1 = out[:, 0:LANES], out[:, LANES : 2 * LANES]
        u = [out[:, LANES * k : LANES * (k + 1)] for k in (2, 3, 4)]
        u_ref[rows, :] = out[:, 2 * LANES : 5 * LANES]
        inv_ref[rows, :] = out[:, 5 * LANES : 6 * LANES]
        ent_ref[rows, :] = out[:, 6 * LANES : 7 * LANES]
        s1 = jax.nn.sigmoid(p1)
        h1 = p1 * s1
        th1 = (s1 * (1.0 + p1 * (1.0 - s1))) * t1
        p2 = dot_k(h1, wmid_f, 1)
        t2_ = dot_k(th1, wmid_f, 1)
        s2 = jax.nn.sigmoid(p2)
        h = p2 * s2
        hid_ref[rows, :] = h
        th_ref[rows, :] = (s2 * (1.0 + p2 * (1.0 - s2))) * t2_
        low = lanes_low(h.shape)
        hh = jnp.where(low, h, swap(h))
        prod = jnp.concatenate([hh * jnp.where(low, 1.0, u[0]), hh * jnp.where(low, u[1], u[2])], axis=1)
        hi, lo = split(prod)
        p_hi[rows, :] = hi
        p_lo[rows, :] = lo

    w1 = held.wout1[...]
    for ref, at, mix in ((r.wm0, 0, held.ms1), (r.wm1, 1, held.mv1)):
        path = w1[:, C * at : C * (at + 1)]
        with_kind = jnp.concatenate([path * held.embed[k : k + 1, :] for k in range(kinds_n)], axis=0)
        ref[...] = stack3(dot3(with_kind, mix[...], 1, 1) * scale, 1)
    r.mq1_f[...] = stack3(held.mq1[...], 1)
    initial = jnp.zeros((nodes, C), f32)
    node_kinds = jnp.concatenate([species_col, list_kinds], axis=0)
    for k in range(kinds_n):
        initial = jnp.where(node_kinds == k, held.embed[k : k + 1, :], initial)
    r.initial[...] = initial

    for c in range(n_chunks):
        rad_ref[rows_of(c), :] = spread_w2(hid_ref[rows_of(c), :])

    wait_in(0)
    wait_in(1)
    far = 8 * G
    rank = lax.broadcasted_iota(jnp.int32, (G, G), 1) == lax.broadcasted_iota(jnp.int32, (G, G), 0)
    lane_a = lax.broadcasted_iota(jnp.int32, (G, atoms), 1)
    kind_far = []
    for s in sides:
        there = jnp.sum(jnp.where(rank, r.lst[s].astype(f32), 0.0), axis=1, keepdims=True).astype(jnp.int32)
        kind_far.append(jnp.sum(jnp.where(lane_a == there, r.spc[s].astype(f32), 0.0), axis=1, keepdims=True))
    total = jnp.zeros((8, edges), f32)
    for s in sides:
        at = row_of(s) * G
        for m in range(G // 8):
            total = total + kind_far[row_of(s)][8 * m : 8 * m + 8] * r.src_f[at + 8 * m : at + 8 * m + 8, :]
    r.kind[...] = r.kind_own[...] + jnp.sum(total, axis=0, keepdims=True)

    listed_sum = None
    own_sums = []
    for c in range(n_chunks):
        rows = rows_of(c)
        kind = r.kind[:, rows]
        own = jnp.where(r.live[8 * c : 8 * c + 8, rows] > 0.0, kind, -1.0)
        far = jnp.where(r.live[atoms:, rows] > 0.0, kind, -1.0)
        hot = [(own == k).astype(f32) for k in range(kinds_n)] + [(far == k).astype(f32) for k in range(kinds_n)]
        hot = jnp.concatenate(hot, axis=0).astype(bf16)
        total = mm(hot, p_hi[rows, :], 1, 0) + mm(hot, p_lo[rows, :], 1, 0)
        own_sums.append(total[0 : 8 * kinds_n])
        tail = total[8 * kinds_n :]
        listed_sum = tail if listed_sum is None else listed_sum + tail
    by_kind = []
    for k in range(kinds_n):
        rows_k = [x[8 * k : 8 * (k + 1)] for x in own_sums] + [listed_sum[G * k : G * (k + 1)]]
        by_kind.append(jnp.concatenate(rows_k, axis=0))

    def turn(parts):
        out = []
        low = lanes_low((parts[0].shape[0], LANES))
        for j in range(4):
            at = slice(LANES * (j // 2), LANES * (j // 2 + 1))
            halves = []
            for m in (0, 2):
                first, second = parts[m][:, at], parts[m + 1][:, at]
                if j % 2 == 0:
                    halves.append(jnp.where(low, first, swap(second)))
                else:
                    halves.append(jnp.where(low, swap(first), second))
            out.append(jnp.concatenate(halves, axis=1))
        return out

    def dot_m(x, stacked):
        hi, lo = split(x)
        w_hi, w_lo = stacked[:, 0:C], stacked[:, 2 * C :]
        return mm(hi, w_hi, 1, 0) + (mm(lo, w_hi, 1, 0) + mm(hi, w_lo, 1, 0))

    turned = turn(by_kind)
    a1 = dot_m(turned[0], r.wm0)
    b1 = dot_m(jnp.concatenate(turned[1:], axis=0), r.wm1)
    b1 = [b1[k * nodes : (k + 1) * nodes] for k in range(3)]
    one_a = 1.0 + a1
    vec_one = [b * one_a for b in b1]
    for k in range(3):
        r.out_v[:, C * k : C * (k + 1)] = vec_one[k][atoms:]
    send_all(2)
    q1 = dot_k(a1 * a1 + (b1[0] * b1[0] + b1[1] * b1[1] + b1[2] * b1[2]), r.mq1_f, 1)
    scalar_one = r.initial[...] + a1 + q1
    r.out_s[...] = scalar_one[atoms:]
    send_all(3)
    r.node_a[...] = a1
    for k in range(3):
        r.node_b[:, C * k : C * (k + 1)] = b1[k]
    own_feats = [scalar_one[0:atoms]] + [v[0:atoms] for v in vec_one]
    r.scalar[...] = own_feats[0]

    tab2 = r.tab2
    for k in range(4):
        hi, lo = split(own_feats[k])
        tab2[0:atoms, C * k : C * (k + 1)] = hi
        tab2[atoms : 2 * atoms, C * k : C * (k + 1)] = lo

    rhp = r.rhp
    rhp[0 : held.rh.shape[0], :] = held.rh[...]
    r.rop[:, 0 : held.ro.shape[1]] = held.ro[...]
    rh_ms = dot3(rhp[...], held.ms2[...], 1, 0)
    rh_mq = dot3(rhp[...], held.mq2[...], 1, 0)
    r.msz_f[...] = stack3(jnp.concatenate([held.ms2[...], rh_ms], axis=0), 1)
    r.mv2_f[...] = stack3(held.mv2[...], 1)
    r.rhq_f[...] = stack3(rh_mq, 1)
    r.rhq_b[...] = stack3(jnp.concatenate([rhp[...], rh_mq], axis=1), 0)
    r.ms2_b[...] = stack3(held.ms2[...], 0)
    r.mv2_b[...] = stack3(held.mv2[...], 0)
    r.mq1_b[...] = stack3(held.mq1[...], 0)
    r.z0[...] = dot3(own_feats[0], rhp[...], 1, 1)

    ru_ref, x_ref, agg_ref, hot_g = r.ru, r.x, r.agg, r.hot_g

    def messages(rows, x):
        s, v = x[0], x[1:]
        ru = [ru_ref[rows, C * k : C * (k + 1)] for k in range(6)]
        r0, r3 = rad_ref[rows, 0:C], rad_ref[rows, 3 * C : 4 * C]
        first = r0 * s + ru[0] * v[0] + (ru[1] * v[1] + ru[2] * v[2])
        return [first] + [ru[3 + k] * s + r3 * v[k] for k in range(3)]

    def slot_sums(msgs):
        return [jnp.sum(m.reshape(8, slots, C), axis=1) for m in msgs]

    for c in range(n_chunks):
        rows = rows_of(c)
        u = [u_ref[rows, LANES * k : LANES * (k + 1)] for k in range(3)]
        for k in range(3):
            ru_ref[rows, C * k : C * (k + 1)] = rad_ref[rows, C : 2 * C] * u[k]
            ru_ref[rows, C * (k + 3) : C * (k + 4)] = rad_ref[rows, 2 * C : 3 * C] * u[k]
        ent = ent_ref[rows, :]
        lane = lax.broadcasted_iota(jnp.int32, ent.shape, 1).astype(f32)
        hot = (ent == lane + float(atoms)).astype(f32).astype(bf16)
        hot_g[rows, 0:LANES] = hot
        hot_g[rows, LANES:] = hot
        near_ent = jnp.where(ent < float(atoms), ent, -1000.0)
        hot = jnp.logical_and(
            near_ent >= 0.0, jnp.logical_or(near_ent == lane, near_ent + float(atoms) == lane)
        )
        x = mm(hot.astype(f32).astype(bf16), tab2[...], 1, 0)
        x_ref[rows, :] = x
        sums = slot_sums(messages(rows, [x[:, C * k : C * (k + 1)] for k in range(4)]))
        for k in range(4):
            agg_ref[8 * c : 8 * c + 8, C * k : C * (k + 1)] = sums[k]

    kind = r.kind[...]
    atom_i = lax.broadcasted_iota(jnp.int32, (atoms, edges), 0).astype(f32)
    at_atom = jnp.sum(r.live[0:atoms, :] * atom_i, axis=0, keepdims=True)
    any_live = jnp.sum(r.live[0:atoms, :], axis=0, keepdims=True)
    key_own = jnp.where(any_live > 0.0, kind * float(atoms) + at_atom, -1.0)
    list_i = lax.broadcasted_iota(jnp.int32, (G, edges), 0).astype(f32)
    at_list = jnp.sum(r.live[atoms:, :] * list_i, axis=0, keepdims=True)
    any_list = jnp.sum(r.live[atoms:, :], axis=0, keepdims=True)
    key_list = jnp.where(any_list > 0.0, kind * float(G) + at_list, -128.0)
    keys = jnp.concatenate([key_own, key_list, jnp.zeros((14, edges), f32)], axis=0).astype(bf16)
    key_shape = (16, 2 * LANES)
    key_rhs = lax.broadcasted_iota(jnp.int32, key_shape, 0) == (lax.broadcasted_iota(jnp.int32, key_shape, 1) >> 7)
    key_rhs = key_rhs.astype(f32).astype(bf16)
    key_own_hot, key_list_ref, jac, radp = r.key_own, r.key_list, r.jac, r.radp
    for c in range(n_chunks):
        rows = rows_of(c)
        out = mm(keys[:, rows], key_rhs, 0, 0)
        lane = lax.broadcasted_iota(jnp.int32, (chunk, LANES), 1).astype(f32)
        hot = (out[:, 0:LANES] == lane).astype(f32).astype(bf16)
        key_own_hot[rows, 0:LANES] = hot
        key_own_hot[rows, LANES:] = hot
        key_list_ref[rows, :] = out[:, LANES:]
        h, th, inv_c = hid_ref[rows, :], th_ref[rows, :], inv_ref[rows, :]
        u = [u_ref[rows, LANES * k : LANES * (k + 1)] for k in range(3)]
        low = lanes_low(h.shape)
        hp = jnp.where(low, th, swap(th))
        ww = jnp.where(low, h, swap(h)) * inv_c
        zz = hp - ww
        q0 = jnp.where(low, hp, zz * u[0])
        q1_ = zz * jnp.where(low, u[1], u[2])
        w_up, w_low = jnp.where(low, 0.0, ww), jnp.where(low, ww, 0.0)
        both = [
            (u[0] * q0 + w_up, u[0] * q1_),
            (u[1] * q0, u[1] * q1_ + w_low),
            (u[2] * q0, u[2] * q1_ + w_up),
        ]
        for k in range(3):
            jac[rows, 2 * LANES * k : 2 * LANES * k + LANES] = both[k][0]
            jac[rows, 2 * LANES * k + LANES : 2 * LANES * (k + 1)] = both[k][1]
        rp = spread_w2(th)
        for k in range(4):
            col = rp[:, C * k : C * (k + 1)]
            if k in (1, 2):
                col = col - inv_c * rad_ref[rows, C * k : C * (k + 1)]
            radp[rows, C * k : C * (k + 1)] = col

    starts = [list_s[0, g] * slots for g in range(G)]
    src_t = r.src_t
    list_edges = G * slots
    for g in range(G):
        rows = slice(g * slots, (g + 1) * slots)
        key = key_list_ref[pl.ds(starts[g], slots), :]
        lane = lax.broadcasted_iota(jnp.int32, key.shape, 1).astype(f32)
        rank = kinds_n * G
        hot = jnp.logical_or(key == lane, key + float(rank) == lane)
        r.key_hot[rows, :] = jnp.where(key >= 0.0, hot.astype(f32), 0.0).astype(bf16)
        src_t[rows, :] = ent_ref[pl.ds(starts[g], slots), :]
    lane = lax.broadcasted_iota(jnp.int32, (list_edges, LANES), 1).astype(f32)
    r.src_gl[...] = jnp.transpose((src_t[...] == lane + float(atoms)).astype(f32)).astype(bf16)
    near = jnp.transpose((src_t[...] == lane).astype(f32))[0:atoms, :]
    spot = lax.broadcasted_iota(jnp.int32, (G, list_edges), 1) - lax.broadcasted_iota(
        jnp.int32, (G, list_edges), 0
    ) * slots
    blocks = ((spot >= 0) & (spot < slots)).astype(f32).astype(bf16)
    r.own_l[...] = (mm(listed, blocks, 0, 0) - near).astype(bf16)
    r.own_all[...] = (r.live[0:atoms, :] - src_hot[0:atoms, :].astype(f32)).astype(bf16)

    wait_in(2)
    wait_in(3)
    tab_g = r.tab_g
    entries_g = 8 * G
    hi, lo = split(r.ghost_v[...])
    tab_g[0:entries_g, C:] = hi
    tab_g[entries_g:, C:] = lo
    hi, lo = split(r.ghost_s[...])
    tab_g[0:entries_g, 0:C] = hi
    tab_g[entries_g:, 0:C] = lo
    xg_ref = r.xg
    for c in range(n_chunks):
        rows = rows_of(c)
        x = mm(hot_g[rows, :], tab_g[...], 1, 0)
        xg_ref[rows, :] = x
        sums = slot_sums(messages(rows, [x[:, C * k : C * (k + 1)] for k in range(4)]))
        for k in range(4):
            at = (slice(8 * c, 8 * c + 8), slice(C * k, C * (k + 1)))
            agg_ref[at] = (agg_ref[at] + sums[k]) * scale
    az = dot_k(agg_ref[:, 0:C], r.msz_f, 1)
    a2 = az[:, 0:C]
    b2 = dot_k(jnp.concatenate([agg_ref[:, C * k : C * (k + 1)] for k in (1, 2, 3)], axis=0), r.mv2_f, 1)
    b2 = [b2[k * atoms : (k + 1) * atoms] for k in range(3)]
    squares = a2 * a2 + (b2[0] * b2[0] + b2[1] * b2[1] + b2[2] * b2[2])
    z = r.z0[...] + az[:, C:] + dot_k(squares, r.rhq_f, 1)
    sz = jax.nn.sigmoid(z)
    dz = r.rop[...] * (sz * (1.0 + z * (1.0 - sz)))
    down = dot_k(dz, r.rhq_b, 0)
    ds_two, dq2 = down[:, 0:C], down[:, C:]
    dagg = r.dagg
    dagg[:, 0:C] = dot_k(ds_two + 2.0 * a2 * dq2, r.ms2_b, 0) * scale
    db = dot_k(jnp.concatenate([2.0 * b * dq2 for b in b2], axis=0), r.mv2_b, 0) * scale
    for k in range(3):
        dagg[:, C * (k + 1) : C * (k + 2)] = db[k * atoms : (k + 1) * atoms]

    def spread_rows(c):
        group = slice(c * 8, (c + 1) * 8)
        out = []
        for k in range(4):
            small = dagg[group, C * k : C * (k + 1)]
            out.append(jnp.broadcast_to(small[:, None, :], (8, slots, C)).reshape(chunk, C))
        return out

    def scatter(first, which):
        hi_ref, lo_ref = r.dx_hi, r.dx_lo
        for c in range(n_chunks):
            rows = rows_of(c)
            d = spread_rows(c)
            for n, k in enumerate(which):
                if k == 0:
                    ru = [ru_ref[rows, C * (3 + m) : C * (4 + m)] for m in range(3)]
                    g = rad_ref[rows, 0:C] * d[0] + ru[0] * d[1] + (ru[1] * d[2] + ru[2] * d[3])
                else:
                    g = ru_ref[rows, C * (k - 1) : C * k] * d[0] + rad_ref[rows, 3 * C : 4 * C] * d[k]
                at = slice(C * (first + n), C * (first + n + 1))
                hi_ref[rows, at], lo_ref[rows, at] = split(g)

    def gather_grads(hot, first):
        at = slice(C * first, C * (first + 2))
        return mm(hot, r.dx_hi[:, at], 1, 0) + mm(hot, r.dx_lo[:, at], 1, 0)

    ghost_hot = slice(atoms, None)
    scatter(0, (1, 2))
    r.grad_a[...] = gather_grads(src_hot[ghost_hot, :], 0)
    send_all(4)
    scatter(2, (3, 0))
    r.grad_b[...] = gather_grads(src_hot[ghost_hot, :], 2)
    send_all(5)

    lin8 = jnp.broadcast_to(held.lin[...], (8, C))
    ro8 = jnp.broadcast_to(r.rop[...], (8, LANES))
    energy = dot3(lin8, r.scalar[...], 1, 1) + dot3(ro8, z * sz, 1, 1)
    r.eout[...] = energy[0:1, :]

    def node_grads(ds, dv, rows):
        a = r.node_a[rows, :]
        b = [r.node_b[rows, C * k : C * (k + 1)] for k in range(3)]
        dq = dot_k(ds, r.mq1_b, 0)
        da = ds + 2.0 * a * dq + (dv[0] * b[0] + dv[1] * b[1] + dv[2] * b[2])
        db = jnp.concatenate([dv[k] * (1.0 + a) + 2.0 * b[k] * dq for k in range(3)], axis=0)
        n = ds.shape[0]
        back = dot_k(db, r.wm1, 1)
        back = [dot_k(da, r.wm0, 1)] + [back[k * n : (k + 1) * n] for k in range(3)]
        hi, lo = split(jnp.concatenate(turn(back), axis=0))
        return jnp.concatenate([hi, lo], axis=0)

    def lane_put(sums):
        lane = lax.broadcasted_iota(jnp.int32, sums[0].shape, 1)
        out = jnp.zeros(sums[0].shape, f32)
        for k in range(3):
            out = jnp.where(lane == k, jnp.sum(sums[k], axis=1, keepdims=True), out)
        return out

    own_a = gather_grads(src_hot[0:atoms, :], 0)
    own_b = gather_grads(src_hot[0:atoms, :], 2)
    ds_own = own_b[:, C:] + ds_two + held.lin[...]
    r.gp[...] = node_grads(ds_own, [own_a[:, 0:C], own_a[:, C:], own_b[:, 0:C]], slice(0, atoms))
    f_own = r.f_own
    for c in range(n_chunks):
        rows = rows_of(c)
        d = spread_rows(c)
        x = [x_ref[rows, C * k : C * (k + 1)] + xg_ref[rows, C * k : C * (k + 1)] for k in range(4)]
        s, v = x[0], x[1:]
        u = [u_ref[rows, LANES * k : LANES * (k + 1)] for k in range(3)]
        rp = [radp[rows, C * k : C * (k + 1)] for k in range(4)]
        uv = u[0] * v[0] + u[1] * v[1] + u[2] * v[2]
        ud = u[0] * d[1] + u[1] * d[2] + u[2] * d[3]
        dv = d[1] * v[0] + d[2] * v[1] + d[3] * v[2]
        along = rp[0] * (d[0] * s) + rp[1] * (d[0] * uv) + (rp[2] * (s * ud) + rp[3] * dv)
        r1d = (rad_ref[rows, C : 2 * C] * d[0]) * inv_ref[rows, :]
        r2s = (rad_ref[rows, 2 * C : 3 * C] * s) * inv_ref[rows, :]
        g = mm(key_own_hot[rows, :], r.gp[...], 1, 0)
        g0, g1 = g[:, 0:LANES], g[:, LANES:]
        sums = []
        for k in range(3):
            j0 = jac[rows, 2 * LANES * k : 2 * LANES * k + LANES]
            j1 = jac[rows, 2 * LANES * k + LANES : 2 * LANES * (k + 1)]
            sums.append((u[k] * along + r1d * v[k]) + (r2s * d[k + 1] + (g0 * j0 + g1 * j1)))
        f_own[rows, :] = lane_put(sums)
    hi, mid, lo = split3(f_own[...])
    hot = src_hot[ghost_hot, :]
    r.force_o[...] = mm(hot, hi, 1, 0) + (mm(hot, mid, 1, 0) + mm(hot, lo, 1, 0))

    wait_in(4)
    wait_in(5)

    def total(ref):
        out = [ref[k] for k in range(8)]
        while len(out) > 1:
            out = [out[i] + out[i + 1] for i in range(0, len(out), 2)]
        return out[0]

    g_a, g_b = total(r.in_a), total(r.in_b)
    gp_l = node_grads(g_b[:, C:], [g_a[:, 0:C], g_a[:, C:], g_b[:, 0:C]], slice(atoms, nodes))
    f_list = []
    for g in range(G):
        rows = slice(g * slots, (g + 1) * slots)
        at = pl.ds(starts[g], slots)
        if g % 4 == 0:
            wide = mm(r.key_hot[g * slots : (g + 4) * slots, :], gp_l, 1, 0)
        m = g % 4
        here = wide[m * slots : (m + 1) * slots]
        g0, g1 = here[:, 0:LANES], here[:, LANES:]
        sums = []
        for k in range(3):
            j0 = jac[at, 2 * LANES * k : 2 * LANES * k + LANES]
            j1 = jac[at, 2 * LANES * k + LANES : 2 * LANES * (k + 1)]
            sums.append(g0 * j0 + g1 * j1)
        f_list.append(lane_put(sums))
    f_list = jnp.concatenate(f_list, axis=0)
    l_hi, l_mid, l_lo = split3(f_list)
    hot = r.src_gl[...]
    r.force_g[...] = r.force_o[...] + (mm(hot, l_hi, 1, 0) + (mm(hot, l_mid, 1, 0) + mm(hot, l_lo, 1, 0)))
    send_all(6)
    own, own_l = r.own_all[...], r.own_l[...]
    force = mm(hi, own, 0, 1) + (mm(mid, own, 0, 1) + mm(lo, own, 0, 1))
    force = force + (mm(l_hi, own_l, 0, 1) + (mm(l_mid, own_l, 0, 1) + mm(l_lo, own_l, 0, 1)))
    for phase in range(6):
        wait_out(phase)
    wait_in(6)
    hi, mid, lo = split3(total(r.in_f))
    late = mm(hi, listed, 0, 0) + (mm(mid, listed, 0, 0) + mm(lo, listed, 0, 0))
    r.fout[...] = (force - late)[0:3, :]
    wait_out(6)


def store_kernel(e_ref, f_ref, eo_ref, fo_ref, sem):
    one = pltpu.make_async_copy(e_ref, eo_ref, sem.at[0])
    two = pltpu.make_async_copy(f_ref, fo_ref, sem.at[1])
    one.start()
    two.start()
    one.wait()
    two.wait()


def in_order(vec, senders, counts, species, list, embed, win1, wmid1, wout1, ms1, mv1, mq1, win2, wmid2, wout2, ms2, mv2, mq2, lin, rh, ro):
    return dict(locals())


def on_device(n_dom, n_sub, *args):
    (vec, senders, counts, species, send_list, embed) = args[:6]
    weights = list(args[6:18])
    read_lin, read_hidden, read_out = args[18:]
    edges = vec.shape[1]
    atoms = species.shape[0]
    G = send_list.shape[0]
    C, kinds_n = embed.shape
    hidden, n_basis = weights[0].shape
    for i in (0, 2, 6, 8):
        weights[i] = weights[i].T
    row = lambda x: x.reshape(1, -1)
    operands = [vec, row(senders), row(counts), row(species), row(send_list), embed.T, *weights]
    operands += [row(read_lin), read_hidden, row(read_out)]
    far, nodes, list_edges = 8 * G, atoms + G, G * (edges // atoms)
    i32 = jnp.int32
    packed = -(-(6 * n_basis + 24) // 16) * 16
    inputs = in_order(*operands)
    scratch = dict(
        spc=((9, 1, atoms), i32),
        lst=((9, 1, G), i32),
        out_v=((G, 3 * C), f32),
        out_s=((G, C), f32),
        ghost_v=((far, 3 * C), f32),
        ghost_s=((far, C), f32),
        grad_a=((far, 2 * C), f32),
        grad_b=((far, 2 * C), f32),
        in_a=((8, G, 2 * C), f32),
        in_b=((8, G, 2 * C), f32),
        force_g=((far, LANES), f32),
        force_o=((far, LANES), f32),
        in_f=((8, G, LANES), f32),
        rhs=((packed, 7 * LANES), f32),
        wide_rhs=((packed, 7 * LANES), bf16),
        pack=((packed, edges), bf16),
        v8=((8, edges), f32),
        winp=((n_basis, LANES), f32),
        wmid=((LANES, LANES), f32),
        wmid_f=((LANES, 3 * LANES), bf16),
        w2_k=((2 * LANES, 4 * C), bf16),
        rhp=((LANES, C), f32),
        rop=((1, LANES), f32),
        kind_own=((1, edges), f32),
        src_f=((far, edges), f32),
        kind=((1, edges), f32),
        live=((nodes, edges), f32),
        src_hot=((atoms + far, edges), bf16),
        hid=((edges, LANES), f32),
        th=((edges, LANES), f32),
        u=((edges, 3 * LANES), f32),
        inv=((edges, LANES), f32),
        ent=((edges, LANES), f32),
        p_hi=((edges, 2 * LANES), bf16),
        p_lo=((edges, 2 * LANES), bf16),
        rad=((edges, 4 * C), f32),
        radp=((edges, 4 * C), f32),
        ru=((edges, 6 * C), f32),
        jac=((edges, 6 * LANES), f32),
        wm0=((kinds_n * hidden, 3 * C), bf16),
        wm1=((kinds_n * hidden, 3 * C), bf16),
        mq1_f=((C, 3 * C), bf16),
        mq1_b=((3 * C, C), bf16),
        msz_f=((C + LANES, 3 * C), bf16),
        mv2_f=((C, 3 * C), bf16),
        rhq_f=((LANES, 3 * C), bf16),
        rhq_b=((3 * LANES, 2 * C), bf16),
        ms2_b=((3 * C, C), bf16),
        mv2_b=((3 * C, C), bf16),
        initial=((nodes, C), f32),
        node_a=((nodes, C), f32),
        node_b=((nodes, 3 * C), f32),
        scalar=((atoms, C), f32),
        z0=((atoms, LANES), f32),
        tab2=((LANES, 4 * C), bf16),
        tab_g=((2 * far, 4 * C), bf16),
        hot_g=((edges, 2 * LANES), bf16),
        x=((edges, 4 * C), f32),
        xg=((edges, 4 * C), f32),
        agg=((atoms, 4 * C), f32),
        dagg=((atoms, 4 * C), f32),
        key_own=((edges, 2 * LANES), bf16),
        key_list=((edges, LANES), f32),
        key_hot=((list_edges, LANES), bf16),
        src_t=((list_edges, LANES), f32),
        src_gl=((far, list_edges), bf16),
        own_l=((atoms, list_edges), bf16),
        own_all=((atoms, edges), bf16),
        dx_hi=((edges, 4 * C), bf16),
        dx_lo=((edges, 4 * C), bf16),
        gp=((2 * kinds_n * atoms, 2 * LANES), bf16),
        f_own=((edges, LANES), f32),
    )
    names = list(inputs) + ["eout", "fout"] + [k + "_" for k in inputs] + list(scratch)
    copies = [pltpu.VMEM(x.shape, x.dtype) for x in operands]
    hbm = pl.BlockSpec(memory_space=pltpu.HBM)
    whole = pl.BlockSpec(memory_space=pltpu.VMEM)
    out = pl.pallas_call(
        functools.partial(kernel, n_dom, n_sub, names),
        out_shape=[pltpu.VMEM((1, atoms), f32), pltpu.VMEM((3, atoms), f32)],
        in_specs=[hbm] * len(operands),
        out_specs=[whole, whole],
        scratch_shapes=copies
        + [pltpu.VMEM(shape, dtype) for shape, dtype in scratch.values()]
        + [pltpu.SMEM((1, G), i32)]
        + [pltpu.SemaphoreType.DMA((7, 9)), pltpu.SemaphoreType.DMA((7, 9))]
        + [pltpu.SemaphoreType.DMA((len(operands) + 1,))],
        compiler_params=pltpu.CompilerParams(
            collective_id=0, has_side_effects=True, vmem_limit_bytes=56 * 1024 * 1024
        ),
    )(*operands)
    out = pl.pallas_call(
        store_kernel,
        out_shape=[jax.ShapeDtypeStruct((1, atoms), f32), jax.ShapeDtypeStruct((3, atoms), f32)],
        in_specs=[whole, whole],
        out_specs=[hbm, hbm],
        scratch_shapes=[pltpu.SemaphoreType.DMA((2,))],
    )(*[pltpu.with_memory_space_constraint(o, pltpu.VMEM) for o in out])
    return out[0].reshape(atoms), out[1]


def solution(mesh):
    one = P(("dom", "sub"))
    return jax.shard_map(
        functools.partial(on_device, mesh.shape["dom"], mesh.shape["sub"]),
        mesh=mesh,
        in_specs=(P(None, ("dom", "sub")), one, one, one, one) + (P(),) * 16,
        out_specs=(one, P(None, ("dom", "sub"))),
        check_vma=False,
    )
```

```python
import functools
import math
import types

import jax
import jax.numpy as jnp
from jax import lax
from jax.experimental import pallas as pl
from jax.experimental.pallas import tpu as pltpu
from jax.sharding import PartitionSpec as P

cutoff_radius = 5.0
f32 = jnp.float32
bf16 = jnp.bfloat16
LANES = 128
MESH = pl.DeviceIdType.MESH


def mm(a, b, ca, cb):
    return lax.dot_general(a, b, (((ca,), (cb,)), ((), ())), preferred_element_type=f32)


def split(x):
    hi = x.astype(bf16)
    return hi, (x - hi.astype(f32)).astype(bf16)


def split3(x):
    hi = x.astype(bf16)
    rest = x - hi.astype(f32)
    mid = rest.astype(bf16)
    return hi, mid, (rest - mid.astype(f32)).astype(bf16)


def dot3(a, b, ca, cb):
    a_hi, a_lo = split(a)
    b_hi, b_lo = split(b)
    return mm(a_hi, b_hi, ca, cb) + (mm(a_hi, b_lo, ca, cb) + mm(a_lo, b_hi, ca, cb))


def hot3(hot, x, ca, cb):
    hi, mid, lo = split3(x)
    return mm(hot, hi, ca, cb) + (mm(hot, mid, ca, cb) + mm(hot, lo, ca, cb))


def to_column(row):
    count = row.shape[1]
    shape = (count, count)
    same = lax.broadcasted_iota(jnp.int32, shape, 0) == lax.broadcasted_iota(jnp.int32, shape, 1)
    return jnp.sum(jnp.where(same, row, 0.0), axis=1, keepdims=True)


def series(t, first, terms):
    total = jnp.ones_like(t)
    for i in reversed(range(terms)):
        low = first + 2 * i
        total = 1.0 - t * (1.0 / (low * (low + 1))) * total
    return total


def kernel(n_dom, n_sub, names, *refs):
    r = types.SimpleNamespace(**dict(zip(names, refs)))
    inputs = len(in_order(*range(21)))
    hbm = types.SimpleNamespace(**dict(zip(names[:inputs], refs[:inputs])))
    held = types.SimpleNamespace(**dict(zip(names[:inputs], refs[inputs + 2 : 2 * inputs + 2])))
    list_s, send_sem, recv_sem, in_sem = refs[-4:]
    dm, sb = lax.axis_index("dom"), lax.axis_index("sub")
    atoms = hbm.species.shape[1]
    edges = hbm.vec.shape[1]
    slots = edges // atoms
    G = hbm.list.shape[1]
    kinds_n, C = hbm.embed.shape
    n_basis, hidden = hbm.win1.shape
    chunk = 8 * slots
    n_chunks = edges // chunk
    scale = slots ** (-0.5)
    sides = [s for s in range(9) if s != 4]
    nodes = atoms + G

    def exists(s):
        ok = None
        for here, count, off in ((dm, n_dom, s // 3 - 1), (sb, n_sub, s % 3 - 1)):
            if off == 0:
                continue
            one = here > 0 if off < 0 else here < count - 1
            ok = one if ok is None else jnp.logical_and(ok, one)
        return ok

    def place(s):
        return (dm + (s // 3 - 1), sb + (s % 3 - 1))

    def row_of(s):
        return s if s < 4 else s - 1

    def block(s):
        return pl.ds(G * row_of(s), G)

    def copies(phase, s, there):
        o = 8 - s
        src, dst = (
            lambda: (r.kind_out, r.ghost_kind.at[block(o)]),
            lambda: (r.out_v, r.ghost_v.at[block(o)]),
            lambda: (r.out_s, r.ghost_s.at[block(o)]),
            lambda: (r.grad_a.at[block(s)], r.in_a.at[row_of(o)]),
            lambda: (r.grad_b.at[block(s)], r.in_b.at[row_of(o)]),
            lambda: (r.force_g.at[block(s)], r.in_f.at[row_of(o)]),
        )[phase]()
        return pltpu.make_async_remote_copy(
            src_ref=src,
            dst_ref=dst,
            send_sem=send_sem.at[phase, s],
            recv_sem=recv_sem.at[phase, o],
            device_id=place(there),
            device_id_type=MESH,
        )

    def send_all(phase):
        for s in sides:
            @pl.when(exists(s))
            def _():
                copies(phase, s, s).start()

    def wait_in(phase):
        for s in sides:
            @pl.when(exists(s))
            def _():
                copies(phase, 8 - s, s).wait_recv()

    def wait_out(phase):
        for s in sides:
            @pl.when(exists(s))
            def _():
                copies(phase, s, s).wait_send()

    groups = [
        [hbm.species, hbm.list],
        [hbm.vec, hbm.counts, hbm.senders, hbm.win1, hbm.win2, hbm.wmid1, hbm.wmid2],
        [hbm.wout1, hbm.embed, hbm.ms1, hbm.mv1, hbm.mq1, hbm.wout2],
    ]
    groups.append([x for x in refs[:inputs] if not any(x is y for group in groups for y in group)])
    inside = dict(zip(map(id, refs[:inputs]), refs[inputs + 2 : 2 * inputs + 2]))
    spots = {id(x): i for i, x in enumerate(refs[:inputs])}
    pulls = [[pltpu.make_async_copy(x, inside[id(x)], in_sem.at[spots[id(x)]]) for x in group] for group in groups]
    pulls[3].append(pltpu.make_async_copy(hbm.list, list_s, in_sem.at[inputs]))

    def start(group):
        for pull in pulls[group]:
            pull.start()

    def arrive(group):
        for pull in pulls[group]:
            pull.wait()

    for group in range(4):
        start(group)
    for ref in (r.ghost_kind, r.ghost_v, r.ghost_s, r.in_a, r.in_b, r.in_f):
        ref[...] = jnp.zeros_like(ref)
    barrier = pltpu.get_barrier_semaphore()
    for s in sides:
        @pl.when(exists(s))
        def _():
            pl.semaphore_signal(barrier, inc=1, device_id=place(s), device_id_type=MESH)
    peers = [
        1 + jnp.where(at > 0, 1, 0) + jnp.where(at < count - 1, 1, 0)
        for at, count in ((dm, n_dom), (sb, n_sub))
    ]

    for ref in (r.rhs, r.v8, r.winp, r.wmid, r.rhp, r.rop, r.tab2):
        ref[...] = jnp.zeros_like(ref)
    arrive(0)
    species_row = held.species[...].astype(f32)
    species_col = to_column(species_row)
    list_col = to_column(held.list[...].astype(f32))
    listed_f = (list_col == lax.broadcasted_iota(jnp.int32, (G, atoms), 1).astype(f32)).astype(f32)
    listed = listed_f.astype(bf16)
    list_kinds = jnp.sum(listed_f * species_row, axis=1, keepdims=True)
    r.kind_out[...] = jnp.broadcast_to(list_kinds, (G, LANES))
    pl.semaphore_wait(barrier, peers[0] * peers[1] - 1)
    send_all(0)
    arrive(1)

    def lanes_low(shape):
        return lax.broadcasted_iota(jnp.int32, shape, 1) < hidden

    def swap(x):
        return pltpu.roll(x, hidden, 1)

    def stack3(x, axis):
        hi, lo = split(x)
        return jnp.concatenate([hi, hi, lo], axis=axis)

    def dot_k(a, stacked, dim):
        k = a.shape[1]
        a_hi, a_lo = split(a)
        both = jnp.concatenate([a_hi, a_lo], axis=1)
        if dim == 1:
            first, last = stacked[:, : 2 * k], stacked[:, 2 * k :]
        else:
            first, last = stacked[: 2 * k, :], stacked[2 * k :, :]
        return mm(both, first, 1, dim) + mm(a_hi, last, 1, dim)

    def rows_of(c):
        return slice(c * chunk, (c + 1) * chunk)

    wmid, winp, rhs = r.wmid, r.winp, r.rhs
    wmid[0:hidden, 0:hidden] = held.wmid1[...]
    wmid[hidden:, hidden:] = held.wmid2[...]
    wmid_f = r.wmid_f
    wmid_f[...] = stack3(wmid[...], 1)
    winp[:, 0:hidden] = held.win1[...]
    winp[:, hidden:] = held.win2[...]
    row_i = lax.broadcasted_iota(jnp.int32, rhs.shape, 0) - 6 * n_basis
    lane_i = lax.broadcasted_iota(jnp.int32, rhs.shape, 1)
    which_block = lane_i >> 7
    part_row = row_i & 7
    hit = jnp.logical_and(which_block >= 2, part_row == which_block - 2)
    rhs[...] = jnp.where(hit & (row_i >= 0) & (row_i < 24), 1.0, 0.0)
    hi, lo = split(winp[...])
    for t in range(2):
        at = slice(LANES * t, LANES * (t + 1))
        base = 3 * n_basis * t
        rhs[base : base + n_basis, at] = hi.astype(f32)
        rhs[base + n_basis : base + 2 * n_basis, at] = hi.astype(f32)
        rhs[base + 2 * n_basis : base + 3 * n_basis, at] = lo.astype(f32)
    r.wide_rhs[...] = rhs[...].astype(bf16)

    v8 = r.v8
    v8[0:3, :] = held.vec[...]
    vectors = v8[...]
    dist = jnp.sqrt(jnp.sum(vectors * vectors, axis=0, keepdims=True))
    inv = 1.0 / dist
    unit = vectors * inv
    x1 = dist * (1.0 / cutoff_radius)
    x2 = x1 * x1
    x5 = x2 * x2 * x1
    x6 = x5 * x1
    env = 1.0 + x6 * (-28.0 + x1 * (48.0 - 21.0 * x1))
    denv = x5 * (-168.0 + x1 * (336.0 - 168.0 * x1)) * (1.0 / cutoff_radius)
    order_n = (lax.broadcasted_iota(jnp.int32, (n_basis, edges), 0) + 1).astype(f32)
    turns = order_n * x1
    near = jnp.floor(turns + 0.5)
    odd = near - 2.0 * jnp.floor(near * 0.5)
    sign = 1.0 - 2.0 * odd
    angle = (turns - near) * math.pi
    t2 = angle * angle
    sine = sign * angle * series(t2, 2, 7)
    cosine = sign * series(t2, 1, 7)
    norm = math.sqrt(2.0 / cutoff_radius)
    wave = (norm * inv) * sine
    basis = wave * env
    dbasis = ((norm * math.pi / cutoff_radius) * order_n * cosine * inv - wave * inv) * env + wave * denv

    counts_row = held.counts[...].astype(f32)
    counts_col = to_column(counts_row).astype(jnp.int32)
    list_counts = jnp.sum(listed_f * counts_row, axis=1, keepdims=True).astype(jnp.int32)
    list_at = list_col.astype(jnp.int32) * slots

    def live_of(rows, start, count):
        spot = lax.broadcasted_iota(jnp.int32, (rows, edges), 1) - start
        return ((spot >= 0) & (spot < count)).astype(f32)

    live = live_of(atoms, lax.broadcasted_iota(jnp.int32, (atoms, edges), 0) * slots, counts_col)
    r.live[0:atoms, :] = live
    r.live[atoms:, :] = live_of(G, list_at, list_counts)
    live_row = jnp.sum(live, axis=0, keepdims=True)
    sent = held.senders[...]
    entry = jnp.where(sent >= atoms + 5 * G, sent - G, sent)
    src_hot = r.src_hot
    source = jnp.where(lax.broadcasted_iota(jnp.int32, src_hot.shape, 0) == entry, live_row, 0.0)
    src_hot[...] = source.astype(bf16)
    r.src_f[...] = source[atoms:, :]
    r.kind_own[...] = jnp.sum(source[0:atoms, :] * species_col, axis=0, keepdims=True)
    live_entry = jnp.where(live_row > 0.0, entry.astype(f32), -1.0)

    eight = lax.broadcasted_iota(jnp.int32, (8, edges), 0)
    unit = jnp.where(eight == 3, inv, jnp.where(eight == 4, live_entry, unit))
    b_hi, b_lo = split(basis)
    d_hi, d_lo = split(dbasis)
    parts = [b_hi, b_lo, b_hi, d_hi, d_lo, d_hi] + list(split3(unit))
    parts = [p.astype(f32) for p in parts] + [jnp.zeros((8, edges), f32)]
    r.pack[...] = jnp.concatenate(parts, axis=0).astype(bf16)

    hid_ref, th_ref, u_ref, inv_ref, ent_ref = r.hid, r.th, r.u, r.inv, r.ent
    p_hi, p_lo, rad_ref = r.p_hi, r.p_lo, r.rad

    def spread_w2(h):
        h_hi, h_lo = split(h)
        twice = jnp.where(lanes_low(h.shape), swap(h), h).astype(bf16)
        return mm(jnp.concatenate([twice, h_lo], axis=1), r.w2_k[...], 1, 0)

    for c in range(n_chunks):
        rows = rows_of(c)
        out = mm(r.pack[:, rows], r.wide_rhs[...], 0, 0)
        p1, t1 = out[:, 0:LANES], out[:, LANES : 2 * LANES]
        u = [out[:, LANES * k : LANES * (k + 1)] for k in (2, 3, 4)]
        u_ref[rows, :] = out[:, 2 * LANES : 5 * LANES]
        inv_ref[rows, :] = out[:, 5 * LANES : 6 * LANES]
        ent_ref[rows, :] = out[:, 6 * LANES : 7 * LANES]
        s1 = jax.nn.sigmoid(p1)
        h1 = p1 * s1
        th1 = (s1 * (1.0 + p1 * (1.0 - s1))) * t1
        p2 = dot_k(h1, wmid_f, 1)
        t2_ = dot_k(th1, wmid_f, 1)
        s2 = jax.nn.sigmoid(p2)
        h = p2 * s2
        hid_ref[rows, :] = h
        th_ref[rows, :] = (s2 * (1.0 + p2 * (1.0 - s2))) * t2_
        low = lanes_low(h.shape)
        hh = jnp.where(low, h, swap(h))
        prod = jnp.concatenate([hh * jnp.where(low, 1.0, u[0]), hh * jnp.where(low, u[1], u[2])], axis=1)
        hi, lo = split(prod)
        p_hi[rows, :] = hi
        p_lo[rows, :] = lo

    arrive(2)
    hi, lo = split(held.wout2[...])
    r.w2_k[...] = jnp.concatenate([lo, hi, jnp.zeros_like(hi), hi], axis=0)
    w1 = held.wout1[...]
    for ref, at, mix in ((r.wm0, 0, held.ms1), (r.wm1, 1, held.mv1)):
        path = w1[:, C * at : C * (at + 1)]
        with_kind = jnp.concatenate([path * held.embed[k : k + 1, :] for k in range(kinds_n)], axis=0)
        ref[...] = stack3(dot3(with_kind, mix[...], 1, 1) * scale, 1)
    r.mq1_f[...] = stack3(held.mq1[...], 1)
    initial = jnp.zeros((nodes, C), f32)
    node_kinds = jnp.concatenate([species_col, list_kinds], axis=0)
    for k in range(kinds_n):
        initial = jnp.where(node_kinds == k, held.embed[k : k + 1, :], initial)
    r.initial[...] = initial

    for c in range(n_chunks):
        rad_ref[rows_of(c), :] = spread_w2(hid_ref[rows_of(c), :])

    wait_in(0)
    total = jnp.zeros((8, edges), f32)
    for s in sides:
        for m in range(G // 8):
            at = slice(row_of(s) * G + 8 * m, row_of(s) * G + 8 * m + 8)
            total = total + r.ghost_kind[at, 0:1] * r.src_f[at, :]
    r.kind[...] = r.kind_own[...] + jnp.sum(total, axis=0, keepdims=True)

    listed_sum = None
    own_sums = []
    for c in range(n_chunks):
        rows = rows_of(c)
        kind = r.kind[:, rows]
        own = jnp.where(r.live[8 * c : 8 * c + 8, rows] > 0.0, kind, -1.0)
        far = jnp.where(r.live[atoms:, rows] > 0.0, kind, -1.0)
        hot = [(own == k).astype(f32) for k in range(kinds_n)] + [(far == k).astype(f32) for k in range(kinds_n)]
        hot = jnp.concatenate(hot, axis=0).astype(bf16)
        total = mm(hot, p_hi[rows, :], 1, 0) + mm(hot, p_lo[rows, :], 1, 0)
        own_sums.append(total[0 : 8 * kinds_n])
        tail = total[8 * kinds_n :]
        listed_sum = tail if listed_sum is None else listed_sum + tail
    by_kind = []
    for k in range(kinds_n):
        rows_k = [x[8 * k : 8 * (k + 1)] for x in own_sums] + [listed_sum[G * k : G * (k + 1)]]
        by_kind.append(jnp.concatenate(rows_k, axis=0))

    def turn(parts):
        out = []
        low = lanes_low((parts[0].shape[0], LANES))
        for j in range(4):
            at = slice(LANES * (j // 2), LANES * (j // 2 + 1))
            halves = []
            for m in (0, 2):
                first, second = parts[m][:, at], parts[m + 1][:, at]
                if j % 2 == 0:
                    halves.append(jnp.where(low, first, swap(second)))
                else:
                    halves.append(jnp.where(low, swap(first), second))
            out.append(jnp.concatenate(halves, axis=1))
        return out

    def dot_m(x, stacked):
        hi, lo = split(x)
        w_hi, w_lo = stacked[:, 0:C], stacked[:, 2 * C :]
        return mm(hi, w_hi, 1, 0) + (mm(lo, w_hi, 1, 0) + mm(hi, w_lo, 1, 0))

    turned = turn(by_kind)
    a1 = dot_m(turned[0], r.wm0)
    b1 = dot_m(jnp.concatenate(turned[1:], axis=0), r.wm1)
    b1 = [b1[k * nodes : (k + 1) * nodes] for k in range(3)]
    one_a = 1.0 + a1
    vec_one = [b * one_a for b in b1]
    for k in range(3):
        r.out_v[:, C * k : C * (k + 1)] = vec_one[k][atoms:]
    send_all(1)
    q1 = dot_k(a1 * a1 + (b1[0] * b1[0] + b1[1] * b1[1] + b1[2] * b1[2]), r.mq1_f, 1)
    scalar_one = r.initial[...] + a1 + q1
    r.out_s[...] = scalar_one[atoms:]
    send_all(2)
    r.node_a[...] = a1
    for k in range(3):
        r.node_b[:, C * k : C * (k + 1)] = b1[k]
    own_feats = [scalar_one[0:atoms]] + [v[0:atoms] for v in vec_one]
    r.scalar[...] = own_feats[0]

    arrive(3)
    tab2 = r.tab2
    for k in range(4):
        hi, lo = split(own_feats[k])
        tab2[0:atoms, C * k : C * (k + 1)] = hi
        tab2[atoms : 2 * atoms, C * k : C * (k + 1)] = lo

    rhp = r.rhp
    rhp[0 : held.rh.shape[0], :] = held.rh[...]
    r.rop[:, 0 : held.ro.shape[1]] = held.ro[...]
    rh_ms = dot3(rhp[...], held.ms2[...], 1, 0)
    rh_mq = dot3(rhp[...], held.mq2[...], 1, 0)
    r.msz_f[...] = stack3(jnp.concatenate([held.ms2[...], rh_ms], axis=0), 1)
    r.mv2_f[...] = stack3(held.mv2[...], 1)
    r.rhq_f[...] = stack3(rh_mq, 1)
    r.rhq_b[...] = stack3(jnp.concatenate([rhp[...], rh_mq], axis=1), 0)
    r.ms2_b[...] = stack3(held.ms2[...], 0)
    r.mv2_b[...] = stack3(held.mv2[...], 0)
    r.mq1_b[...] = stack3(held.mq1[...], 0)
    r.z0[...] = dot3(own_feats[0], rhp[...], 1, 1)

    ru_ref, x_ref, agg_ref, hot_g = r.ru, r.x, r.agg, r.hot_g

    def messages(rows, x):
        s, v = x[0], x[1:]
        ru = [ru_ref[rows, C * k : C * (k + 1)] for k in range(6)]
        r0, r3 = rad_ref[rows, 0:C], rad_ref[rows, 3 * C : 4 * C]
        first = r0 * s + ru[0] * v[0] + (ru[1] * v[1] + ru[2] * v[2])
        return [first] + [ru[3 + k] * s + r3 * v[k] for k in range(3)]

    def slot_sums(msgs):
        sub = lax.broadcasted_iota(jnp.int32, (8, C), 0)
        outs = []
        for m in msgs:
            parts = [sum(m[a * slots + 8 * i : a * slots + 8 * i + 8] for i in range(slots // 8)) for a in range(8)]
            low = sub < 4
            parts = [
                jnp.where(low, x, y) + pltpu.roll(jnp.where(low, y, x), 4, 0)
                for x, y in zip(parts[:4], parts[4:])
            ]
            for width in (2, 1):
                first = (sub & width) == 0
                parts = [
                    jnp.where(first, x + pltpu.roll(x, 8 - width, 0), y + pltpu.roll(y, width, 0))
                    for x, y in zip(parts[:width], parts[width:])
                ]
            outs.append(parts[0])
        return outs

    for c in range(n_chunks):
        rows = rows_of(c)
        u = [u_ref[rows, LANES * k : LANES * (k + 1)] for k in range(3)]
        for k in range(3):
            ru_ref[rows, C * k : C * (k + 1)] = rad_ref[rows, C : 2 * C] * u[k]
            ru_ref[rows, C * (k + 3) : C * (k + 4)] = rad_ref[rows, 2 * C : 3 * C] * u[k]
        ent = ent_ref[rows, :]
        lane = lax.broadcasted_iota(jnp.int32, ent.shape, 1).astype(f32)
        hot = (ent == lane + float(atoms)).astype(f32).astype(bf16)
        hot_g[rows, 0:LANES] = hot
        hot_g[rows, LANES:] = hot
        near_ent = jnp.where(ent < float(atoms), ent, -1000.0)
        hot = jnp.logical_and(
            near_ent >= 0.0, jnp.logical_or(near_ent == lane, near_ent + float(atoms) == lane)
        )
        x = mm(hot.astype(f32).astype(bf16), tab2[...], 1, 0)
        x_ref[rows, :] = x
        sums = slot_sums(messages(rows, [x[:, C * k : C * (k + 1)] for k in range(4)]))
        for k in range(4):
            agg_ref[8 * c : 8 * c + 8, C * k : C * (k + 1)] = sums[k]

    kind = r.kind[...]
    atom_i = lax.broadcasted_iota(jnp.int32, (atoms, edges), 0).astype(f32)
    at_atom = jnp.sum(r.live[0:atoms, :] * atom_i, axis=0, keepdims=True)
    any_live = jnp.sum(r.live[0:atoms, :], axis=0, keepdims=True)
    key_own = jnp.where(any_live > 0.0, kind * float(atoms) + at_atom, -1.0)
    list_i = lax.broadcasted_iota(jnp.int32, (G, edges), 0).astype(f32)
    at_list = jnp.sum(r.live[atoms:, :] * list_i, axis=0, keepdims=True)
    any_list = jnp.sum(r.live[atoms:, :], axis=0, keepdims=True)
    key_list = jnp.where(any_list > 0.0, kind * float(G) + at_list, -128.0)
    keys = jnp.concatenate([key_own, key_list, jnp.zeros((14, edges), f32)], axis=0).astype(bf16)
    key_shape = (16, 2 * LANES)
    key_rhs = lax.broadcasted_iota(jnp.int32, key_shape, 0) == (lax.broadcasted_iota(jnp.int32, key_shape, 1) >> 7)
    key_rhs = key_rhs.astype(f32).astype(bf16)
    key_own_hot, key_list_ref, jac, radp = r.key_own, r.key_list, r.jac, r.radp
    for c in range(n_chunks):
        rows = rows_of(c)
        out = mm(keys[:, rows], key_rhs, 0, 0)
        lane = lax.broadcasted_iota(jnp.int32, (chunk, LANES), 1).astype(f32)
        hot = (out[:, 0:LANES] == lane).astype(f32).astype(bf16)
        key_own_hot[rows, 0:LANES] = hot
        key_own_hot[rows, LANES:] = hot
        key_list_ref[rows, :] = out[:, LANES:]
        h, th, inv_c = hid_ref[rows, :], th_ref[rows, :], inv_ref[rows, :]
        u = [u_ref[rows, LANES * k : LANES * (k + 1)] for k in range(3)]
        low = lanes_low(h.shape)
        hp = jnp.where(low, th, swap(th))
        ww = jnp.where(low, h, swap(h)) * inv_c
        zz = hp - ww
        q0 = jnp.where(low, hp, zz * u[0])
        q1_ = zz * jnp.where(low, u[1], u[2])
        w_up, w_low = jnp.where(low, 0.0, ww), jnp.where(low, ww, 0.0)
        both = [
            (u[0] * q0 + w_up, u[0] * q1_),
            (u[1] * q0, u[1] * q1_ + w_low),
            (u[2] * q0, u[2] * q1_ + w_up),
        ]
        for k in range(3):
            jac[rows, 2 * LANES * k : 2 * LANES * k + LANES] = both[k][0]
            jac[rows, 2 * LANES * k + LANES : 2 * LANES * (k + 1)] = both[k][1]
        rp = spread_w2(th)
        for k in range(4):
            col = rp[:, C * k : C * (k + 1)]
            if k in (1, 2):
                col = col - inv_c * rad_ref[rows, C * k : C * (k + 1)]
            radp[rows, C * k : C * (k + 1)] = col

    starts = [list_s[0, g] * slots for g in range(G)]
    src_t = r.src_t
    list_edges = G * slots
    for g in range(G):
        rows = slice(g * slots, (g + 1) * slots)
        key = key_list_ref[pl.ds(starts[g], slots), :]
        lane = lax.broadcasted_iota(jnp.int32, key.shape, 1).astype(f32)
        rank = kinds_n * G
        hot = jnp.logical_or(key == lane, key + float(rank) == lane)
        r.key_hot[rows, :] = jnp.where(key >= 0.0, hot.astype(f32), 0.0).astype(bf16)
        src_t[rows, :] = ent_ref[pl.ds(starts[g], slots), :]
    lane = lax.broadcasted_iota(jnp.int32, (list_edges, LANES), 1).astype(f32)
    r.src_gl[...] = jnp.transpose((src_t[...] == lane + float(atoms)).astype(f32)).astype(bf16)
    near = jnp.transpose((src_t[...] == lane).astype(f32))[0:atoms, :]
    spot = lax.broadcasted_iota(jnp.int32, (G, list_edges), 1) - lax.broadcasted_iota(
        jnp.int32, (G, list_edges), 0
    ) * slots
    blocks = ((spot >= 0) & (spot < slots)).astype(f32).astype(bf16)
    r.own_l[...] = (mm(listed, blocks, 0, 0) - near).astype(bf16)
    r.own_all[...] = (r.live[0:atoms, :] - src_hot[0:atoms, :].astype(f32)).astype(bf16)

    wait_in(1)
    wait_in(2)
    tab_g = r.tab_g
    entries_g = 8 * G
    hi, lo = split(r.ghost_v[...])
    tab_g[0:entries_g, C:] = hi
    tab_g[entries_g:, C:] = lo
    hi, lo = split(r.ghost_s[...])
    tab_g[0:entries_g, 0:C] = hi
    tab_g[entries_g:, 0:C] = lo
    xg_ref = r.xg
    for c in range(n_chunks):
        rows = rows_of(c)
        x = mm(hot_g[rows, :], tab_g[...], 1, 0)
        xg_ref[rows, :] = x
        sums = slot_sums(messages(rows, [x[:, C * k : C * (k + 1)] for k in range(4)]))
        for k in range(4):
            at = (slice(8 * c, 8 * c + 8), slice(C * k, C * (k + 1)))
            agg_ref[at] = (agg_ref[at] + sums[k]) * scale
    az = dot_k(agg_ref[:, 0:C], r.msz_f, 1)
    a2 = az[:, 0:C]
    b2 = dot_k(jnp.concatenate([agg_ref[:, C * k : C * (k + 1)] for k in (1, 2, 3)], axis=0), r.mv2_f, 1)
    b2 = [b2[k * atoms : (k + 1) * atoms] for k in range(3)]
    squares = a2 * a2 + (b2[0] * b2[0] + b2[1] * b2[1] + b2[2] * b2[2])
    z = r.z0[...] + az[:, C:] + dot_k(squares, r.rhq_f, 1)
    sz = jax.nn.sigmoid(z)
    dz = r.rop[...] * (sz * (1.0 + z * (1.0 - sz)))
    down = dot_k(dz, r.rhq_b, 0)
    ds_two, dq2 = down[:, 0:C], down[:, C:]
    dagg = r.dagg
    dagg[:, 0:C] = dot_k(ds_two + 2.0 * a2 * dq2, r.ms2_b, 0) * scale
    db = dot_k(jnp.concatenate([2.0 * b * dq2 for b in b2], axis=0), r.mv2_b, 0) * scale
    for k in range(3):
        dagg[:, C * (k + 1) : C * (k + 2)] = db[k * atoms : (k + 1) * atoms]

    def spread_rows(c):
        out = []
        for k in range(4):
            small = [dagg[a : a + 1, C * k : C * (k + 1)] for a in range(c * 8, (c + 1) * 8)]
            out.append(jnp.concatenate([jnp.broadcast_to(x, (slots, C)) for x in small], axis=0))
        return out

    def scatter(first, which):
        hi_ref, lo_ref = r.dx_hi, r.dx_lo
        for a in range(atoms):
            rows = slice(a * slots, (a + 1) * slots)
            d = [dagg[a : a + 1, C * k : C * (k + 1)] for k in range(4)]
            for n, k in enumerate(which):
                if k == 0:
                    ru = [ru_ref[rows, C * (3 + m) : C * (4 + m)] for m in range(3)]
                    g = rad_ref[rows, 0:C] * d[0] + ru[0] * d[1] + (ru[1] * d[2] + ru[2] * d[3])
                else:
                    g = ru_ref[rows, C * (k - 1) : C * k] * d[0] + rad_ref[rows, 3 * C : 4 * C] * d[k]
                at = slice(C * (first + n), C * (first + n + 1))
                hi_ref[rows, at], lo_ref[rows, at] = split(g)

    def gather_grads(hot, first):
        at = slice(C * first, C * (first + 2))
        return mm(hot, r.dx_hi[:, at], 1, 0) + mm(hot, r.dx_lo[:, at], 1, 0)

    ghost_hot = slice(atoms, None)
    scatter(0, (1, 2))
    r.grad_a[...] = gather_grads(src_hot[ghost_hot, :], 0)
    send_all(3)
    scatter(2, (3, 0))
    r.grad_b[...] = gather_grads(src_hot[ghost_hot, :], 2)
    send_all(4)

    lin8 = jnp.broadcast_to(held.lin[...], (8, C))
    ro8 = jnp.broadcast_to(r.rop[...], (8, LANES))
    energy = dot3(lin8, r.scalar[...], 1, 1) + dot3(ro8, z * sz, 1, 1)
    r.eout[...] = energy[0:1, :]

    def node_grads(ds, dv, rows):
        a = r.node_a[rows, :]
        b = [r.node_b[rows, C * k : C * (k + 1)] for k in range(3)]
        dq = dot_k(ds, r.mq1_b, 0)
        da = ds + 2.0 * a * dq + (dv[0] * b[0] + dv[1] * b[1] + dv[2] * b[2])
        db = jnp.concatenate([dv[k] * (1.0 + a) + 2.0 * b[k] * dq for k in range(3)], axis=0)
        n = ds.shape[0]
        back = dot_k(db, r.wm1, 1)
        back = [dot_k(da, r.wm0, 1)] + [back[k * n : (k + 1) * n] for k in range(3)]
        hi, lo = split(jnp.concatenate(turn(back), axis=0))
        return jnp.concatenate([hi, lo], axis=0)

    def lane_put(sums):
        lane = lax.broadcasted_iota(jnp.int32, sums[0].shape, 1)
        out = jnp.zeros(sums[0].shape, f32)
        for k in range(3):
            out = jnp.where(lane == k, jnp.sum(sums[k], axis=1, keepdims=True), out)
        return out

    own_a = gather_grads(src_hot[0:atoms, :], 0)
    own_b = gather_grads(src_hot[0:atoms, :], 2)
    ds_own = own_b[:, C:] + ds_two + held.lin[...]
    r.gp[...] = node_grads(ds_own, [own_a[:, 0:C], own_a[:, C:], own_b[:, 0:C]], slice(0, atoms))
    f_own = r.f_own
    for c in range(n_chunks):
        rows = rows_of(c)
        d = spread_rows(c)
        x = [x_ref[rows, C * k : C * (k + 1)] + xg_ref[rows, C * k : C * (k + 1)] for k in range(4)]
        s, v = x[0], x[1:]
        u = [u_ref[rows, LANES * k : LANES * (k + 1)] for k in range(3)]
        rp = [radp[rows, C * k : C * (k + 1)] for k in range(4)]
        uv = u[0] * v[0] + u[1] * v[1] + u[2] * v[2]
        ud = u[0] * d[1] + u[1] * d[2] + u[2] * d[3]
        dv = d[1] * v[0] + d[2] * v[1] + d[3] * v[2]
        along = rp[0] * (d[0] * s) + rp[1] * (d[0] * uv) + (rp[2] * (s * ud) + rp[3] * dv)
        r1d = (rad_ref[rows, C : 2 * C] * d[0]) * inv_ref[rows, :]
        r2s = (rad_ref[rows, 2 * C : 3 * C] * s) * inv_ref[rows, :]
        g = mm(key_own_hot[rows, :], r.gp[...], 1, 0)
        g0, g1 = g[:, 0:LANES], g[:, LANES:]
        sums = []
        for k in range(3):
            j0 = jac[rows, 2 * LANES * k : 2 * LANES * k + LANES]
            j1 = jac[rows, 2 * LANES * k + LANES : 2 * LANES * (k + 1)]
            sums.append((u[k] * along + r1d * v[k]) + (r2s * d[k + 1] + (g0 * j0 + g1 * j1)))
        f_own[rows, :] = lane_put(sums)
    hi, mid, lo = split3(f_own[...])
    hot = src_hot[ghost_hot, :]
    r.force_o[...] = mm(hot, hi, 1, 0) + (mm(hot, mid, 1, 0) + mm(hot, lo, 1, 0))
    own = r.own_all[...]
    r.force_n[...] = mm(own, hi, 1, 0) + (mm(own, mid, 1, 0) + mm(own, lo, 1, 0))

    wait_in(3)
    wait_in(4)

    def total(ref):
        out = [ref[k] for k in range(8)]
        while len(out) > 1:
            out = [out[i] + out[i + 1] for i in range(0, len(out), 2)]
        return out[0]

    g_a, g_b = total(r.in_a), total(r.in_b)
    gp_l = node_grads(g_b[:, C:], [g_a[:, 0:C], g_a[:, C:], g_b[:, 0:C]], slice(atoms, nodes))
    f_list = []
    for g in range(G):
        rows = slice(g * slots, (g + 1) * slots)
        at = pl.ds(starts[g], slots)
        if g % 4 == 0:
            wide = mm(r.key_hot[g * slots : (g + 4) * slots, :], gp_l, 1, 0)
        m = g % 4
        here = wide[m * slots : (m + 1) * slots]
        g0, g1 = here[:, 0:LANES], here[:, LANES:]
        sums = []
        for k in range(3):
            j0 = jac[at, 2 * LANES * k : 2 * LANES * k + LANES]
            j1 = jac[at, 2 * LANES * k + LANES : 2 * LANES * (k + 1)]
            sums.append(g0 * j0 + g1 * j1)
        f_list.append(lane_put(sums))
    f_list = jnp.concatenate(f_list, axis=0)
    l_hi, l_lo = split(f_list)
    hot = r.src_gl[...]
    r.force_g[...] = r.force_o[...] + (mm(hot, l_hi, 1, 0) + mm(hot, l_lo, 1, 0))
    send_all(5)
    own_l = r.own_l[...]
    force = r.force_n[...] + (mm(own_l, l_hi, 1, 0) + mm(own_l, l_lo, 1, 0))
    force = jnp.transpose(force)
    for phase in range(5):
        wait_out(phase)
    wait_in(5)
    late = total(r.in_f)
    for k in range(3):
        back = jnp.sum(late[:, k : k + 1] * listed_f, axis=0, keepdims=True)
        r.fout[k : k + 1, :] = force[k : k + 1, :] - back
    wait_out(5)


def store_kernel(e_ref, f_ref, eo_ref, fo_ref, sem):
    one = pltpu.make_async_copy(e_ref, eo_ref, sem.at[0])
    two = pltpu.make_async_copy(f_ref, fo_ref, sem.at[1])
    one.start()
    two.start()
    one.wait()
    two.wait()


def in_order(vec, senders, counts, species, list, embed, win1, wmid1, wout1, ms1, mv1, mq1, win2, wmid2, wout2, ms2, mv2, mq2, lin, rh, ro):
    return dict(locals())


def on_device(n_dom, n_sub, *args):
    (vec, senders, counts, species, send_list, embed) = args[:6]
    weights = list(args[6:18])
    read_lin, read_hidden, read_out = args[18:]
    edges = vec.shape[1]
    atoms = species.shape[0]
    G = send_list.shape[0]
    C, kinds_n = embed.shape
    hidden, n_basis = weights[0].shape
    for i in (0, 2, 6, 8):
        weights[i] = weights[i].T
    row = lambda x: x.reshape(1, -1)
    operands = [vec, row(senders), row(counts), row(species), row(send_list), embed.T, *weights]
    operands += [row(read_lin), read_hidden, row(read_out)]
    far, nodes, list_edges = 8 * G, atoms + G, G * (edges // atoms)
    i32 = jnp.int32
    packed = -(-(6 * n_basis + 24) // 16) * 16
    inputs = in_order(*operands)
    scratch = dict(
        kind_out=((G, LANES), f32),
        ghost_kind=((far, LANES), f32),
        out_v=((G, 3 * C), f32),
        out_s=((G, C), f32),
        ghost_v=((far, 3 * C), f32),
        ghost_s=((far, C), f32),
        grad_a=((far, 2 * C), f32),
        grad_b=((far, 2 * C), f32),
        in_a=((8, G, 2 * C), f32),
        in_b=((8, G, 2 * C), f32),
        force_g=((far, LANES), f32),
        force_o=((far, LANES), f32),
        force_n=((atoms, LANES), f32),
        in_f=((8, G, LANES), f32),
        rhs=((packed, 7 * LANES), f32),
        wide_rhs=((packed, 7 * LANES), bf16),
        pack=((packed, edges), bf16),
        v8=((8, edges), f32),
        winp=((n_basis, LANES), f32),
        wmid=((LANES, LANES), f32),
        wmid_f=((LANES, 3 * LANES), bf16),
        w2_k=((2 * LANES, 4 * C), bf16),
        rhp=((LANES, C), f32),
        rop=((1, LANES), f32),
        kind_own=((1, edges), f32),
        src_f=((far, edges), f32),
        kind=((1, edges), f32),
        live=((nodes, edges), f32),
        src_hot=((atoms + far, edges), bf16),
        hid=((edges, LANES), f32),
        th=((edges, LANES), f32),
        u=((edges, 3 * LANES), f32),
        inv=((edges, LANES), f32),
        ent=((edges, LANES), f32),
        p_hi=((edges, 2 * LANES), bf16),
        p_lo=((edges, 2 * LANES), bf16),
        rad=((edges, 4 * C), f32),
        radp=((edges, 4 * C), f32),
        ru=((edges, 6 * C), f32),
        jac=((edges, 6 * LANES), f32),
        wm0=((kinds_n * hidden, 3 * C), bf16),
        wm1=((kinds_n * hidden, 3 * C), bf16),
        mq1_f=((C, 3 * C), bf16),
        mq1_b=((3 * C, C), bf16),
        msz_f=((C + LANES, 3 * C), bf16),
        mv2_f=((C, 3 * C), bf16),
        rhq_f=((LANES, 3 * C), bf16),
        rhq_b=((3 * LANES, 2 * C), bf16),
        ms2_b=((3 * C, C), bf16),
        mv2_b=((3 * C, C), bf16),
        initial=((nodes, C), f32),
        node_a=((nodes, C), f32),
        node_b=((nodes, 3 * C), f32),
        scalar=((atoms, C), f32),
        z0=((atoms, LANES), f32),
        tab2=((LANES, 4 * C), bf16),
        tab_g=((2 * far, 4 * C), bf16),
        hot_g=((edges, 2 * LANES), bf16),
        x=((edges, 4 * C), f32),
        xg=((edges, 4 * C), f32),
        agg=((atoms, 4 * C), f32),
        dagg=((atoms, 4 * C), f32),
        key_own=((edges, 2 * LANES), bf16),
        key_list=((edges, LANES), f32),
        key_hot=((list_edges, LANES), bf16),
        src_t=((list_edges, LANES), f32),
        src_gl=((far, list_edges), bf16),
        own_l=((atoms, list_edges), bf16),
        own_all=((atoms, edges), bf16),
        dx_hi=((edges, 4 * C), bf16),
        dx_lo=((edges, 4 * C), bf16),
        gp=((2 * kinds_n * atoms, 2 * LANES), bf16),
        f_own=((edges, LANES), f32),
    )
    names = list(inputs) + ["eout", "fout"] + [k + "_" for k in inputs] + list(scratch)
    copies = [pltpu.VMEM(x.shape, x.dtype) for x in operands]
    hbm = pl.BlockSpec(memory_space=pltpu.HBM)
    whole = pl.BlockSpec(memory_space=pltpu.VMEM)
    out = pl.pallas_call(
        functools.partial(kernel, n_dom, n_sub, names),
        out_shape=[pltpu.VMEM((1, atoms), f32), pltpu.VMEM((3, atoms), f32)],
        in_specs=[hbm] * len(operands),
        out_specs=[whole, whole],
        scratch_shapes=copies
        + [pltpu.VMEM(shape, dtype) for shape, dtype in scratch.values()]
        + [pltpu.SMEM((1, G), i32)]
        + [pltpu.SemaphoreType.DMA((6, 9)), pltpu.SemaphoreType.DMA((6, 9))]
        + [pltpu.SemaphoreType.DMA((len(operands) + 1,))],
        compiler_params=pltpu.CompilerParams(
            collective_id=0, has_side_effects=True, vmem_limit_bytes=56 * 1024 * 1024
        ),
    )(*operands)
    out = pl.pallas_call(
        store_kernel,
        out_shape=[jax.ShapeDtypeStruct((1, atoms), f32), jax.ShapeDtypeStruct((3, atoms), f32)],
        in_specs=[whole, whole],
        out_specs=[hbm, hbm],
        scratch_shapes=[pltpu.SemaphoreType.DMA((2,))],
    )(*[pltpu.with_memory_space_constraint(o, pltpu.VMEM) for o in out])
    return out[0].reshape(atoms), out[1]


def solution(mesh):
    one = P(("dom", "sub"))
    return jax.shard_map(
        functools.partial(on_device, mesh.shape["dom"], mesh.shape["sub"]),
        mesh=mesh,
        in_specs=(P(None, ("dom", "sub")), one, one, one, one) + (P(),) * 16,
        out_specs=(one, P(None, ("dom", "sub"))),
        check_vma=False,
    )
```

```python
import functools
import math
import types

import jax
import jax.numpy as jnp
from jax import lax
from jax.experimental import pallas as pl
from jax.experimental.pallas import tpu as pltpu
from jax.sharding import PartitionSpec as P

cutoff_radius = 5.0
f32 = jnp.float32
bf16 = jnp.bfloat16
LANES = 128
MESH = pl.DeviceIdType.MESH


def mm(a, b, ca, cb):
    return lax.dot_general(a, b, (((ca,), (cb,)), ((), ())), preferred_element_type=f32)


def split(x):
    hi = x.astype(bf16)
    return hi, (x - hi.astype(f32)).astype(bf16)


def split3(x):
    hi = x.astype(bf16)
    rest = x - hi.astype(f32)
    mid = rest.astype(bf16)
    return hi, mid, (rest - mid.astype(f32)).astype(bf16)


def dot3(a, b, ca, cb):
    a_hi, a_lo = split(a)
    b_hi, b_lo = split(b)
    return mm(a_hi, b_hi, ca, cb) + (mm(a_hi, b_lo, ca, cb) + mm(a_lo, b_hi, ca, cb))


def hot3(hot, x, ca, cb):
    hi, mid, lo = split3(x)
    return mm(hot, hi, ca, cb) + (mm(hot, mid, ca, cb) + mm(hot, lo, ca, cb))


def to_column(row):
    count = row.shape[1]
    shape = (count, count)
    same = lax.broadcasted_iota(jnp.int32, shape, 0) == lax.broadcasted_iota(jnp.int32, shape, 1)
    return jnp.sum(jnp.where(same, row, 0.0), axis=1, keepdims=True)


def series(t, first, terms):
    total = jnp.ones_like(t)
    for i in reversed(range(terms)):
        low = first + 2 * i
        total = 1.0 - t * (1.0 / (low * (low + 1))) * total
    return total


def kernel(n_dom, n_sub, names, *refs):
    r = types.SimpleNamespace(**dict(zip(names, refs)))
    inputs = len(in_order(*range(21)))
    hbm = types.SimpleNamespace(**dict(zip(names[:inputs], refs[:inputs])))
    held = types.SimpleNamespace(**dict(zip(names[:inputs], refs[inputs + 2 : 2 * inputs + 2])))
    list_s, send_sem, recv_sem, in_sem = refs[-4:]
    dm, sb = lax.axis_index("dom"), lax.axis_index("sub")
    atoms = hbm.species.shape[1]
    edges = hbm.vec.shape[1]
    slots = edges // atoms
    G = hbm.list.shape[1]
    kinds_n, C = hbm.embed.shape
    n_basis, hidden = hbm.win1.shape
    chunk = 8 * slots
    n_chunks = edges // chunk
    scale = slots ** (-0.5)
    sides = [s for s in range(9) if s != 4]
    nodes = atoms + G

    def exists(s):
        ok = None
        for here, count, off in ((dm, n_dom, s // 3 - 1), (sb, n_sub, s % 3 - 1)):
            if off == 0:
                continue
            one = here > 0 if off < 0 else here < count - 1
            ok = one if ok is None else jnp.logical_and(ok, one)
        return ok

    def place(s):
        return (dm + (s // 3 - 1), sb + (s % 3 - 1))

    def row_of(s):
        return s if s < 4 else s - 1

    def block(s):
        return pl.ds(G * row_of(s), G)

    def copies(phase, s, there):
        o = 8 - s
        src, dst = (
            lambda: (r.kind_out, r.ghost_kind.at[block(o)]),
            lambda: (r.out_f, r.ghost_f.at[block(o)]),
            lambda: (r.out_f, r.ghost_f.at[block(o)]),
            lambda: (r.grad_a.at[block(s)], r.in_a.at[row_of(o)]),
            lambda: (r.grad_b.at[block(s)], r.in_b.at[row_of(o)]),
            lambda: (r.force_g.at[block(s)], r.in_f.at[row_of(o)]),
        )[phase]()
        return pltpu.make_async_remote_copy(
            src_ref=src,
            dst_ref=dst,
            send_sem=send_sem.at[phase, s],
            recv_sem=recv_sem.at[phase, o],
            device_id=place(there),
            device_id_type=MESH,
        )

    def send_all(phase):
        for s in sides:
            @pl.when(exists(s))
            def _():
                copies(phase, s, s).start()

    def wait_in(phase):
        for s in sides:
            @pl.when(exists(s))
            def _():
                copies(phase, 8 - s, s).wait_recv()

    def wait_out(phase):
        for s in sides:
            @pl.when(exists(s))
            def _():
                copies(phase, s, s).wait_send()

    groups = [
        [hbm.species, hbm.list],
        [hbm.vec, hbm.counts, hbm.senders, hbm.win1, hbm.win2, hbm.wmid1, hbm.wmid2],
        [hbm.wout1, hbm.embed, hbm.ms1, hbm.mv1, hbm.mq1, hbm.wout2],
    ]
    groups.append([x for x in refs[:inputs] if not any(x is y for group in groups for y in group)])
    inside = dict(zip(map(id, refs[:inputs]), refs[inputs + 2 : 2 * inputs + 2]))
    spots = {id(x): i for i, x in enumerate(refs[:inputs])}
    pulls = [[pltpu.make_async_copy(x, inside[id(x)], in_sem.at[spots[id(x)]]) for x in group] for group in groups]
    pulls[3].append(pltpu.make_async_copy(hbm.list, list_s, in_sem.at[inputs]))

    def start(group):
        for pull in pulls[group]:
            pull.start()

    def arrive(group):
        for pull in pulls[group]:
            pull.wait()

    start(0)
    r.ghost_kind[...] = jnp.zeros_like(r.ghost_kind)
    barrier = pltpu.get_barrier_semaphore()
    for s in sides:
        @pl.when(exists(s))
        def _():
            pl.semaphore_signal(barrier, inc=1, device_id=place(s), device_id_type=MESH)
    for group in (1, 2, 3):
        start(group)
    peers = [
        1 + jnp.where(at > 0, 1, 0) + jnp.where(at < count - 1, 1, 0)
        for at, count in ((dm, n_dom), (sb, n_sub))
    ]

    for ref in (r.ghost_f, r.in_a, r.in_b, r.in_f):
        ref[...] = jnp.zeros_like(ref)
    for ref in (r.rhs, r.v8, r.winp, r.wmid, r.rhp, r.rop, r.tab2):
        ref[...] = jnp.zeros_like(ref)
    arrive(0)
    species_row = held.species[...].astype(f32)
    species_col = to_column(species_row)
    list_col = to_column(held.list[...].astype(f32))
    listed_f = (list_col == lax.broadcasted_iota(jnp.int32, (G, atoms), 1).astype(f32)).astype(f32)
    listed = listed_f.astype(bf16)
    list_kinds = jnp.sum(listed_f * species_row, axis=1, keepdims=True)
    r.kind_out[...] = jnp.broadcast_to(list_kinds, (G, LANES))
    pl.semaphore_wait(barrier, peers[0] * peers[1] - 1)
    send_all(0)
    arrive(1)

    def lanes_low(shape):
        return lax.broadcasted_iota(jnp.int32, shape, 1) < hidden

    def swap(x):
        return pltpu.roll(x, hidden, 1)

    def stack3(x, axis):
        hi, lo = split(x)
        return jnp.concatenate([hi, hi, lo], axis=axis)

    def dot_k(a, stacked, dim):
        k = a.shape[1]
        a_hi, a_lo = split(a)
        both = jnp.concatenate([a_hi, a_lo], axis=1)
        if dim == 1:
            first, last = stacked[:, : 2 * k], stacked[:, 2 * k :]
        else:
            first, last = stacked[: 2 * k, :], stacked[2 * k :, :]
        return mm(both, first, 1, dim) + mm(a_hi, last, 1, dim)

    def rows_of(c):
        return slice(c * chunk, (c + 1) * chunk)

    wmid, winp, rhs = r.wmid, r.winp, r.rhs
    wmid[0:hidden, 0:hidden] = held.wmid1[...]
    wmid[hidden:, hidden:] = held.wmid2[...]
    wmid_f = r.wmid_f
    wmid_f[...] = stack3(wmid[...], 1)
    winp[:, 0:hidden] = held.win1[...]
    winp[:, hidden:] = held.win2[...]
    row_i = lax.broadcasted_iota(jnp.int32, rhs.shape, 0) - 6 * n_basis
    lane_i = lax.broadcasted_iota(jnp.int32, rhs.shape, 1)
    which_block = lane_i >> 7
    part_row = row_i & 7
    hit = jnp.logical_and(which_block >= 2, part_row == which_block - 2)
    rhs[...] = jnp.where(hit & (row_i >= 0) & (row_i < 24), 1.0, 0.0)
    hi, lo = split(winp[...])
    for t in range(2):
        at = slice(LANES * t, LANES * (t + 1))
        base = 3 * n_basis * t
        rhs[base : base + n_basis, at] = hi.astype(f32)
        rhs[base + n_basis : base + 2 * n_basis, at] = hi.astype(f32)
        rhs[base + 2 * n_basis : base + 3 * n_basis, at] = lo.astype(f32)
    r.wide_rhs[...] = rhs[...].astype(bf16)

    v8 = r.v8
    v8[0:3, :] = held.vec[...]
    vectors = v8[...]
    dist = jnp.sqrt(jnp.sum(vectors * vectors, axis=0, keepdims=True))
    inv = 1.0 / dist
    unit = vectors * inv
    x1 = dist * (1.0 / cutoff_radius)
    x2 = x1 * x1
    x5 = x2 * x2 * x1
    x6 = x5 * x1
    env = 1.0 + x6 * (-28.0 + x1 * (48.0 - 21.0 * x1))
    denv = x5 * (-168.0 + x1 * (336.0 - 168.0 * x1)) * (1.0 / cutoff_radius)
    order_n = (lax.broadcasted_iota(jnp.int32, (n_basis, edges), 0) + 1).astype(f32)
    turns = order_n * x1
    near = jnp.floor(turns + 0.5)
    odd = near - 2.0 * jnp.floor(near * 0.5)
    sign = 1.0 - 2.0 * odd
    angle = (turns - near) * math.pi
    t2 = angle * angle
    sine = sign * angle * series(t2, 2, 7)
    cosine = sign * series(t2, 1, 7)
    norm = math.sqrt(2.0 / cutoff_radius)
    wave = (norm * inv) * sine
    basis = wave * env
    dbasis = ((norm * math.pi / cutoff_radius) * order_n * cosine * inv - wave * inv) * env + wave * denv

    counts_row = held.counts[...].astype(f32)
    counts_col = to_column(counts_row).astype(jnp.int32)
    list_counts = jnp.sum(listed_f * counts_row, axis=1, keepdims=True).astype(jnp.int32)
    list_at = list_col.astype(jnp.int32) * slots

    def live_of(rows, start, count):
        spot = lax.broadcasted_iota(jnp.int32, (rows, edges), 1) - start
        return ((spot >= 0) & (spot < count)).astype(f32)

    live = live_of(atoms, lax.broadcasted_iota(jnp.int32, (atoms, edges), 0) * slots, counts_col)
    r.live[0:atoms, :] = live
    r.live[atoms:, :] = live_of(G, list_at, list_counts)
    live_row = jnp.sum(live, axis=0, keepdims=True)
    sent = held.senders[...]
    entry = jnp.where(sent >= atoms + 5 * G, sent - G, sent)
    src_hot = r.src_hot
    source = jnp.where(lax.broadcasted_iota(jnp.int32, src_hot.shape, 0) == entry, live_row, 0.0)
    src_hot[...] = source.astype(bf16)
    r.src_f[...] = source[atoms:, :]
    r.kind_own[...] = jnp.sum(source[0:atoms, :] * species_col, axis=0, keepdims=True)
    live_entry = jnp.where(live_row > 0.0, entry.astype(f32), -1.0)

    eight = lax.broadcasted_iota(jnp.int32, (8, edges), 0)
    unit = jnp.where(eight == 3, inv, jnp.where(eight == 4, live_entry, unit))
    b_hi, b_lo = split(basis)
    d_hi, d_lo = split(dbasis)
    parts = [b_hi, b_lo, b_hi, d_hi, d_lo, d_hi] + list(split3(unit))
    parts = [p.astype(f32) for p in parts] + [jnp.zeros((8, edges), f32)]
    r.pack[...] = jnp.concatenate(parts, axis=0).astype(bf16)

    hid_ref, th_ref, u_ref, inv_ref, ent_ref = r.hid, r.th, r.u, r.inv, r.ent
    p_hi, p_lo, rad_ref = r.p_hi, r.p_lo, r.rad

    def spread_w2(h):
        h_hi, h_lo = split(h)
        twice = jnp.where(lanes_low(h.shape), swap(h), h).astype(bf16)
        return mm(jnp.concatenate([twice, h_lo], axis=1), r.w2_k[...], 1, 0)

    for c in range(n_chunks):
        rows = rows_of(c)
        out = mm(r.pack[:, rows], r.wide_rhs[...], 0, 0)
        p1, t1 = out[:, 0:LANES], out[:, LANES : 2 * LANES]
        u = [out[:, LANES * k : LANES * (k + 1)] for k in (2, 3, 4)]
        u_ref[rows, :] = out[:, 2 * LANES : 5 * LANES]
        inv_ref[rows, :] = out[:, 5 * LANES : 6 * LANES]
        ent_ref[rows, :] = out[:, 6 * LANES : 7 * LANES]
        s1 = jax.nn.sigmoid(p1)
        h1 = p1 * s1
        th1 = (s1 * (1.0 + p1 * (1.0 - s1))) * t1
        p2 = dot_k(h1, wmid_f, 1)
        t2_ = dot_k(th1, wmid_f, 1)
        s2 = jax.nn.sigmoid(p2)
        h = p2 * s2
        hid_ref[rows, :] = h
        th_ref[rows, :] = (s2 * (1.0 + p2 * (1.0 - s2))) * t2_
        low = lanes_low(h.shape)
        hh = jnp.where(low, h, swap(h))
        prod = jnp.concatenate([hh * jnp.where(low, 1.0, u[0]), hh * jnp.where(low, u[1], u[2])], axis=1)
        hi, lo = split(prod)
        p_hi[rows, :] = hi
        p_lo[rows, :] = lo

    arrive(2)
    hi, lo = split(held.wout2[...])
    r.w2_k[...] = jnp.concatenate([lo, hi, jnp.zeros_like(hi), hi], axis=0)
    w1 = held.wout1[...]
    for ref, at, mix in ((r.wm0, 0, held.ms1), (r.wm1, 1, held.mv1)):
        path = w1[:, C * at : C * (at + 1)]
        with_kind = jnp.concatenate([path * held.embed[k : k + 1, :] for k in range(kinds_n)], axis=0)
        ref[...] = stack3(dot3(with_kind, mix[...], 1, 1) * scale, 1)
    r.mq1_f[...] = stack3(held.mq1[...], 1)
    initial = jnp.zeros((nodes, C), f32)
    node_kinds = jnp.concatenate([species_col, list_kinds], axis=0)
    for k in range(kinds_n):
        initial = jnp.where(node_kinds == k, held.embed[k : k + 1, :], initial)
    r.initial[...] = initial

    for c in range(n_chunks):
        rad_ref[rows_of(c), :] = spread_w2(hid_ref[rows_of(c), :])

    wait_in(0)
    total = jnp.zeros((8, edges), f32)
    for s in sides:
        for m in range(G // 8):
            at = slice(row_of(s) * G + 8 * m, row_of(s) * G + 8 * m + 8)
            total = total + r.ghost_kind[at, 0:1] * r.src_f[at, :]
    r.kind[...] = r.kind_own[...] + jnp.sum(total, axis=0, keepdims=True)

    listed_sum = None
    own_sums = []
    for c in range(n_chunks):
        rows = rows_of(c)
        kind = r.kind[:, rows]
        own = jnp.where(r.live[8 * c : 8 * c + 8, rows] > 0.0, kind, -1.0)
        far = jnp.where(r.live[atoms:, rows] > 0.0, kind, -1.0)
        hot = [(own == k).astype(f32) for k in range(kinds_n)] + [(far == k).astype(f32) for k in range(kinds_n)]
        hot = jnp.concatenate(hot, axis=0).astype(bf16)
        total = mm(hot, p_hi[rows, :], 1, 0) + mm(hot, p_lo[rows, :], 1, 0)
        own_sums.append(total[0 : 8 * kinds_n])
        tail = total[8 * kinds_n :]
        listed_sum = tail if listed_sum is None else listed_sum + tail
    by_kind = []
    for k in range(kinds_n):
        rows_k = [x[8 * k : 8 * (k + 1)] for x in own_sums] + [listed_sum[G * k : G * (k + 1)]]
        by_kind.append(jnp.concatenate(rows_k, axis=0))

    def turn(parts):
        out = []
        low = lanes_low((parts[0].shape[0], LANES))
        for j in range(4):
            at = slice(LANES * (j // 2), LANES * (j // 2 + 1))
            halves = []
            for m in (0, 2):
                first, second = parts[m][:, at], parts[m + 1][:, at]
                if j % 2 == 0:
                    halves.append(jnp.where(low, first, swap(second)))
                else:
                    halves.append(jnp.where(low, swap(first), second))
            out.append(jnp.concatenate(halves, axis=1))
        return out

    def dot_m(x, stacked):
        hi, lo = split(x)
        w_hi, w_lo = stacked[:, 0:C], stacked[:, 2 * C :]
        return mm(hi, w_hi, 1, 0) + (mm(lo, w_hi, 1, 0) + mm(hi, w_lo, 1, 0))

    turned = turn(by_kind)
    a1 = dot_m(turned[0], r.wm0)
    b1 = dot_m(jnp.concatenate(turned[1:], axis=0), r.wm1)
    b1 = [b1[k * nodes : (k + 1) * nodes] for k in range(3)]
    one_a = 1.0 + a1
    vec_one = [b * one_a for b in b1]
    for k in range(3):
        r.out_f[:, C * (k + 1) : C * (k + 2)] = vec_one[k][atoms:]
    q1 = dot_k(a1 * a1 + (b1[0] * b1[0] + b1[1] * b1[1] + b1[2] * b1[2]), r.mq1_f, 1)
    scalar_one = r.initial[...] + a1 + q1
    r.out_f[:, 0:C] = scalar_one[atoms:]
    send_all(2)
    r.node_a[...] = a1
    for k in range(3):
        r.node_b[:, C * k : C * (k + 1)] = b1[k]
    own_feats = [scalar_one[0:atoms]] + [v[0:atoms] for v in vec_one]
    r.scalar[...] = own_feats[0]

    arrive(3)
    tab2 = r.tab2
    for k in range(4):
        hi, lo = split(own_feats[k])
        tab2[0:atoms, C * k : C * (k + 1)] = hi
        tab2[atoms : 2 * atoms, C * k : C * (k + 1)] = lo

    rhp = r.rhp
    rhp[0 : held.rh.shape[0], :] = held.rh[...]
    r.rop[:, 0 : held.ro.shape[1]] = held.ro[...]
    rh_ms = dot3(rhp[...], held.ms2[...], 1, 0)
    rh_mq = dot3(rhp[...], held.mq2[...], 1, 0)
    r.msz_f[...] = stack3(jnp.concatenate([held.ms2[...], rh_ms], axis=0), 1)
    r.mv2_f[...] = stack3(held.mv2[...], 1)
    r.rhq_f[...] = stack3(rh_mq, 1)
    r.rhq_b[...] = stack3(jnp.concatenate([rhp[...], rh_mq], axis=1), 0)
    r.ms2_b[...] = stack3(held.ms2[...], 0)
    r.mv2_b[...] = stack3(held.mv2[...], 0)
    r.mq1_b[...] = stack3(held.mq1[...], 0)
    r.z0[...] = dot3(own_feats[0], rhp[...], 1, 1)

    ru_ref, x_ref, agg_ref, hot_g = r.ru, r.x, r.agg, r.hot_g

    def messages(rows, x):
        s, v = x[0], x[1:]
        ru = [ru_ref[rows, C * k : C * (k + 1)] for k in range(6)]
        r0, r3 = rad_ref[rows, 0:C], rad_ref[rows, 3 * C : 4 * C]
        first = r0 * s + ru[0] * v[0] + (ru[1] * v[1] + ru[2] * v[2])
        return [first] + [ru[3 + k] * s + r3 * v[k] for k in range(3)]

    def slot_sums(msgs):
        sub = lax.broadcasted_iota(jnp.int32, (8, C), 0)
        outs = []
        for m in msgs:
            parts = [sum(m[a * slots + 8 * i : a * slots + 8 * i + 8] for i in range(slots // 8)) for a in range(8)]
            low = sub < 4
            parts = [
                jnp.where(low, x, y) + pltpu.roll(jnp.where(low, y, x), 4, 0)
                for x, y in zip(parts[:4], parts[4:])
            ]
            for width in (2, 1):
                first = (sub & width) == 0
                parts = [
                    jnp.where(first, x + pltpu.roll(x, 8 - width, 0), y + pltpu.roll(y, width, 0))
                    for x, y in zip(parts[:width], parts[width:])
                ]
            outs.append(parts[0])
        return outs

    for c in range(n_chunks):
        rows = rows_of(c)
        u = [u_ref[rows, LANES * k : LANES * (k + 1)] for k in range(3)]
        for k in range(3):
            ru_ref[rows, C * k : C * (k + 1)] = rad_ref[rows, C : 2 * C] * u[k]
            ru_ref[rows, C * (k + 3) : C * (k + 4)] = rad_ref[rows, 2 * C : 3 * C] * u[k]
        ent = ent_ref[rows, :]
        lane = lax.broadcasted_iota(jnp.int32, ent.shape, 1).astype(f32)
        hot = (ent == lane + float(atoms)).astype(f32).astype(bf16)
        hot_g[rows, 0:LANES] = hot
        hot_g[rows, LANES:] = hot
        near_ent = jnp.where(ent < float(atoms), ent, -1000.0)
        hot = jnp.logical_and(
            near_ent >= 0.0, jnp.logical_or(near_ent == lane, near_ent + float(atoms) == lane)
        )
        x = mm(hot.astype(f32).astype(bf16), tab2[...], 1, 0)
        x_ref[rows, :] = x
        sums = slot_sums(messages(rows, [x[:, C * k : C * (k + 1)] for k in range(4)]))
        for k in range(4):
            agg_ref[8 * c : 8 * c + 8, C * k : C * (k + 1)] = sums[k]

    kind = r.kind[...]
    atom_i = lax.broadcasted_iota(jnp.int32, (atoms, edges), 0).astype(f32)
    at_atom = jnp.sum(r.live[0:atoms, :] * atom_i, axis=0, keepdims=True)
    any_live = jnp.sum(r.live[0:atoms, :], axis=0, keepdims=True)
    key_own = jnp.where(any_live > 0.0, kind * float(atoms) + at_atom, -1.0)
    list_i = lax.broadcasted_iota(jnp.int32, (G, edges), 0).astype(f32)
    at_list = jnp.sum(r.live[atoms:, :] * list_i, axis=0, keepdims=True)
    any_list = jnp.sum(r.live[atoms:, :], axis=0, keepdims=True)
    key_list = jnp.where(any_list > 0.0, kind * float(G) + at_list, -128.0)
    keys = jnp.concatenate([key_own, key_list, jnp.zeros((14, edges), f32)], axis=0).astype(bf16)
    key_shape = (16, 2 * LANES)
    key_rhs = lax.broadcasted_iota(jnp.int32, key_shape, 0) == (lax.broadcasted_iota(jnp.int32, key_shape, 1) >> 7)
    key_rhs = key_rhs.astype(f32).astype(bf16)
    key_own_hot, key_list_ref, jac, radp = r.key_own, r.key_list, r.jac, r.radp
    for c in range(n_chunks):
        rows = rows_of(c)
        out = mm(keys[:, rows], key_rhs, 0, 0)
        lane = lax.broadcasted_iota(jnp.int32, (chunk, LANES), 1).astype(f32)
        hot = (out[:, 0:LANES] == lane).astype(f32).astype(bf16)
        key_own_hot[rows, 0:LANES] = hot
        key_own_hot[rows, LANES:] = hot
        key_list_ref[rows, :] = out[:, LANES:]
        h, th, inv_c = hid_ref[rows, :], th_ref[rows, :], inv_ref[rows, :]
        u = [u_ref[rows, LANES * k : LANES * (k + 1)] for k in range(3)]
        low = lanes_low(h.shape)
        hp = jnp.where(low, th, swap(th))
        ww = jnp.where(low, h, swap(h)) * inv_c
        zz = hp - ww
        q0 = jnp.where(low, hp, zz * u[0])
        q1_ = zz * jnp.where(low, u[1], u[2])
        w_up, w_low = jnp.where(low, 0.0, ww), jnp.where(low, ww, 0.0)
        both = [
            (u[0] * q0 + w_up, u[0] * q1_),
            (u[1] * q0, u[1] * q1_ + w_low),
            (u[2] * q0, u[2] * q1_ + w_up),
        ]
        for k in range(3):
            jac[rows, 2 * LANES * k : 2 * LANES * k + LANES] = both[k][0]
            jac[rows, 2 * LANES * k + LANES : 2 * LANES * (k + 1)] = both[k][1]
        rp = spread_w2(th)
        for k in range(4):
            col = rp[:, C * k : C * (k + 1)]
            if k in (1, 2):
                col = col - inv_c * rad_ref[rows, C * k : C * (k + 1)]
            radp[rows, C * k : C * (k + 1)] = col

    starts = [list_s[0, g] * slots for g in range(G)]
    src_t = r.src_t
    list_edges = G * slots
    for g in range(G):
        rows = slice(g * slots, (g + 1) * slots)
        key = key_list_ref[pl.ds(starts[g], slots), :]
        lane = lax.broadcasted_iota(jnp.int32, key.shape, 1).astype(f32)
        rank = kinds_n * G
        hot = jnp.logical_or(key == lane, key + float(rank) == lane)
        r.key_hot[rows, :] = jnp.where(key >= 0.0, hot.astype(f32), 0.0).astype(bf16)
        src_t[rows, :] = ent_ref[pl.ds(starts[g], slots), :]
    lane = lax.broadcasted_iota(jnp.int32, (list_edges, LANES), 1).astype(f32)
    r.src_gl[...] = jnp.transpose((src_t[...] == lane + float(atoms)).astype(f32)).astype(bf16)
    near = jnp.transpose((src_t[...] == lane).astype(f32))[0:atoms, :]
    spot = lax.broadcasted_iota(jnp.int32, (G, list_edges), 1) - lax.broadcasted_iota(
        jnp.int32, (G, list_edges), 0
    ) * slots
    blocks = ((spot >= 0) & (spot < slots)).astype(f32).astype(bf16)
    r.own_l[...] = (mm(listed, blocks, 0, 0) - near).astype(bf16)
    r.own_all[...] = (r.live[0:atoms, :] - src_hot[0:atoms, :].astype(f32)).astype(bf16)

    wait_in(2)
    tab_g = r.tab_g
    entries_g = 8 * G
    hi, lo = split(r.ghost_f[:, C:])
    tab_g[0:entries_g, C:] = hi
    tab_g[entries_g:, C:] = lo
    hi, lo = split(r.ghost_f[:, 0:C])
    tab_g[0:entries_g, 0:C] = hi
    tab_g[entries_g:, 0:C] = lo
    xg_ref = r.xg
    for c in range(n_chunks):
        rows = rows_of(c)
        x = mm(hot_g[rows, :], tab_g[...], 1, 0)
        xg_ref[rows, :] = x
        sums = slot_sums(messages(rows, [x[:, C * k : C * (k + 1)] for k in range(4)]))
        for k in range(4):
            at = (slice(8 * c, 8 * c + 8), slice(C * k, C * (k + 1)))
            agg_ref[at] = (agg_ref[at] + sums[k]) * scale
    az = dot_k(agg_ref[:, 0:C], r.msz_f, 1)
    a2 = az[:, 0:C]
    b2 = dot_k(jnp.concatenate([agg_ref[:, C * k : C * (k + 1)] for k in (1, 2, 3)], axis=0), r.mv2_f, 1)
    b2 = [b2[k * atoms : (k + 1) * atoms] for k in range(3)]
    squares = a2 * a2 + (b2[0] * b2[0] + b2[1] * b2[1] + b2[2] * b2[2])
    z = r.z0[...] + az[:, C:] + dot_k(squares, r.rhq_f, 1)
    sz = jax.nn.sigmoid(z)
    dz = r.rop[...] * (sz * (1.0 + z * (1.0 - sz)))
    down = dot_k(dz, r.rhq_b, 0)
    ds_two, dq2 = down[:, 0:C], down[:, C:]
    dagg = r.dagg
    dagg[:, 0:C] = dot_k(ds_two + 2.0 * a2 * dq2, r.ms2_b, 0) * scale
    db = dot_k(jnp.concatenate([2.0 * b * dq2 for b in b2], axis=0), r.mv2_b, 0) * scale
    for k in range(3):
        dagg[:, C * (k + 1) : C * (k + 2)] = db[k * atoms : (k + 1) * atoms]

    def spread_rows(c):
        out = []
        for k in range(4):
            small = [dagg[a : a + 1, C * k : C * (k + 1)] for a in range(c * 8, (c + 1) * 8)]
            out.append(jnp.concatenate([jnp.broadcast_to(x, (slots, C)) for x in small], axis=0))
        return out

    def scatter(first, which):
        hi_ref, lo_ref = r.dx_hi, r.dx_lo
        for a in range(atoms):
            rows = slice(a * slots, (a + 1) * slots)
            d = [dagg[a : a + 1, C * k : C * (k + 1)] for k in range(4)]
            for n, k in enumerate(which):
                if k == 0:
                    ru = [ru_ref[rows, C * (3 + m) : C * (4 + m)] for m in range(3)]
                    g = rad_ref[rows, 0:C] * d[0] + ru[0] * d[1] + (ru[1] * d[2] + ru[2] * d[3])
                else:
                    g = ru_ref[rows, C * (k - 1) : C * k] * d[0] + rad_ref[rows, 3 * C : 4 * C] * d[k]
                at = slice(C * (first + n), C * (first + n + 1))
                hi_ref[rows, at], lo_ref[rows, at] = split(g)

    def gather_grads(hot, first):
        at = slice(C * first, C * (first + 2))
        return mm(hot, r.dx_hi[:, at], 1, 0) + mm(hot, r.dx_lo[:, at], 1, 0)

    ghost_hot = slice(atoms, None)
    scatter(0, (1, 2))
    r.grad_a[...] = gather_grads(src_hot[ghost_hot, :], 0)
    send_all(3)
    scatter(2, (3, 0))
    r.grad_b[...] = gather_grads(src_hot[ghost_hot, :], 2)
    send_all(4)

    lin8 = jnp.broadcast_to(held.lin[...], (8, C))
    ro8 = jnp.broadcast_to(r.rop[...], (8, LANES))
    energy = dot3(lin8, r.scalar[...], 1, 1) + dot3(ro8, z * sz, 1, 1)
    r.eout[...] = energy[0:1, :]

    def node_grads(ds, dv, rows):
        a = r.node_a[rows, :]
        b = [r.node_b[rows, C * k : C * (k + 1)] for k in range(3)]
        dq = dot_k(ds, r.mq1_b, 0)
        da = ds + 2.0 * a * dq + (dv[0] * b[0] + dv[1] * b[1] + dv[2] * b[2])
        db = jnp.concatenate([dv[k] * (1.0 + a) + 2.0 * b[k] * dq for k in range(3)], axis=0)
        n = ds.shape[0]
        back = dot_k(db, r.wm1, 1)
        back = [dot_k(da, r.wm0, 1)] + [back[k * n : (k + 1) * n] for k in range(3)]
        hi, lo = split(jnp.concatenate(turn(back), axis=0))
        return jnp.concatenate([hi, lo], axis=0)

    def lane_put(sums):
        lane = lax.broadcasted_iota(jnp.int32, sums[0].shape, 1)
        out = jnp.zeros(sums[0].shape, f32)
        for k in range(3):
            out = jnp.where(lane == k, jnp.sum(sums[k], axis=1, keepdims=True), out)
        return out

    own_a = gather_grads(src_hot[0:atoms, :], 0)
    own_b = gather_grads(src_hot[0:atoms, :], 2)
    ds_own = own_b[:, C:] + ds_two + held.lin[...]
    r.gp[...] = node_grads(ds_own, [own_a[:, 0:C], own_a[:, C:], own_b[:, 0:C]], slice(0, atoms))
    f_own = r.f_own
    for c in range(n_chunks):
        rows = rows_of(c)
        d = spread_rows(c)
        x = [x_ref[rows, C * k : C * (k + 1)] + xg_ref[rows, C * k : C * (k + 1)] for k in range(4)]
        s, v = x[0], x[1:]
        u = [u_ref[rows, LANES * k : LANES * (k + 1)] for k in range(3)]
        rp = [radp[rows, C * k : C * (k + 1)] for k in range(4)]
        uv = u[0] * v[0] + u[1] * v[1] + u[2] * v[2]
        ud = u[0] * d[1] + u[1] * d[2] + u[2] * d[3]
        dv = d[1] * v[0] + d[2] * v[1] + d[3] * v[2]
        along = rp[0] * (d[0] * s) + rp[1] * (d[0] * uv) + (rp[2] * (s * ud) + rp[3] * dv)
        r1d = (rad_ref[rows, C : 2 * C] * d[0]) * inv_ref[rows, :]
        r2s = (rad_ref[rows, 2 * C : 3 * C] * s) * inv_ref[rows, :]
        g = mm(key_own_hot[rows, :], r.gp[...], 1, 0)
        g0, g1 = g[:, 0:LANES], g[:, LANES:]
        sums = []
        for k in range(3):
            j0 = jac[rows, 2 * LANES * k : 2 * LANES * k + LANES]
            j1 = jac[rows, 2 * LANES * k + LANES : 2 * LANES * (k + 1)]
            sums.append((u[k] * along + r1d * v[k]) + (r2s * d[k + 1] + (g0 * j0 + g1 * j1)))
        f_own[rows, :] = lane_put(sums)
    hi, mid, lo = split3(f_own[...])
    hot = src_hot[ghost_hot, :]
    r.force_o[...] = mm(hot, hi, 1, 0) + (mm(hot, mid, 1, 0) + mm(hot, lo, 1, 0))
    own = r.own_all[...]
    r.force_n[...] = mm(own, hi, 1, 0) + (mm(own, mid, 1, 0) + mm(own, lo, 1, 0))


    def total(ref):
        out = [ref[k] for k in range(8)]
        while len(out) > 1:
            out = [out[i] + out[i + 1] for i in range(0, len(out), 2)]
        return out[0]

    wait_in(3)
    g_a = total(r.in_a)
    wait_in(4)
    g_b = total(r.in_b)
    gp_l = node_grads(g_b[:, C:], [g_a[:, 0:C], g_a[:, C:], g_b[:, 0:C]], slice(atoms, nodes))
    f_list = []
    for g in range(G):
        rows = slice(g * slots, (g + 1) * slots)
        at = pl.ds(starts[g], slots)
        if g % 4 == 0:
            wide = mm(r.key_hot[g * slots : (g + 4) * slots, :], gp_l, 1, 0)
        m = g % 4
        here = wide[m * slots : (m + 1) * slots]
        g0, g1 = here[:, 0:LANES], here[:, LANES:]
        sums = []
        for k in range(3):
            j0 = jac[at, 2 * LANES * k : 2 * LANES * k + LANES]
            j1 = jac[at, 2 * LANES * k + LANES : 2 * LANES * (k + 1)]
            sums.append(g0 * j0 + g1 * j1)
        f_list.append(lane_put(sums))
    f_list = jnp.concatenate(f_list, axis=0)
    l_hi, l_lo = split(f_list)
    hot = r.src_gl[...]
    r.force_g[...] = r.force_o[...] + (mm(hot, l_hi, 1, 0) + mm(hot, l_lo, 1, 0))
    send_all(5)
    own_l = r.own_l[...]
    force = r.force_n[...] + (mm(own_l, l_hi, 1, 0) + mm(own_l, l_lo, 1, 0))
    force = jnp.transpose(force)
    for phase in (0, 2, 3, 4):
        wait_out(phase)
    wait_in(5)
    late = total(r.in_f)
    for k in range(3):
        back = jnp.sum(late[:, k : k + 1] * listed_f, axis=0, keepdims=True)
        r.fout[k : k + 1, :] = force[k : k + 1, :] - back
    wait_out(5)


def store_kernel(e_ref, f_ref, eo_ref, fo_ref, sem):
    one = pltpu.make_async_copy(e_ref, eo_ref, sem.at[0])
    two = pltpu.make_async_copy(f_ref, fo_ref, sem.at[1])
    one.start()
    two.start()
    one.wait()
    two.wait()


def in_order(vec, senders, counts, species, list, embed, win1, wmid1, wout1, ms1, mv1, mq1, win2, wmid2, wout2, ms2, mv2, mq2, lin, rh, ro):
    return dict(locals())


def on_device(n_dom, n_sub, *args):
    (vec, senders, counts, species, send_list, embed) = args[:6]
    weights = list(args[6:18])
    read_lin, read_hidden, read_out = args[18:]
    edges = vec.shape[1]
    atoms = species.shape[0]
    G = send_list.shape[0]
    C, kinds_n = embed.shape
    hidden, n_basis = weights[0].shape
    for i in (0, 2, 6, 8):
        weights[i] = weights[i].T
    row = lambda x: x.reshape(1, -1)
    operands = [vec, row(senders), row(counts), row(species), row(send_list), embed.T, *weights]
    operands += [row(read_lin), read_hidden, row(read_out)]
    far, nodes, list_edges = 8 * G, atoms + G, G * (edges // atoms)
    i32 = jnp.int32
    packed = -(-(6 * n_basis + 24) // 16) * 16
    inputs = in_order(*operands)
    scratch = dict(
        kind_out=((G, LANES), f32),
        ghost_kind=((far, LANES), f32),
        out_f=((G, 4 * C), f32),
        ghost_f=((far, 4 * C), f32),
        grad_a=((far, 2 * C), f32),
        grad_b=((far, 2 * C), f32),
        in_a=((8, G, 2 * C), f32),
        in_b=((8, G, 2 * C), f32),
        force_g=((far, LANES), f32),
        force_o=((far, LANES), f32),
        force_n=((atoms, LANES), f32),
        in_f=((8, G, LANES), f32),
        rhs=((packed, 7 * LANES), f32),
        wide_rhs=((packed, 7 * LANES), bf16),
        pack=((packed, edges), bf16),
        v8=((8, edges), f32),
        winp=((n_basis, LANES), f32),
        wmid=((LANES, LANES), f32),
        wmid_f=((LANES, 3 * LANES), bf16),
        w2_k=((2 * LANES, 4 * C), bf16),
        rhp=((LANES, C), f32),
        rop=((1, LANES), f32),
        kind_own=((1, edges), f32),
        src_f=((far, edges), f32),
        kind=((1, edges), f32),
        live=((nodes, edges), f32),
        src_hot=((atoms + far, edges), bf16),
        hid=((edges, LANES), f32),
        th=((edges, LANES), f32),
        u=((edges, 3 * LANES), f32),
        inv=((edges, LANES), f32),
        ent=((edges, LANES), f32),
        p_hi=((edges, 2 * LANES), bf16),
        p_lo=((edges, 2 * LANES), bf16),
        rad=((edges, 4 * C), f32),
        radp=((edges, 4 * C), f32),
        ru=((edges, 6 * C), f32),
        jac=((edges, 6 * LANES), f32),
        wm0=((kinds_n * hidden, 3 * C), bf16),
        wm1=((kinds_n * hidden, 3 * C), bf16),
        mq1_f=((C, 3 * C), bf16),
        mq1_b=((3 * C, C), bf16),
        msz_f=((C + LANES, 3 * C), bf16),
        mv2_f=((C, 3 * C), bf16),
        rhq_f=((LANES, 3 * C), bf16),
        rhq_b=((3 * LANES, 2 * C), bf16),
        ms2_b=((3 * C, C), bf16),
        mv2_b=((3 * C, C), bf16),
        initial=((nodes, C), f32),
        node_a=((nodes, C), f32),
        node_b=((nodes, 3 * C), f32),
        scalar=((atoms, C), f32),
        z0=((atoms, LANES), f32),
        tab2=((LANES, 4 * C), bf16),
        tab_g=((2 * far, 4 * C), bf16),
        hot_g=((edges, 2 * LANES), bf16),
        x=((edges, 4 * C), f32),
        xg=((edges, 4 * C), f32),
        agg=((atoms, 4 * C), f32),
        dagg=((atoms, 4 * C), f32),
        key_own=((edges, 2 * LANES), bf16),
        key_list=((edges, LANES), f32),
        key_hot=((list_edges, LANES), bf16),
        src_t=((list_edges, LANES), f32),
        src_gl=((far, list_edges), bf16),
        own_l=((atoms, list_edges), bf16),
        own_all=((atoms, edges), bf16),
        dx_hi=((edges, 4 * C), bf16),
        dx_lo=((edges, 4 * C), bf16),
        gp=((2 * kinds_n * atoms, 2 * LANES), bf16),
        f_own=((edges, LANES), f32),
    )
    names = list(inputs) + ["eout", "fout"] + [k + "_" for k in inputs] + list(scratch)
    copies = [pltpu.VMEM(x.shape, x.dtype) for x in operands]
    hbm = pl.BlockSpec(memory_space=pltpu.HBM)
    whole = pl.BlockSpec(memory_space=pltpu.VMEM)
    out = pl.pallas_call(
        functools.partial(kernel, n_dom, n_sub, names),
        out_shape=[pltpu.VMEM((1, atoms), f32), pltpu.VMEM((3, atoms), f32)],
        in_specs=[hbm] * len(operands),
        out_specs=[whole, whole],
        scratch_shapes=copies
        + [pltpu.VMEM(shape, dtype) for shape, dtype in scratch.values()]
        + [pltpu.SMEM((1, G), i32)]
        + [pltpu.SemaphoreType.DMA((6, 9)), pltpu.SemaphoreType.DMA((6, 9))]
        + [pltpu.SemaphoreType.DMA((len(operands) + 1,))],
        compiler_params=pltpu.CompilerParams(
            collective_id=0, has_side_effects=True, vmem_limit_bytes=56 * 1024 * 1024
        ),
    )(*operands)
    out = pl.pallas_call(
        store_kernel,
        out_shape=[jax.ShapeDtypeStruct((1, atoms), f32), jax.ShapeDtypeStruct((3, atoms), f32)],
        in_specs=[whole, whole],
        out_specs=[hbm, hbm],
        scratch_shapes=[pltpu.SemaphoreType.DMA((2,))],
    )(*[pltpu.with_memory_space_constraint(o, pltpu.VMEM) for o in out])
    return out[0].reshape(atoms), out[1]


def solution(mesh):
    one = P(("dom", "sub"))
    return jax.shard_map(
        functools.partial(on_device, mesh.shape["dom"], mesh.shape["sub"]),
        mesh=mesh,
        in_specs=(P(None, ("dom", "sub")), one, one, one, one) + (P(),) * 16,
        out_specs=(one, P(None, ("dom", "sub"))),
        check_vma=False,
    )
```

```python
import functools
import math
import types

import jax
import jax.numpy as jnp
from jax import lax
from jax.experimental import pallas as pl
from jax.experimental.pallas import tpu as pltpu
from jax.sharding import PartitionSpec as P

cutoff_radius = 5.0
f32 = jnp.float32
bf16 = jnp.bfloat16
LANES = 128
MESH = pl.DeviceIdType.MESH


def mm(a, b, ca, cb):
    return lax.dot_general(a, b, (((ca,), (cb,)), ((), ())), preferred_element_type=f32)


def split(x):
    hi = x.astype(bf16)
    return hi, (x - hi.astype(f32)).astype(bf16)


def split3(x):
    hi = x.astype(bf16)
    rest = x - hi.astype(f32)
    mid = rest.astype(bf16)
    return hi, mid, (rest - mid.astype(f32)).astype(bf16)


def dot3(a, b, ca, cb):
    a_hi, a_lo = split(a)
    b_hi, b_lo = split(b)
    return mm(a_hi, b_hi, ca, cb) + (mm(a_hi, b_lo, ca, cb) + mm(a_lo, b_hi, ca, cb))


def hot3(hot, x, ca, cb):
    hi, mid, lo = split3(x)
    return mm(hot, hi, ca, cb) + (mm(hot, mid, ca, cb) + mm(hot, lo, ca, cb))


def to_column(row):
    count = row.shape[1]
    shape = (count, count)
    same = lax.broadcasted_iota(jnp.int32, shape, 0) == lax.broadcasted_iota(jnp.int32, shape, 1)
    return jnp.sum(jnp.where(same, row, 0.0), axis=1, keepdims=True)


def series(t, first, terms):
    total = jnp.ones_like(t)
    for i in reversed(range(terms)):
        low = first + 2 * i
        total = 1.0 - t * (1.0 / (low * (low + 1))) * total
    return total


def kernel(n_dom, n_sub, names, *refs):
    r = types.SimpleNamespace(**dict(zip(names, refs)))
    inputs = len(in_order(*range(21)))
    hbm = types.SimpleNamespace(**dict(zip(names[:inputs], refs[:inputs])))
    held = types.SimpleNamespace(**dict(zip(names[:inputs], refs[inputs + 2 : 2 * inputs + 2])))
    list_s, send_sem, recv_sem, in_sem = refs[-4:]
    dm, sb = lax.axis_index("dom"), lax.axis_index("sub")
    atoms = hbm.species.shape[1]
    edges = hbm.vec.shape[1]
    slots = edges // atoms
    G = hbm.list.shape[1]
    kinds_n, C = hbm.embed.shape
    n_basis, hidden = hbm.win1.shape
    chunk = 8 * slots
    n_chunks = edges // chunk
    scale = slots ** (-0.5)
    sides = [s for s in range(9) if s != 4]
    nodes = atoms + G

    def exists(s):
        ok = None
        for here, count, off in ((dm, n_dom, s // 3 - 1), (sb, n_sub, s % 3 - 1)):
            if off == 0:
                continue
            one = here > 0 if off < 0 else here < count - 1
            ok = one if ok is None else jnp.logical_and(ok, one)
        return ok

    def place(s):
        return (dm + (s // 3 - 1), sb + (s % 3 - 1))

    def row_of(s):
        return s if s < 4 else s - 1

    def block(s):
        return pl.ds(G * row_of(s), G)

    def copies(phase, s, there):
        o = 8 - s
        src, dst = (
            lambda: (r.kind_out, r.ghost_kind.at[row_of(o)]),
            lambda: (r.out_f, r.ghost_f.at[block(o)]),
            lambda: (r.out_f, r.ghost_f.at[block(o)]),
            lambda: (r.grad_a.at[block(s)], r.in_a.at[row_of(o)]),
            lambda: (r.grad_b.at[block(s)], r.in_b.at[row_of(o)]),
            lambda: (r.force_g.at[pl.ds(row_of(s) * (G // 2), G // 2)], r.in_f.at[row_of(o)]),
        )[phase]()
        return pltpu.make_async_remote_copy(
            src_ref=src,
            dst_ref=dst,
            send_sem=send_sem.at[phase, s],
            recv_sem=recv_sem.at[phase, o],
            device_id=place(there),
            device_id_type=MESH,
        )

    def send_all(phase):
        for s in sides:
            @pl.when(exists(s))
            def _():
                copies(phase, s, s).start()

    def wait_in(phase):
        for s in sides:
            @pl.when(exists(s))
            def _():
                copies(phase, 8 - s, s).wait_recv()

    def wait_out(phase):
        for s in sides:
            @pl.when(exists(s))
            def _():
                copies(phase, s, s).wait_send()

    groups = [
        [hbm.species, hbm.list],
        [hbm.vec, hbm.counts, hbm.senders, hbm.win1, hbm.win2, hbm.wmid1, hbm.wmid2],
        [hbm.wout1, hbm.embed, hbm.ms1, hbm.mv1, hbm.mq1, hbm.wout2],
    ]
    groups.append([x for x in refs[:inputs] if not any(x is y for group in groups for y in group)])
    inside = dict(zip(map(id, refs[:inputs]), refs[inputs + 2 : 2 * inputs + 2]))
    spots = {id(x): i for i, x in enumerate(refs[:inputs])}
    pulls = [[pltpu.make_async_copy(x, inside[id(x)], in_sem.at[spots[id(x)]]) for x in group] for group in groups]
    pulls[3].append(pltpu.make_async_copy(hbm.list, list_s, in_sem.at[inputs]))

    def start(group):
        for pull in pulls[group]:
            pull.start()

    def arrive(group):
        for pull in pulls[group]:
            pull.wait()

    start(0)
    r.ghost_kind[...] = jnp.zeros_like(r.ghost_kind)
    barrier = pltpu.get_barrier_semaphore()
    for s in sides:
        @pl.when(exists(s))
        def _():
            pl.semaphore_signal(barrier, inc=1, device_id=place(s), device_id_type=MESH)
    for group in (1, 2, 3):
        start(group)
    peers = [
        1 + jnp.where(at > 0, 1, 0) + jnp.where(at < count - 1, 1, 0)
        for at, count in ((dm, n_dom), (sb, n_sub))
    ]

    for ref in (r.ghost_f, r.in_a, r.in_b, r.in_f):
        ref[...] = jnp.zeros_like(ref)
    for ref in (r.rhs, r.v8, r.winp, r.wmid, r.rhp, r.rop, r.tab2):
        ref[...] = jnp.zeros_like(ref)
    arrive(0)
    species_row = held.species[...].astype(f32)
    species_col = to_column(species_row)
    list_col = to_column(held.list[...].astype(f32))
    listed_f = (list_col == lax.broadcasted_iota(jnp.int32, (G, atoms), 1).astype(f32)).astype(f32)
    listed = listed_f.astype(bf16)
    list_kinds = jnp.sum(listed_f * species_row, axis=1, keepdims=True)
    half = G // 2
    left = lax.broadcasted_iota(jnp.int32, (half, LANES), 1) < LANES // 2
    r.kind_out[...] = jnp.where(left, list_kinds[0:half], list_kinds[half:])
    pl.semaphore_wait(barrier, peers[0] * peers[1] - 1)
    send_all(0)
    arrive(1)

    def lanes_low(shape):
        return lax.broadcasted_iota(jnp.int32, shape, 1) < hidden

    def swap(x):
        return pltpu.roll(x, hidden, 1)

    def stack3(x, axis):
        hi, lo = split(x)
        return jnp.concatenate([hi, hi, lo], axis=axis)

    def dot_k(a, stacked, dim):
        k = a.shape[1]
        a_hi, a_lo = split(a)
        both = jnp.concatenate([a_hi, a_lo], axis=1)
        if dim == 1:
            first, last = stacked[:, : 2 * k], stacked[:, 2 * k :]
        else:
            first, last = stacked[: 2 * k, :], stacked[2 * k :, :]
        return mm(both, first, 1, dim) + mm(a_hi, last, 1, dim)

    def rows_of(c):
        return slice(c * chunk, (c + 1) * chunk)

    wmid, winp, rhs = r.wmid, r.winp, r.rhs
    wmid[0:hidden, 0:hidden] = held.wmid1[...]
    wmid[hidden:, hidden:] = held.wmid2[...]
    wmid_f = r.wmid_f
    wmid_f[...] = stack3(wmid[...], 1)
    winp[:, 0:hidden] = held.win1[...]
    winp[:, hidden:] = held.win2[...]
    row_i = lax.broadcasted_iota(jnp.int32, rhs.shape, 0) - 6 * n_basis
    lane_i = lax.broadcasted_iota(jnp.int32, rhs.shape, 1)
    which_block = lane_i >> 7
    part_row = row_i & 7
    hit = jnp.logical_and(which_block >= 2, part_row == which_block - 2)
    rhs[...] = jnp.where(hit & (row_i >= 0) & (row_i < 24), 1.0, 0.0)
    hi, lo = split(winp[...])
    for t in range(2):
        at = slice(LANES * t, LANES * (t + 1))
        base = 3 * n_basis * t
        rhs[base : base + n_basis, at] = hi.astype(f32)
        rhs[base + n_basis : base + 2 * n_basis, at] = hi.astype(f32)
        rhs[base + 2 * n_basis : base + 3 * n_basis, at] = lo.astype(f32)
    r.wide_rhs[...] = rhs[...].astype(bf16)

    v8 = r.v8
    v8[0:3, :] = held.vec[...]
    vectors = v8[...]
    dist = jnp.sqrt(jnp.sum(vectors * vectors, axis=0, keepdims=True))
    inv = 1.0 / dist
    unit = vectors * inv
    x1 = dist * (1.0 / cutoff_radius)
    x2 = x1 * x1
    x5 = x2 * x2 * x1
    x6 = x5 * x1
    env = 1.0 + x6 * (-28.0 + x1 * (48.0 - 21.0 * x1))
    denv = x5 * (-168.0 + x1 * (336.0 - 168.0 * x1)) * (1.0 / cutoff_radius)
    order_n = (lax.broadcasted_iota(jnp.int32, (n_basis, edges), 0) + 1).astype(f32)
    turns = order_n * x1
    near = jnp.floor(turns + 0.5)
    odd = near - 2.0 * jnp.floor(near * 0.5)
    sign = 1.0 - 2.0 * odd
    angle = (turns - near) * math.pi
    t2 = angle * angle
    sine = sign * angle * series(t2, 2, 7)
    cosine = sign * series(t2, 1, 7)
    norm = math.sqrt(2.0 / cutoff_radius)
    wave = (norm * inv) * sine
    basis = wave * env
    dbasis = ((norm * math.pi / cutoff_radius) * order_n * cosine * inv - wave * inv) * env + wave * denv

    counts_row = held.counts[...].astype(f32)
    counts_col = to_column(counts_row).astype(jnp.int32)
    list_counts = jnp.sum(listed_f * counts_row, axis=1, keepdims=True).astype(jnp.int32)
    list_at = list_col.astype(jnp.int32) * slots

    def live_of(rows, start, count):
        spot = lax.broadcasted_iota(jnp.int32, (rows, edges), 1) - start
        return ((spot >= 0) & (spot < count)).astype(f32)

    live = live_of(atoms, lax.broadcasted_iota(jnp.int32, (atoms, edges), 0) * slots, counts_col)
    r.live[0:atoms, :] = live
    r.live[atoms:, :] = live_of(G, list_at, list_counts)
    live_row = jnp.sum(live, axis=0, keepdims=True)
    sent = held.senders[...]
    entry = jnp.where(sent >= atoms + 5 * G, sent - G, sent)
    src_hot = r.src_hot
    source = jnp.where(lax.broadcasted_iota(jnp.int32, src_hot.shape, 0) == entry, live_row, 0.0)
    src_hot[...] = source.astype(bf16)
    r.src_f[...] = source[atoms:, :]
    r.kind_own[...] = jnp.sum(source[0:atoms, :] * species_col, axis=0, keepdims=True)
    live_entry = jnp.where(live_row > 0.0, entry.astype(f32), -1.0)

    eight = lax.broadcasted_iota(jnp.int32, (8, edges), 0)
    unit = jnp.where(eight == 3, inv, jnp.where(eight == 4, live_entry, unit))
    b_hi, b_lo = split(basis)
    d_hi, d_lo = split(dbasis)
    parts = [b_hi, b_lo, b_hi, d_hi, d_lo, d_hi] + list(split3(unit))
    parts = [p.astype(f32) for p in parts] + [jnp.zeros((8, edges), f32)]
    r.pack[...] = jnp.concatenate(parts, axis=0).astype(bf16)

    hid_ref, th_ref, u_ref, inv_ref, ent_ref = r.hid, r.th, r.u, r.inv, r.ent
    p_hi, p_lo, rad_ref = r.p_hi, r.p_lo, r.rad

    def spread_w2(h):
        h_hi, h_lo = split(h)
        twice = jnp.where(lanes_low(h.shape), swap(h), h).astype(bf16)
        return mm(jnp.concatenate([twice, h_lo], axis=1), r.w2_k[...], 1, 0)

    for c in range(n_chunks):
        rows = rows_of(c)
        out = mm(r.pack[:, rows], r.wide_rhs[...], 0, 0)
        p1, t1 = out[:, 0:LANES], out[:, LANES : 2 * LANES]
        u = [out[:, LANES * k : LANES * (k + 1)] for k in (2, 3, 4)]
        u_ref[rows, :] = out[:, 2 * LANES : 5 * LANES]
        inv_ref[rows, :] = out[:, 5 * LANES : 6 * LANES]
        ent_ref[rows, :] = out[:, 6 * LANES : 7 * LANES]
        s1 = jax.nn.sigmoid(p1)
        h1 = p1 * s1
        th1 = (s1 * (1.0 + p1 * (1.0 - s1))) * t1
        p2 = dot_k(h1, wmid_f, 1)
        t2_ = dot_k(th1, wmid_f, 1)
        s2 = jax.nn.sigmoid(p2)
        h = p2 * s2
        hid_ref[rows, :] = h
        th_ref[rows, :] = (s2 * (1.0 + p2 * (1.0 - s2))) * t2_
        low = lanes_low(h.shape)
        hh = jnp.where(low, h, swap(h))
        prod = jnp.concatenate([hh * jnp.where(low, 1.0, u[0]), hh * jnp.where(low, u[1], u[2])], axis=1)
        hi, lo = split(prod)
        p_hi[rows, :] = hi
        p_lo[rows, :] = lo

    arrive(2)
    hi, lo = split(held.wout2[...])
    r.w2_k[...] = jnp.concatenate([lo, hi, jnp.zeros_like(hi), hi], axis=0)
    w1 = held.wout1[...]
    for ref, at, mix in ((r.wm0, 0, held.ms1), (r.wm1, 1, held.mv1)):
        path = w1[:, C * at : C * (at + 1)]
        with_kind = jnp.concatenate([path * held.embed[k : k + 1, :] for k in range(kinds_n)], axis=0)
        ref[...] = stack3(dot3(with_kind, mix[...], 1, 1) * scale, 1)
    r.mq1_f[...] = stack3(held.mq1[...], 1)
    initial = jnp.zeros((nodes, C), f32)
    node_kinds = jnp.concatenate([species_col, list_kinds], axis=0)
    for k in range(kinds_n):
        initial = jnp.where(node_kinds == k, held.embed[k : k + 1, :], initial)
    r.initial[...] = initial

    for c in range(n_chunks):
        rad_ref[rows_of(c), :] = spread_w2(hid_ref[rows_of(c), :])

    wait_in(0)
    total = jnp.zeros((half, edges), f32)
    for s in sides:
        for m in range(2):
            at = slice(row_of(s) * G + half * m, row_of(s) * G + half * (m + 1))
            lane = m * (LANES // 2)
            total = total + r.ghost_kind[row_of(s), :, lane : lane + 1] * r.src_f[at, :]
    r.kind[...] = r.kind_own[...] + jnp.sum(total, axis=0, keepdims=True)

    listed_sum = None
    own_sums = []
    for c in range(n_chunks):
        rows = rows_of(c)
        kind = r.kind[:, rows]
        own = jnp.where(r.live[8 * c : 8 * c + 8, rows] > 0.0, kind, -1.0)
        far = jnp.where(r.live[atoms:, rows] > 0.0, kind, -1.0)
        hot = [(own == k).astype(f32) for k in range(kinds_n)] + [(far == k).astype(f32) for k in range(kinds_n)]
        hot = jnp.concatenate(hot, axis=0).astype(bf16)
        total = mm(hot, p_hi[rows, :], 1, 0) + mm(hot, p_lo[rows, :], 1, 0)
        own_sums.append(total[0 : 8 * kinds_n])
        tail = total[8 * kinds_n :]
        listed_sum = tail if listed_sum is None else listed_sum + tail
    by_kind = []
    for k in range(kinds_n):
        rows_k = [x[8 * k : 8 * (k + 1)] for x in own_sums] + [listed_sum[G * k : G * (k + 1)]]
        by_kind.append(jnp.concatenate(rows_k, axis=0))

    def turn(parts):
        out = []
        low = lanes_low((parts[0].shape[0], LANES))
        for j in range(4):
            at = slice(LANES * (j // 2), LANES * (j // 2 + 1))
            halves = []
            for m in (0, 2):
                first, second = parts[m][:, at], parts[m + 1][:, at]
                if j % 2 == 0:
                    halves.append(jnp.where(low, first, swap(second)))
                else:
                    halves.append(jnp.where(low, swap(first), second))
            out.append(jnp.concatenate(halves, axis=1))
        return out

    def dot_m(x, stacked):
        hi, lo = split(x)
        w_hi, w_lo = stacked[:, 0:C], stacked[:, 2 * C :]
        return mm(hi, w_hi, 1, 0) + (mm(lo, w_hi, 1, 0) + mm(hi, w_lo, 1, 0))

    turned = turn(by_kind)
    a1 = dot_m(turned[0], r.wm0)
    b1 = dot_m(jnp.concatenate(turned[1:], axis=0), r.wm1)
    b1 = [b1[k * nodes : (k + 1) * nodes] for k in range(3)]
    one_a = 1.0 + a1
    vec_one = [b * one_a for b in b1]
    for k in range(3):
        r.out_f[:, C * (k + 1) : C * (k + 2)] = vec_one[k][atoms:]
    q1 = dot_k(a1 * a1 + (b1[0] * b1[0] + b1[1] * b1[1] + b1[2] * b1[2]), r.mq1_f, 1)
    scalar_one = r.initial[...] + a1 + q1
    r.out_f[:, 0:C] = scalar_one[atoms:]
    send_all(2)
    r.node_a[...] = a1
    for k in range(3):
        r.node_b[:, C * k : C * (k + 1)] = b1[k]
    own_feats = [scalar_one[0:atoms]] + [v[0:atoms] for v in vec_one]
    r.scalar[...] = own_feats[0]

    arrive(3)
    tab2 = r.tab2
    for k in range(4):
        hi, lo = split(own_feats[k])
        tab2[0:atoms, C * k : C * (k + 1)] = hi
        tab2[atoms : 2 * atoms, C * k : C * (k + 1)] = lo

    rhp = r.rhp
    rhp[0 : held.rh.shape[0], :] = held.rh[...]
    r.rop[:, 0 : held.ro.shape[1]] = held.ro[...]
    rh_ms = dot3(rhp[...], held.ms2[...], 1, 0)
    rh_mq = dot3(rhp[...], held.mq2[...], 1, 0)
    r.msz_f[...] = stack3(jnp.concatenate([held.ms2[...], rh_ms], axis=0), 1)
    r.mv2_f[...] = stack3(held.mv2[...], 1)
    r.rhq_f[...] = stack3(rh_mq, 1)
    r.rhq_b[...] = stack3(jnp.concatenate([rhp[...], rh_mq], axis=1), 0)
    r.ms2_b[...] = stack3(held.ms2[...], 0)
    r.mv2_b[...] = stack3(held.mv2[...], 0)
    r.mq1_b[...] = stack3(held.mq1[...], 0)
    r.z0[...] = dot3(own_feats[0], rhp[...], 1, 1)

    ru_ref, x_ref, agg_ref, hot_g = r.ru, r.x, r.agg, r.hot_g

    def messages(rows, x):
        s, v = x[0], x[1:]
        ru = [ru_ref[rows, C * k : C * (k + 1)] for k in range(6)]
        r0, r3 = rad_ref[rows, 0:C], rad_ref[rows, 3 * C : 4 * C]
        first = r0 * s + ru[0] * v[0] + (ru[1] * v[1] + ru[2] * v[2])
        return [first] + [ru[3 + k] * s + r3 * v[k] for k in range(3)]

    def slot_sums(msgs):
        sub = lax.broadcasted_iota(jnp.int32, (8, C), 0)
        outs = []
        for m in msgs:
            parts = [sum(m[a * slots + 8 * i : a * slots + 8 * i + 8] for i in range(slots // 8)) for a in range(8)]
            low = sub < 4
            parts = [
                jnp.where(low, x, y) + pltpu.roll(jnp.where(low, y, x), 4, 0)
                for x, y in zip(parts[:4], parts[4:])
            ]
            for width in (2, 1):
                first = (sub & width) == 0
                parts = [
                    jnp.where(first, x + pltpu.roll(x, 8 - width, 0), y + pltpu.roll(y, width, 0))
                    for x, y in zip(parts[:width], parts[width:])
                ]
            outs.append(parts[0])
        return outs

    for c in range(n_chunks):
        rows = rows_of(c)
        u = [u_ref[rows, LANES * k : LANES * (k + 1)] for k in range(3)]
        for k in range(3):
            ru_ref[rows, C * k : C * (k + 1)] = rad_ref[rows, C : 2 * C] * u[k]
            ru_ref[rows, C * (k + 3) : C * (k + 4)] = rad_ref[rows, 2 * C : 3 * C] * u[k]
        ent = ent_ref[rows, :]
        lane = lax.broadcasted_iota(jnp.int32, ent.shape, 1).astype(f32)
        hot = (ent == lane + float(atoms)).astype(f32).astype(bf16)
        hot_g[rows, 0:LANES] = hot
        hot_g[rows, LANES:] = hot
        near_ent = jnp.where(ent < float(atoms), ent, -1000.0)
        hot = jnp.logical_and(
            near_ent >= 0.0, jnp.logical_or(near_ent == lane, near_ent + float(atoms) == lane)
        )
        x = mm(hot.astype(f32).astype(bf16), tab2[...], 1, 0)
        x_ref[rows, :] = x
        sums = slot_sums(messages(rows, [x[:, C * k : C * (k + 1)] for k in range(4)]))
        for k in range(4):
            agg_ref[8 * c : 8 * c + 8, C * k : C * (k + 1)] = sums[k]

    kind = r.kind[...]
    atom_i = lax.broadcasted_iota(jnp.int32, (atoms, edges), 0).astype(f32)
    at_atom = jnp.sum(r.live[0:atoms, :] * atom_i, axis=0, keepdims=True)
    any_live = jnp.sum(r.live[0:atoms, :], axis=0, keepdims=True)
    key_own = jnp.where(any_live > 0.0, kind * float(atoms) + at_atom, -1.0)
    list_i = lax.broadcasted_iota(jnp.int32, (G, edges), 0).astype(f32)
    at_list = jnp.sum(r.live[atoms:, :] * list_i, axis=0, keepdims=True)
    any_list = jnp.sum(r.live[atoms:, :], axis=0, keepdims=True)
    key_list = jnp.where(any_list > 0.0, kind * float(G) + at_list, -128.0)
    keys = jnp.concatenate([key_own, key_list, jnp.zeros((14, edges), f32)], axis=0).astype(bf16)
    key_shape = (16, 2 * LANES)
    key_rhs = lax.broadcasted_iota(jnp.int32, key_shape, 0) == (lax.broadcasted_iota(jnp.int32, key_shape, 1) >> 7)
    key_rhs = key_rhs.astype(f32).astype(bf16)
    key_own_hot, key_list_ref, jac, radp = r.key_own, r.key_list, r.jac, r.radp
    for c in range(n_chunks):
        rows = rows_of(c)
        out = mm(keys[:, rows], key_rhs, 0, 0)
        lane = lax.broadcasted_iota(jnp.int32, (chunk, LANES), 1).astype(f32)
        hot = (out[:, 0:LANES] == lane).astype(f32).astype(bf16)
        key_own_hot[rows, 0:LANES] = hot
        key_own_hot[rows, LANES:] = hot
        key_list_ref[rows, :] = out[:, LANES:]
        h, th, inv_c = hid_ref[rows, :], th_ref[rows, :], inv_ref[rows, :]
        u = [u_ref[rows, LANES * k : LANES * (k + 1)] for k in range(3)]
        low = lanes_low(h.shape)
        hp = jnp.where(low, th, swap(th))
        ww = jnp.where(low, h, swap(h)) * inv_c
        zz = hp - ww
        q0 = jnp.where(low, hp, zz * u[0])
        q1_ = zz * jnp.where(low, u[1], u[2])
        w_up, w_low = jnp.where(low, 0.0, ww), jnp.where(low, ww, 0.0)
        both = [
            (u[0] * q0 + w_up, u[0] * q1_),
            (u[1] * q0, u[1] * q1_ + w_low),
            (u[2] * q0, u[2] * q1_ + w_up),
        ]
        for k in range(3):
            jac[rows, 2 * LANES * k : 2 * LANES * k + LANES] = both[k][0]
            jac[rows, 2 * LANES * k + LANES : 2 * LANES * (k + 1)] = both[k][1]
        rp = spread_w2(th)
        for k in range(4):
            col = rp[:, C * k : C * (k + 1)]
            if k in (1, 2):
                col = col - inv_c * rad_ref[rows, C * k : C * (k + 1)]
            radp[rows, C * k : C * (k + 1)] = col

    starts = [list_s[0, g] * slots for g in range(G)]
    src_t = r.src_t
    list_edges = G * slots
    for g in range(G):
        rows = slice(g * slots, (g + 1) * slots)
        key = key_list_ref[pl.ds(starts[g], slots), :]
        lane = lax.broadcasted_iota(jnp.int32, key.shape, 1).astype(f32)
        rank = kinds_n * G
        hot = jnp.logical_or(key == lane, key + float(rank) == lane)
        r.key_hot[rows, :] = jnp.where(key >= 0.0, hot.astype(f32), 0.0).astype(bf16)
        src_t[rows, :] = ent_ref[pl.ds(starts[g], slots), :]
    lane = lax.broadcasted_iota(jnp.int32, (list_edges, LANES), 1).astype(f32)
    r.src_gl[...] = jnp.transpose((src_t[...] == lane + float(atoms)).astype(f32)).astype(bf16)
    near = jnp.transpose((src_t[...] == lane).astype(f32))[0:atoms, :]
    spot = lax.broadcasted_iota(jnp.int32, (G, list_edges), 1) - lax.broadcasted_iota(
        jnp.int32, (G, list_edges), 0
    ) * slots
    blocks = ((spot >= 0) & (spot < slots)).astype(f32).astype(bf16)
    r.own_l[...] = (mm(listed, blocks, 0, 0) - near).astype(bf16)
    r.own_all[...] = (r.live[0:atoms, :] - src_hot[0:atoms, :].astype(f32)).astype(bf16)

    wait_in(2)
    tab_g = r.tab_g
    entries_g = 8 * G
    hi, lo = split(r.ghost_f[:, C:])
    tab_g[0:entries_g, C:] = hi
    tab_g[entries_g:, C:] = lo
    hi, lo = split(r.ghost_f[:, 0:C])
    tab_g[0:entries_g, 0:C] = hi
    tab_g[entries_g:, 0:C] = lo
    xg_ref = r.xg
    for c in range(n_chunks):
        rows = rows_of(c)
        x = mm(hot_g[rows, :], tab_g[...], 1, 0)
        xg_ref[rows, :] = x
        sums = slot_sums(messages(rows, [x[:, C * k : C * (k + 1)] for k in range(4)]))
        for k in range(4):
            at = (slice(8 * c, 8 * c + 8), slice(C * k, C * (k + 1)))
            agg_ref[at] = (agg_ref[at] + sums[k]) * scale
    az = dot_k(agg_ref[:, 0:C], r.msz_f, 1)
    a2 = az[:, 0:C]
    b2 = dot_k(jnp.concatenate([agg_ref[:, C * k : C * (k + 1)] for k in (1, 2, 3)], axis=0), r.mv2_f, 1)
    b2 = [b2[k * atoms : (k + 1) * atoms] for k in range(3)]
    squares = a2 * a2 + (b2[0] * b2[0] + b2[1] * b2[1] + b2[2] * b2[2])
    z = r.z0[...] + az[:, C:] + dot_k(squares, r.rhq_f, 1)
    sz = jax.nn.sigmoid(z)
    dz = r.rop[...] * (sz * (1.0 + z * (1.0 - sz)))
    down = dot_k(dz, r.rhq_b, 0)
    ds_two, dq2 = down[:, 0:C], down[:, C:]
    dagg = r.dagg
    dagg[:, 0:C] = dot_k(ds_two + 2.0 * a2 * dq2, r.ms2_b, 0) * scale
    db = dot_k(jnp.concatenate([2.0 * b * dq2 for b in b2], axis=0), r.mv2_b, 0) * scale
    for k in range(3):
        dagg[:, C * (k + 1) : C * (k + 2)] = db[k * atoms : (k + 1) * atoms]

    def spread_rows(c):
        out = []
        for k in range(4):
            small = [dagg[a : a + 1, C * k : C * (k + 1)] for a in range(c * 8, (c + 1) * 8)]
            out.append(jnp.concatenate([jnp.broadcast_to(x, (slots, C)) for x in small], axis=0))
        return out

    def scatter(first, which, some):
        hi_ref, lo_ref = r.dx_hi, r.dx_lo
        for a in some:
            rows = slice(a * slots, (a + 1) * slots)
            d = [dagg[a : a + 1, C * k : C * (k + 1)] for k in range(4)]
            for n, k in enumerate(which):
                if k == 0:
                    ru = [ru_ref[rows, C * (3 + m) : C * (4 + m)] for m in range(3)]
                    g = rad_ref[rows, 0:C] * d[0] + ru[0] * d[1] + (ru[1] * d[2] + ru[2] * d[3])
                else:
                    g = ru_ref[rows, C * (k - 1) : C * k] * d[0] + rad_ref[rows, 3 * C : 4 * C] * d[k]
                at = slice(C * (first + n), C * (first + n + 1))
                hi_ref[rows, at], lo_ref[rows, at] = split(g)

    def gather_grads(hot, first):
        at = slice(C * first, C * (first + 2))
        return mm(hot, r.dx_hi[:, at], 1, 0) + mm(hot, r.dx_lo[:, at], 1, 0)

    ghost_hot = slice(atoms, None)
    scatter(0, (1, 2), range(atoms))
    r.grad_a[...] = gather_grads(src_hot[ghost_hot, :], 0)
    early = atoms // 2
    scatter(2, (3, 0), range(early))
    send_all(3)
    scatter(2, (3, 0), range(early, atoms))
    r.grad_b[...] = gather_grads(src_hot[ghost_hot, :], 2)
    send_all(4)

    lin8 = jnp.broadcast_to(held.lin[...], (8, C))
    ro8 = jnp.broadcast_to(r.rop[...], (8, LANES))
    energy = dot3(lin8, r.scalar[...], 1, 1) + dot3(ro8, z * sz, 1, 1)
    r.eout[...] = energy[0:1, :]

    def node_grads(ds, dv, rows):
        a = r.node_a[rows, :]
        b = [r.node_b[rows, C * k : C * (k + 1)] for k in range(3)]
        dq = dot_k(ds, r.mq1_b, 0)
        da = ds + 2.0 * a * dq + (dv[0] * b[0] + dv[1] * b[1] + dv[2] * b[2])
        db = jnp.concatenate([dv[k] * (1.0 + a) + 2.0 * b[k] * dq for k in range(3)], axis=0)
        n = ds.shape[0]
        back = dot_k(db, r.wm1, 1)
        back = [dot_k(da, r.wm0, 1)] + [back[k * n : (k + 1) * n] for k in range(3)]
        hi, lo = split(jnp.concatenate(turn(back), axis=0))
        return jnp.concatenate([hi, lo], axis=0)

    def lane_put(sums):
        lane = lax.broadcasted_iota(jnp.int32, sums[0].shape, 1)
        out = jnp.zeros(sums[0].shape, f32)
        for k in range(3):
            out = jnp.where(lane == k, jnp.sum(sums[k], axis=1, keepdims=True), out)
        return out

    own_a = gather_grads(src_hot[0:atoms, :], 0)
    own_b = gather_grads(src_hot[0:atoms, :], 2)
    ds_own = own_b[:, C:] + ds_two + held.lin[...]
    r.gp[...] = node_grads(ds_own, [own_a[:, 0:C], own_a[:, C:], own_b[:, 0:C]], slice(0, atoms))
    f_own = r.f_own
    for c in range(n_chunks):
        rows = rows_of(c)
        d = spread_rows(c)
        x = [x_ref[rows, C * k : C * (k + 1)] + xg_ref[rows, C * k : C * (k + 1)] for k in range(4)]
        s, v = x[0], x[1:]
        u = [u_ref[rows, LANES * k : LANES * (k + 1)] for k in range(3)]
        rp = [radp[rows, C * k : C * (k + 1)] for k in range(4)]
        uv = u[0] * v[0] + u[1] * v[1] + u[2] * v[2]
        ud = u[0] * d[1] + u[1] * d[2] + u[2] * d[3]
        dv = d[1] * v[0] + d[2] * v[1] + d[3] * v[2]
        along = rp[0] * (d[0] * s) + rp[1] * (d[0] * uv) + (rp[2] * (s * ud) + rp[3] * dv)
        r1d = (rad_ref[rows, C : 2 * C] * d[0]) * inv_ref[rows, :]
        r2s = (rad_ref[rows, 2 * C : 3 * C] * s) * inv_ref[rows, :]
        g = mm(key_own_hot[rows, :], r.gp[...], 1, 0)
        g0, g1 = g[:, 0:LANES], g[:, LANES:]
        sums = []
        for k in range(3):
            j0 = jac[rows, 2 * LANES * k : 2 * LANES * k + LANES]
            j1 = jac[rows, 2 * LANES * k + LANES : 2 * LANES * (k + 1)]
            sums.append((u[k] * along + r1d * v[k]) + (r2s * d[k + 1] + (g0 * j0 + g1 * j1)))
        f_own[rows, :] = lane_put(sums)
    hi, mid, lo = split3(f_own[...])
    hot = src_hot[ghost_hot, :]
    r.force_o[...] = mm(hot, hi, 1, 0) + (mm(hot, mid, 1, 0) + mm(hot, lo, 1, 0))
    own = r.own_all[...]
    r.force_n[...] = mm(own, hi, 1, 0) + (mm(own, mid, 1, 0) + mm(own, lo, 1, 0))


    def total(ref):
        out = [ref[k] for k in range(8)]
        while len(out) > 1:
            out = [out[i] + out[i + 1] for i in range(0, len(out), 2)]
        return out[0]

    wait_in(3)
    g_a = total(r.in_a)
    wait_in(4)
    g_b = total(r.in_b)
    gp_l = node_grads(g_b[:, C:], [g_a[:, 0:C], g_a[:, C:], g_b[:, 0:C]], slice(atoms, nodes))
    f_list = []
    for g in range(G):
        rows = slice(g * slots, (g + 1) * slots)
        at = pl.ds(starts[g], slots)
        if g % 4 == 0:
            wide = mm(r.key_hot[g * slots : (g + 4) * slots, :], gp_l, 1, 0)
        m = g % 4
        here = wide[m * slots : (m + 1) * slots]
        g0, g1 = here[:, 0:LANES], here[:, LANES:]
        sums = []
        for k in range(3):
            j0 = jac[at, 2 * LANES * k : 2 * LANES * k + LANES]
            j1 = jac[at, 2 * LANES * k + LANES : 2 * LANES * (k + 1)]
            sums.append(g0 * j0 + g1 * j1)
        f_list.append(lane_put(sums))
    f_list = jnp.concatenate(f_list, axis=0)
    l_hi, l_lo = split(f_list)
    hot = r.src_gl[...]
    far_force = r.force_o[...] + (mm(hot, l_hi, 1, 0) + mm(hot, l_lo, 1, 0))
    for side in range(8):
        first = far_force[side * G : side * G + half]
        second = far_force[side * G + half : (side + 1) * G]
        r.force_g[side * half : (side + 1) * half, :] = jnp.where(left, first, pltpu.roll(second, LANES // 2, 1))
    send_all(5)
    own_l = r.own_l[...]
    force = r.force_n[...] + (mm(own_l, l_hi, 1, 0) + mm(own_l, l_lo, 1, 0))
    force = jnp.transpose(force)
    for phase in (0, 2, 3, 4):
        wait_out(phase)
    wait_in(5)
    late = total(r.in_f)
    for k in range(3):
        other = k + LANES // 2
        back = late[:, k : k + 1] * listed_f[0:half] + late[:, other : other + 1] * listed_f[half:]
        back = jnp.sum(back, axis=0, keepdims=True)
        r.fout[k : k + 1, :] = force[k : k + 1, :] - back
    wait_out(5)


def store_kernel(e_ref, f_ref, eo_ref, fo_ref, sem):
    one = pltpu.make_async_copy(e_ref, eo_ref, sem.at[0])
    two = pltpu.make_async_copy(f_ref, fo_ref, sem.at[1])
    one.start()
    two.start()
    one.wait()
    two.wait()


def in_order(vec, senders, counts, species, list, embed, win1, wmid1, wout1, ms1, mv1, mq1, win2, wmid2, wout2, ms2, mv2, mq2, lin, rh, ro):
    return dict(locals())


def on_device(n_dom, n_sub, *args):
    (vec, senders, counts, species, send_list, embed) = args[:6]
    weights = list(args[6:18])
    read_lin, read_hidden, read_out = args[18:]
    edges = vec.shape[1]
    atoms = species.shape[0]
    G = send_list.shape[0]
    C, kinds_n = embed.shape
    hidden, n_basis = weights[0].shape
    for i in (0, 2, 6, 8):
        weights[i] = weights[i].T
    row = lambda x: x.reshape(1, -1)
    operands = [vec, row(senders), row(counts), row(species), row(send_list), embed.T, *weights]
    operands += [row(read_lin), read_hidden, row(read_out)]
    far, nodes, list_edges = 8 * G, atoms + G, G * (edges // atoms)
    i32 = jnp.int32
    packed = -(-(6 * n_basis + 24) // 16) * 16
    inputs = in_order(*operands)
    scratch = dict(
        kind_out=((G // 2, LANES), f32),
        ghost_kind=((8, G // 2, LANES), f32),
        out_f=((G, 4 * C), f32),
        ghost_f=((far, 4 * C), f32),
        grad_a=((far, 2 * C), f32),
        grad_b=((far, 2 * C), f32),
        in_a=((8, G, 2 * C), f32),
        in_b=((8, G, 2 * C), f32),
        force_g=((far // 2, LANES), f32),
        force_o=((far, LANES), f32),
        force_n=((atoms, LANES), f32),
        in_f=((8, G // 2, LANES), f32),
        rhs=((packed, 7 * LANES), f32),
        wide_rhs=((packed, 7 * LANES), bf16),
        pack=((packed, edges), bf16),
        v8=((8, edges), f32),
        winp=((n_basis, LANES), f32),
        wmid=((LANES, LANES), f32),
        wmid_f=((LANES, 3 * LANES), bf16),
        w2_k=((2 * LANES, 4 * C), bf16),
        rhp=((LANES, C), f32),
        rop=((1, LANES), f32),
        kind_own=((1, edges), f32),
        src_f=((far, edges), f32),
        kind=((1, edges), f32),
        live=((nodes, edges), f32),
        src_hot=((atoms + far, edges), bf16),
        hid=((edges, LANES), f32),
        th=((edges, LANES), f32),
        u=((edges, 3 * LANES), f32),
        inv=((edges, LANES), f32),
        ent=((edges, LANES), f32),
        p_hi=((edges, 2 * LANES), bf16),
        p_lo=((edges, 2 * LANES), bf16),
        rad=((edges, 4 * C), f32),
        radp=((edges, 4 * C), f32),
        ru=((edges, 6 * C), f32),
        jac=((edges, 6 * LANES), f32),
        wm0=((kinds_n * hidden, 3 * C), bf16),
        wm1=((kinds_n * hidden, 3 * C), bf16),
        mq1_f=((C, 3 * C), bf16),
        mq1_b=((3 * C, C), bf16),
        msz_f=((C + LANES, 3 * C), bf16),
        mv2_f=((C, 3 * C), bf16),
        rhq_f=((LANES, 3 * C), bf16),
        rhq_b=((3 * LANES, 2 * C), bf16),
        ms2_b=((3 * C, C), bf16),
        mv2_b=((3 * C, C), bf16),
        initial=((nodes, C), f32),
        node_a=((nodes, C), f32),
        node_b=((nodes, 3 * C), f32),
        scalar=((atoms, C), f32),
        z0=((atoms, LANES), f32),
        tab2=((LANES, 4 * C), bf16),
        tab_g=((2 * far, 4 * C), bf16),
        hot_g=((edges, 2 * LANES), bf16),
        x=((edges, 4 * C), f32),
        xg=((edges, 4 * C), f32),
        agg=((atoms, 4 * C), f32),
        dagg=((atoms, 4 * C), f32),
        key_own=((edges, 2 * LANES), bf16),
        key_list=((edges, LANES), f32),
        key_hot=((list_edges, LANES), bf16),
        src_t=((list_edges, LANES), f32),
        src_gl=((far, list_edges), bf16),
        own_l=((atoms, list_edges), bf16),
        own_all=((atoms, edges), bf16),
        dx_hi=((edges, 4 * C), bf16),
        dx_lo=((edges, 4 * C), bf16),
        gp=((2 * kinds_n * atoms, 2 * LANES), bf16),
        f_own=((edges, LANES), f32),
    )
    names = list(inputs) + ["eout", "fout"] + [k + "_" for k in inputs] + list(scratch)
    copies = [pltpu.VMEM(x.shape, x.dtype) for x in operands]
    hbm = pl.BlockSpec(memory_space=pltpu.HBM)
    whole = pl.BlockSpec(memory_space=pltpu.VMEM)
    out = pl.pallas_call(
        functools.partial(kernel, n_dom, n_sub, names),
        out_shape=[pltpu.VMEM((1, atoms), f32), pltpu.VMEM((3, atoms), f32)],
        in_specs=[hbm] * len(operands),
        out_specs=[whole, whole],
        scratch_shapes=copies
        + [pltpu.VMEM(shape, dtype) for shape, dtype in scratch.values()]
        + [pltpu.SMEM((1, G), i32)]
        + [pltpu.SemaphoreType.DMA((6, 9)), pltpu.SemaphoreType.DMA((6, 9))]
        + [pltpu.SemaphoreType.DMA((len(operands) + 1,))],
        compiler_params=pltpu.CompilerParams(
            collective_id=0, has_side_effects=True, vmem_limit_bytes=56 * 1024 * 1024
        ),
    )(*operands)
    out = pl.pallas_call(
        store_kernel,
        out_shape=[jax.ShapeDtypeStruct((1, atoms), f32), jax.ShapeDtypeStruct((3, atoms), f32)],
        in_specs=[whole, whole],
        out_specs=[hbm, hbm],
        scratch_shapes=[pltpu.SemaphoreType.DMA((2,))],
    )(*[pltpu.with_memory_space_constraint(o, pltpu.VMEM) for o in out])
    return out[0].reshape(atoms), out[1]


def solution(mesh):
    one = P(("dom", "sub"))
    return jax.shard_map(
        functools.partial(on_device, mesh.shape["dom"], mesh.shape["sub"]),
        mesh=mesh,
        in_specs=(P(None, ("dom", "sub")), one, one, one, one) + (P(),) * 16,
        out_specs=(one, P(None, ("dom", "sub"))),
        check_vma=False,
    )
```
